256 devices in a mesh: zone: 32 (over z, y), var: 8 (over x, core).
Axes of the slice: x: 4, y: 4, z: 8, core: 2. Of those that a mesh axis runs over, the one named last changes fastest.
Arguments:
- history: float32 [48, 64, 16384], P('var', None, 'zone'), may hold values from -6 to 6
- adjacency: int32 [6, 16384], P(None, 'zone'), may hold values from -1 to 16383, as said below
- volume_op: float32 [64, 64], replicated, may hold values from -0.375 to 0.375
- face_lift: float32 [6, 64, 64], replicated, may hold values from -0.1875 to 0.1875
- schmid_map: float32 [48, 12], replicated, may hold values from -0.875 to 0.875
- hardening: float32 [12, 48], replicated, may hold values from -1.75 to 1.75
Outputs:
- remapped: float32 [48, 64, 16384], P('var', None, 'zone')
The draws below stay inside these ranges and needn't reach their ends.
Inputs may be any that keep to these rules, and one draw needn't show every extreme that they name: `adjacency`: every entry is -1 or a zone whose index differs from the zone's own by at most 64; differences of exactly 64 and -64 occur.
All inputs are finite; a program needn't handle non-finite values.
Results may differ from the reference program's by a relative error of at most 0.0001.
Values sent between devices are 32-bit elements; how exact they have to be, the bound alone decides.
No kernel may reach another device: no remote copies, remote signals or barrier semaphores. Data moves between devices by JAX's collectives and lax.ppermute only.
A program may use at most 64 MiB of HBM per device.

```python
import jax
import jax.numpy as jnp
from jax import lax

V = 48
P_SIZE = 64
SLIP = 12
ZDEV = 512
ZONES = 16384
RIM = 64
N_VAR = 8


def draw_adjacency(key, part):
    zone_ids = jnp.arange(ZONES, dtype=jnp.int32)
    position = zone_ids % ZDEV
    offsets = jax.random.randint(jax.random.fold_in(key, 11), (6, ZONES), -RIM, RIM + 1)
    offsets = offsets.at[0].set(jnp.where(position == ZDEV - 1, RIM, offsets[0]))
    offsets = offsets.at[1].set(jnp.where(position == 0, -RIM, offsets[1]))
    offsets = offsets.at[2].set(jnp.where(position == ZDEV - 2, 1, offsets[2]))
    target = zone_ids[None, :] + offsets
    open_face = jax.random.randint(jax.random.fold_in(key, 12), (6, ZONES), 0, 16)
    keep_face = (open_face != 0) | (jnp.arange(6)[:, None] < 3)
    target = jnp.where((target < 0) | (target >= ZONES) | jnp.logical_not(keep_face), -1, target)
    return target.astype(jnp.int32)


def block_scale(rng, dims, cuts, smallest, high):
    def one(dim, parts):
        draws = jax.random.uniform(jax.random.fold_in(jax.random.fold_in(rng, 6), dim), (parts,), jnp.float32, smallest / len(cuts), high / len(cuts))
        return jnp.repeat(jnp.exp(draws), dims[dim] // parts).reshape((-1,) + (1,) * (len(dims) - dim - 1))

    level = one(*cuts[0])
    for cut in cuts[1:]:
        level = level * one(*cut)
    return level


def noise(rng, dims, deviation, bound, split=(), kind=jnp.bfloat16):
    array = deviation * jax.random.normal(rng, dims, jnp.float32)
    if split:
        array = array * block_scale(rng, dims, split, -0.22, 0.18)
    return jnp.clip(array, -bound, bound).astype(kind)


def setup_inputs(seed: int = 0) -> dict:
    splits = jax.random.split(jax.random.key(seed), 7)
    history = noise(splits[0], (V, P_SIZE, ZONES), 1.0, 6.0, ((0, 8), (2, 32)), jnp.float32)
    adjacency = draw_adjacency(jax.random.fold_in(splits[6], 71), 0)
    volume_op = noise(splits[2], (P_SIZE, P_SIZE), (4 * P_SIZE) ** -0.5, 0.375, (), jnp.float32)
    face_lift = noise(splits[3], (6, P_SIZE, P_SIZE), (16 * P_SIZE) ** -0.5, 0.1875, (), jnp.float32)
    schmid_map = noise(splits[4], (V, SLIP), V ** -0.5, 0.875, (), jnp.float32)
    hardening = noise(splits[5], (SLIP, V), SLIP ** -0.5, 1.75, (), jnp.float32)
    return {"history": history, "adjacency": adjacency, "volume_op": volume_op, "face_lift": face_lift, "schmid_map": schmid_map, "hardening": hardening}


def advect_operator(field, adjacency, volume_op, face_lift):
    result = jnp.dot(volume_op.T, field, precision=lax.Precision.HIGHEST)
    for face in range(6):
        face_index = adjacency[face]
        safe_index = jnp.clip(face_index, 0, ZONES - 1).astype(jnp.int32)
        neighbour = jnp.take(field, safe_index, axis=1)
        neighbour = jnp.where(face_index[None, :] >= 0, neighbour, jnp.float32(0.0))
        result = result + jnp.dot(face_lift[face].T, neighbour, precision=lax.Precision.HIGHEST)
    return result

def advect_variable(field, adjacency, volume_op, face_lift):
    section_one = field + advect_operator(field, adjacency, volume_op, face_lift)
    section_two = 0.75 * field + 0.25 * (section_one + advect_operator(section_one, adjacency, volume_op, face_lift))
    return field / 3.0 + 2.0 / 3.0 * (section_two + advect_operator(section_two, adjacency, volume_op, face_lift))

def reference(history, adjacency, volume_op, face_lift, schmid_map, hardening):
    advected = lax.map(lambda field: advect_variable(field, adjacency, volume_op, face_lift), history)
    shear = jnp.einsum('va,vpz->apz', schmid_map, advected, precision=lax.Precision.HIGHEST)
    updated = advected + jnp.einsum('av,apz->vpz', hardening, jnp.tanh(shear), precision=lax.Precision.HIGHEST)
    stride = V // N_VAR
    rotation = updated[0:4 * stride:stride]
    length = jnp.sqrt(lax.optimization_barrier(jnp.sum(rotation * rotation, axis=0)))
    factor = 1.0 / jnp.maximum(length, 1.0)
    return updated.at[0:4 * stride:stride].multiply(factor[None])
```

```python
import jax
import jax.numpy as jnp
from jax import lax
from jax.experimental import pallas as pl
from jax.experimental.pallas import tpu as pltpu
from jax.sharding import PartitionSpec as P

F32 = jnp.float32
BF16 = jnp.bfloat16
NV = 6
NP = 64
NZ = 512
ROWS = NV * NP
LANE = 128
HALF = 64
NFACE = 6
KDIM = (NFACE + 1) * NP


def lane_iota(rows):
    return lax.broadcasted_iota(jnp.int32, (rows, LANE), 1)


def swap(x):
    return pltpu.roll(x, HALF, 1)


def split(x):
    high = x.astype(BF16)
    low = (x - high.astype(F32)).astype(BF16)
    return high, low


def pack_kernel(history, adjacency, forward, backward):
    first = lane_iota(ROWS // 2) < HALF
    forward[0:ROWS, :] = history[:, 384:512]
    forward[ROWS : ROWS + ROWS // 2, :] = jnp.where(
        first, swap(history[0 : ROWS // 2, 256:384]), history[ROWS // 2 :, 256:384]
    )
    forward[576:584, :] = adjacency[:, 384:512]
    backward[0:ROWS, :] = history[:, 0:128]
    backward[ROWS : ROWS + ROWS // 2, :] = jnp.where(
        first, history[0 : ROWS // 2, 128:256], swap(history[ROWS // 2 :, 128:256])
    )
    backward[576:584, :] = adjacency[:, 0:128]


def onehot_block(zones, window_start, onehots, slot):
    position = (lax.broadcasted_iota(jnp.int32, (2 * LANE, LANE), 0) + window_start).astype(F32)
    for face in range(NFACE):
        hit = position == zones[face : face + 1, :]
        onehots[slot, :, face * LANE : (face + 1) * LANE] = jnp.where(hit, 1.0, 0.0).astype(BF16)


def advect_kernel(base, history, adjacency, low, high, weights, out, u0, u64, adj, onehots, parts, gathered, t1, t2):
    first = lane_iota(ROWS // 2) < HALF
    u64[:, 0:128] = low[0:ROWS, :]
    u64[:, 128:640] = history[...]
    u64[:, 640:768] = high[0:ROWS, :]
    half = ROWS // 2
    low_far = low[ROWS : ROWS + half, :]
    high_far = high[ROWS : ROWS + half, :]
    near_low = swap(low[0:ROWS, :])
    u0[0:half, 0:128] = jnp.where(first, low_far, near_low[0:half])
    u0[half:, 0:128] = jnp.where(first, swap(low_far), near_low[half:])
    near_high = swap(high[0:ROWS, :])
    u0[0:half, 768:896] = jnp.where(first, near_high[0:half], swap(high_far))
    u0[half:, 768:896] = jnp.where(first, near_high[half:], high_far)
    whole = lane_iota(ROWS) < HALF
    for c in range(1, 6):
        u0[:, c * LANE : (c + 1) * LANE] = jnp.where(
            whole, swap(u64[:, (c - 1) * LANE : c * LANE]), swap(u64[:, c * LANE : (c + 1) * LANE])
        )
    u0[:, 768:896] = jnp.where(whole, swap(u64[:, 640:768]), u0[:, 768:896])
    origin = base[0].astype(F32)

    def located(a):
        return jnp.where(a < 0.0, -1000.0, a - origin)

    adj[:, 0:128] = located(low[576:584, :])
    adj[:, 128:640] = located(adjacency[...])
    adj[:, 640:768] = located(high[576:584, :])
    small = lane_iota(8) < HALF
    for b in range(6):
        onehot_block(adj[:, b * LANE : (b + 1) * LANE], 128 * b, onehots, b)
    for b in range(5):
        zones = jnp.where(
            small, swap(adj[:, b * LANE : (b + 1) * LANE]), swap(adj[:, (b + 1) * LANE : (b + 2) * LANE])
        )
        onehot_block(zones, 128 * b + 64, onehots, 6 + b)

    def section(source, blocks, slot, own_ready, finish):
        for c in range(blocks + 1):
            h, l = split(source[:, c * LANE : (c + 1) * LANE])
            parts[0:ROWS, c * LANE : (c + 1) * LANE] = h
            parts[ROWS:, c * LANE : (c + 1) * LANE] = l
        for c in range(blocks):
            if own_ready is None:
                own = jnp.where(
                    whole,
                    swap(source[:, c * LANE : (c + 1) * LANE]),
                    swap(source[:, (c + 1) * LANE : (c + 2) * LANE]),
                )
            else:
                own = own_ready[:, c * LANE : (c + 1) * LANE]
            h, l = split(own)
            for v in range(NV):
                gathered[v, 0, 384:448, c * LANE : (c + 1) * LANE] = h[v * NP : (v + 1) * NP]
                gathered[v, 1, 384:448, c * LANE : (c + 1) * LANE] = l[v * NP : (v + 1) * NP]

        def gather(b, carry):
            start = pl.multiple_of(b * LANE, LANE)
            for pair in range(NFACE // 2):
                picked = jnp.dot(
                    parts[:, pl.ds(start, 2 * LANE)],
                    onehots[slot + b, :, pair * 256 : (pair + 1) * 256],
                    preferred_element_type=F32,
                ).astype(BF16)
                for part in range(2):
                    for v in range(NV):
                        row = part * ROWS + v * NP
                        for k in range(2):
                            face = 2 * pair + k
                            gathered[v, part, face * NP : (face + 1) * NP, pl.ds(start, LANE)] = picked[
                                row : row + NP, k * LANE : (k + 1) * LANE
                            ]
            return carry

        lax.fori_loop(0, blocks, gather, 0)
        width = blocks * LANE

        def lift(v, carry):
            both = jnp.dot(weights[...], gathered[v, 0, :, 0:width], preferred_element_type=F32)
            rest = jnp.dot(weights[0:NP, :], gathered[v, 1, :, 0:width], preferred_element_type=F32)
            finish(v, both[0:NP] + (both[NP:] + rest))
            return carry

        lax.fori_loop(0, NV, lift, 0)

    def finish_one(v, value):
        row = pl.multiple_of(v * NP, NP)
        t1[pl.ds(row, NP), :] = u64[pl.ds(row, NP), :] + value * (1.0 / 3.0)

    def finish_two(v, value):
        row = pl.multiple_of(v * NP, NP)
        t2[pl.ds(row, NP), :] = u0[pl.ds(row, NP), 128:768] + value * 0.5

    def finish_three(v, value):
        row = pl.multiple_of(v * NP, NP)
        result = u64[pl.ds(row, NP), 128:640] + value
        for slab in range(8):
            out[slab, v, :, :] = result[slab * 8 : (slab + 1) * 8, :]

    section(u0, 6, 0, u64, finish_one)
    section(t1, 5, 6, None, finish_two)
    section(t2, 4, 1, None, finish_three)


def point_kernel(schmid, hardening, points, out):
    nvar = 48
    nslip = 12
    rates = []
    for a in range(nslip):
        total = points[0] * schmid[0, a]
        for v in range(1, nvar):
            total = total + points[v] * schmid[v, a]
        rates.append(jnp.tanh(total))

    def renew(v):
        value = points[v]
        for a in range(nslip):
            value = value + rates[a] * hardening[a, v]
        return value

    rotation = [renew(6 * k) for k in range(4)]
    square = rotation[0] * rotation[0]
    for k in range(1, 4):
        square = square + rotation[k] * rotation[k]
    factor = 1.0 / jnp.maximum(jnp.sqrt(square), 1.0)
    for v in range(nvar):
        if v % 6 == 0 and v < 24:
            out[v] = rotation[v // 6] * factor
        else:
            out[v] = renew(v)


def vmem():
    return pl.BlockSpec(memory_space=pltpu.VMEM)


def smem():
    return pl.BlockSpec(memory_space=pltpu.SMEM)


def per_device(history, adjacency, volume_op, face_lift, schmid_map, hardening):
    count = lax.axis_size("zone")
    flat = history.reshape(ROWS, NZ)
    adj8 = jnp.concatenate([adjacency, adjacency[:2]], axis=0).astype(F32)
    payload = jax.ShapeDtypeStruct((584, LANE), F32)
    forward, backward = pl.pallas_call(
        pack_kernel,
        out_shape=(payload, payload),
        in_specs=[vmem(), vmem()],
        out_specs=(vmem(), vmem()),
        name="pack",
    )(flat, adj8)
    up = [(i, i + 1) for i in range(count - 1)]
    down = [(i + 1, i) for i in range(count - 1)]
    low = lax.ppermute(forward, "zone", up)
    high = lax.ppermute(backward, "zone", down)
    lift = jnp.concatenate([face_lift, volume_op[None]], axis=0)
    lift = lift.transpose(2, 0, 1).reshape(NP, KDIM)
    lift_high = lax.reduce_precision(lift, 8, 7)
    lift_low = lift - lift_high
    weights = jnp.concatenate([lift_high, lift_low], axis=0).astype(BF16)
    base = (lax.axis_index("zone") * NZ - 192).astype(jnp.int32).reshape(1)
    advected = pl.pallas_call(
        advect_kernel,
        out_shape=jax.ShapeDtypeStruct((8, NV, 8, NZ), F32),
        in_specs=[smem(), vmem(), vmem(), vmem(), vmem(), vmem()],
        out_specs=vmem(),
        scratch_shapes=[
            pltpu.VMEM((ROWS, 896), F32),
            pltpu.VMEM((ROWS, 768), F32),
            pltpu.VMEM((8, 768), F32),
            pltpu.VMEM((11, 256, 768), BF16),
            pltpu.VMEM((2 * ROWS, 896), BF16),
            pltpu.VMEM((NV, 2, KDIM, 768), BF16),
            pltpu.VMEM((ROWS, 768), F32),
            pltpu.VMEM((ROWS, 640), F32),
        ],
        compiler_params=pltpu.CompilerParams(vmem_limit_bytes=40 << 20),
        name="advect",
    )(base, flat, adj8, low, high, weights)
    points = lax.all_to_all(advected, "var", split_axis=0, concat_axis=0, tiled=True)
    renewed = pl.pallas_call(
        point_kernel,
        out_shape=jax.ShapeDtypeStruct((48, 8, NZ), F32),
        in_specs=[smem(), smem(), vmem()],
        out_specs=vmem(),
        name="points",
    )(schmid_map, hardening, points.reshape(48, 8, NZ))
    back = lax.all_to_all(renewed.reshape(8, NV, 8, NZ), "var", split_axis=0, concat_axis=0, tiled=True)
    return back.transpose(1, 0, 2, 3).reshape(NV, NP, NZ)


def solution(mesh):
    in_specs = (P("var", None, "zone"), P(None, "zone"), P(), P(), P(), P())
    out_specs = P("var", None, "zone")
    return jax.shard_map(
        per_device, mesh=mesh, in_specs=in_specs, out_specs=out_specs, check_vma=False
    )
```

```python
import jax
import jax.numpy as jnp
from jax import lax
from jax.experimental import pallas as pl
from jax.experimental.pallas import tpu as pltpu
from jax.sharding import PartitionSpec as P

F32 = jnp.float32
BF16 = jnp.bfloat16
NV = 6
NP = 64
NZ = 512
ROWS = NV * NP
LANE = 128
HALF = 64
NFACE = 6
MATMUL_FACES = 4
KDIM = (NFACE + 1) * NP
SLOTS = [(0, 0), (2, 0), (2, 1), (1, 0), (3, 0), (1, 1), (3, 1), (0, 1)]


def first_half(rows):
    return lax.broadcasted_iota(jnp.int32, (rows, LANE), 1) < HALF


def swap(x):
    return pltpu.roll(x, HALF, 1)


def straddle(left, right):
    return jnp.where(first_half(left.shape[0]), swap(left), swap(right))


def split(x):
    high = x.astype(BF16)
    low = (x - high.astype(F32)).astype(BF16)
    return high, low


def cols(b, n=1):
    return slice(b * LANE, (b + n) * LANE)


def put_parts(parts, where, x):
    high, low = split(x)
    parts[0:ROWS, where] = high
    parts[ROWS:, where] = low


def pack_kernel(history, adjacency, forward, backward):
    half = ROWS // 2
    first = first_half(half)
    forward[0:ROWS, :] = history[:, 384:512]
    forward[ROWS : ROWS + half, :] = jnp.where(first, swap(history[0:half, 256:384]), history[half:, 256:384])
    backward[0:ROWS, :] = history[:, 0:128]
    backward[ROWS : ROWS + half, :] = jnp.where(first, history[0:half, 128:256], swap(history[half:, 128:256]))
    for target, lanes in ((forward, slice(384, 512)), (backward, slice(0, 128))):
        target[576:584, :] = jnp.zeros((8, LANE), F32)
        target[576 : 576 + NFACE, :] = adjacency[:, lanes].astype(F32)


def place(adjacency, start):
    return jnp.where(adjacency < 0, 1000, adjacency - start)


def write_onehots(onehots, slot, rel):
    position = lax.broadcasted_iota(jnp.int32, (2 * LANE, LANE), 0)
    for face in range(MATMUL_FACES):
        hit = position == rel[face : face + 1, :]
        onehots[slot, :, cols(face)] = jnp.where(hit, 1.0, 0.0).astype(BF16)


def apply_block(source, parts, col, onehots, slot, rel, own, gathered, weights):
    for pair in range(MATMUL_FACES // 2):
        picked = jnp.dot(
            parts[:, pl.ds(col, 2 * LANE)], onehots[slot, :, cols(2 * pair, 2)], preferred_element_type=F32
        ).astype(BF16)
        for part in range(2):
            for v in range(NV):
                row = part * ROWS + v * NP
                for k in range(2):
                    face = 2 * pair + k
                    gathered[part, face * NP : (face + 1) * NP, cols(v)] = picked[row : row + NP, cols(k)]
    for face in range(MATMUL_FACES, NFACE):
        index = jnp.broadcast_to(rel[face : face + 1, :], (ROWS, LANE))
        lane = index & (LANE - 1)
        near = jnp.take_along_axis(source[:, pl.ds(col, LANE)], lane, axis=1)
        far = jnp.take_along_axis(source[:, pl.ds(col + LANE, LANE)], lane, axis=1)
        value = jnp.where(index >= 2 * LANE, 0.0, jnp.where(index >= LANE, far, near))
        for part, piece in enumerate(split(value)):
            for v in range(NV):
                gathered[part, face * NP : (face + 1) * NP, cols(v)] = piece[v * NP : (v + 1) * NP]
    for part, piece in enumerate(split(own)):
        for v in range(NV):
            gathered[part, NFACE * NP :, cols(v)] = piece[v * NP : (v + 1) * NP]
    both = jnp.dot(weights[...], gathered[0], preferred_element_type=F32)
    rest = jnp.dot(weights[0:NP, :], gathered[1], preferred_element_type=F32)
    value = both[0:NP] + (both[NP:] + rest)
    return [value[:, cols(v)] for v in range(NV)]


def finish(values, base, scale, target, parts, where):
    for v in range(NV):
        rows = slice(v * NP, (v + 1) * NP)
        result = base[rows] + values[v] * scale
        target[rows, where] = result
        high, low = split(result)
        parts[rows, where] = high
        parts[ROWS + v * NP : ROWS + (v + 1) * NP, where] = low


def inner_kernel(place_ref, history, adjacency, weights, u0, parts, onehots, t1, parts2, t2, parts3, gat_a, gat_b):
    origin = place_ref[0]
    zero = jnp.zeros((ROWS, LANE), F32)
    blocks = [history[:, cols(b)] for b in range(4)]
    padded = [zero] + blocks + [zero]
    for c in range(5):
        u0[:, cols(c)] = straddle(padded[c], padded[c + 1])
    for c in range(1, 4):
        put_parts(parts, cols(c - 1), u0[:, cols(c)])
    for b in range(4):
        write_onehots(onehots, b, place(adjacency[:, cols(b)], origin + (128 * b + 128)))
    near = [
        jnp.where(first_half(NFACE), pltpu.roll(adjacency[:, cols(b)], HALF, 1), pltpu.roll(adjacency[:, cols(b + 1)], HALF, 1))
        for b in range(3)
    ]
    for b in range(3):
        write_onehots(onehots, 4 + b, place(near[b], origin + (128 * b + 192)))
    for b, gathered in ((2, gat_a), (3, gat_b)):
        rel = place(adjacency[:, cols(b - 1)], origin + 128 * b)
        values = apply_block(
            u0.at[:, 128:512], parts, (b - 2) * LANE, onehots, b - 1, rel, blocks[b - 1], gathered, weights
        )
        finish(values, history[:, cols(b - 1)], 1.0 / 3.0, t1, parts2, cols(b - 2))
    rel = place(near[1], origin + 320)
    own = straddle(t1[:, cols(0)], t1[:, cols(1)])
    values = apply_block(t1, parts2, 0, onehots, 5, rel, own, gat_a, weights)
    finish(values, u0[:, cols(2)], 0.5, t2, parts3, cols(0))


def outer_kernel(
    place_ref, history, adjacency, low, high, weights, u0m, partsm, onehots, t1m, parts2m, t2m, parts3m,
    *rest,
):
    outs = rest[:8]
    u0, parts, edge, t1, parts2, t2, parts3, gat_a, gat_b = rest[8:]
    origin = place_ref[0]
    x = place_ref[1]
    core = place_ref[2]
    half = ROWS // 2
    first = first_half(half)
    whole = first_half(ROWS)
    low_far = low[ROWS : ROWS + half, :]
    high_far = high[ROWS : ROWS + half, :]
    near_low = swap(low[0:ROWS, :])
    near_high = swap(high[0:ROWS, :])
    u0[0:half, cols(0)] = jnp.where(first, low_far, near_low[0:half])
    u0[half:, cols(0)] = jnp.where(first, swap(low_far), near_low[half:])
    u0[:, cols(1)] = jnp.where(whole, near_low, u0m[:, cols(0)])
    u0[:, cols(2, 3)] = u0m[:, cols(1, 3)]
    u0[:, cols(5)] = jnp.where(whole, u0m[:, cols(4)], near_high)
    u0[0:half, cols(6)] = jnp.where(first, near_high[0:half], swap(high_far))
    u0[half:, cols(6)] = jnp.where(first, near_high[half:], high_far)
    parts[:, cols(2)] = partsm[:, cols(0)]
    parts[:, cols(4)] = partsm[:, cols(2)]
    for c in (0, 1, 5, 6):
        put_parts(parts, cols(c), u0[:, cols(c)])
    t1[:, cols(2, 2)] = t1m[...]
    parts2[:, cols(2, 2)] = parts2m[...]
    t2[:, cols(2)] = t2m[...]
    parts3[:, cols(2)] = parts3m[...]
    low_adj = low[576:584, :].astype(jnp.int32)[0:NFACE]
    high_adj = high[576:584, :].astype(jnp.int32)[0:NFACE]

    def mix(left, right):
        return jnp.where(first_half(NFACE), pltpu.roll(left, HALF, 1), pltpu.roll(right, HALF, 1))

    adj = [low_adj] + [adjacency[:, cols(b)] for b in range(4)] + [high_adj]
    edges = {}
    for slot, (section, b) in enumerate(((1, 0), (1, 5), (2, 0), (2, 4))):
        if section == 1:
            rel = place(adj[b], origin + 128 * b)
        else:
            rel = place(mix(adj[b], adj[b + 1]), origin + (128 * b + 64))
        write_onehots(edge, slot, rel)
        edges[section, b] = slot

    def base_block(b):
        if b == 0:
            return low[0:ROWS, :]
        if b == 5:
            return high[0:ROWS, :]
        return history[:, cols(b - 1)]

    for b, gathered in ((1, gat_a), (4, gat_b), (0, gat_a), (5, gat_b)):
        rel = place(adj[b], origin + 128 * b)
        table, slot = (edge, edges[1, b]) if (1, b) in edges else (onehots, b - 1)
        values = apply_block(u0, parts, b * LANE, table, slot, rel, base_block(b), gathered, weights)
        finish(values, base_block(b), 1.0 / 3.0, t1, parts2, cols(b))
    for b, gathered in ((1, gat_a), (3, gat_b), (0, gat_a), (4, gat_b)):
        rel = place(mix(adj[b], adj[b + 1]), origin + (128 * b + 64))
        table, slot = (edge, edges[2, b]) if (2, b) in edges else (onehots, 3 + b)
        own = straddle(t1[:, cols(b)], t1[:, cols(b + 1)])
        values = apply_block(t1, parts2, b * LANE, table, slot, rel, own, gathered, weights)
        finish(values, u0[:, cols(b + 1)], 0.5, t2, parts3, cols(b))
    for dx, gathered in ((2, gat_a), (1, gat_b), (3, gat_a), (0, gat_b)):
        b = (x + dx) & 3
        col = pl.multiple_of(b * LANE, LANE)
        rel = place(adjacency[:, pl.ds(col, LANE)], origin + 128 + col)
        own = straddle(t2[:, pl.ds(col, LANE)], t2[:, pl.ds(col + LANE, LANE)])
        values = apply_block(t2, parts3, col, onehots, b, rel, own, gathered, weights)
        upper = core == 1
        for v in range(NV):
            result = history[v * NP : (v + 1) * NP, pl.ds(col, LANE)] + values[v]
            below, above = result[0:32], result[32:64]
            outs[SLOTS.index((dx, 0))][v] = jnp.where(upper, above, below)
            outs[SLOTS.index((dx, 1))][v] = jnp.where(upper, below, above)


def source_of(x, core, slot):
    dx, dc = SLOTS[slot]
    return ((x - dx) & 3) * 2 + (core ^ dc)


def table_kernel(place_ref, volume_op, face_lift, schmid_map, hardening, weights, mixing, renewing):
    x = place_ref[1]
    core = place_ref[2]
    for lanes, matrix in ((slice(0, 384), face_lift[...].T), (slice(384, 448), volume_op[...].T)):
        high, low = split(matrix)
        weights[0:NP, lanes] = high
        weights[NP:, lanes] = low

    def variable(index):
        total = jnp.zeros(index.shape, jnp.int32)
        for slot in range(8):
            inside = (index >= slot * 48) & (index < slot * 48 + 48)
            total = jnp.where(inside, source_of(x, core, slot) * NV + ((index - slot * 48) >> 3), total)
        return total

    def onehot(hit):
        return jnp.where(hit, 1.0, 0.0).astype(BF16)

    def iota(shape, axis):
        return lax.broadcasted_iota(jnp.int32, shape, axis)

    columns = onehot(iota((48, ROWS), 0) == variable(iota((48, ROWS), 1)))
    rows = onehot(iota((ROWS, 48), 1) == variable(iota((ROWS, 48), 0)))
    slips = onehot(iota((96, 12), 1) == (iota((96, 12), 0) >> 3))
    spread = onehot(iota((12, 96), 0) == (iota((12, 96), 1) >> 3))
    wide = onehot((iota((96, ROWS), 0) & 7) == (iota((96, ROWS), 1) & 7)).astype(F32)
    tall = onehot((iota((ROWS, 96), 0) & 7) == (iota((ROWS, 96), 1) & 7)).astype(F32)
    second = (((1,), (1,)), ((), ()))
    for part, piece in enumerate(split(schmid_map[...])):
        picked = lax.dot_general(slips, piece, second, preferred_element_type=F32).astype(BF16)
        picked = jnp.dot(picked, columns, preferred_element_type=F32) * wide
        mixing[part * 96 : (part + 1) * 96, :] = picked.astype(BF16)
    for part, piece in enumerate(split(hardening[...])):
        picked = lax.dot_general(rows, piece, second, preferred_element_type=F32).astype(BF16)
        picked = (jnp.dot(picked, spread, preferred_element_type=F32) * tall).astype(BF16)
        if part == 0:
            renewing[:, 0:96] = picked
            renewing[:, 96:192] = picked
        else:
            renewing[:, 192:288] = picked


def point_kernel(place_ref, mixing, renewing, *rest):
    own = [source_of(place_ref[1], place_ref[2], slot) < 4 for slot in range(8)]
    points = rest[:8]
    outs = rest[8:16]
    highs, lows, rate_parts = rest[16:]
    for slot in range(8):
        for i in range(NV):
            row = (slot * NV + i) * 8
            for g in range(4):
                high, low = split(points[slot][i, g * 8 : (g + 1) * 8, :])
                highs[row : row + 8, cols(g)] = high
                lows[row : row + 8, cols(g)] = low
    both = jnp.dot(mixing[...], highs[...], preferred_element_type=F32)
    rest_ = jnp.dot(mixing[0:96, :], lows[...], preferred_element_type=F32)
    rates = jnp.tanh(both[0:96] + (both[96:] + rest_))
    high, low = split(rates)
    rate_parts[0:96, :] = high
    rate_parts[96:192, :] = low
    rate_parts[192:288, :] = high
    change = jnp.dot(renewing[...], rate_parts[...], preferred_element_type=F32)
    for g in range(4):
        rows = [points[slot][0, g * 8 : (g + 1) * 8, :] + change[slot * 48 : slot * 48 + 8, cols(g)] for slot in range(8)]
        square = jnp.zeros((8, LANE), F32)
        for slot in range(8):
            square = square + jnp.where(own[slot], rows[slot] * rows[slot], 0.0)
        factor = 1.0 / jnp.maximum(jnp.sqrt(square), 1.0)
        for slot in range(8):
            outs[slot][0, g * 8 : (g + 1) * 8, :] = jnp.where(own[slot], rows[slot] * factor, rows[slot])
            for i in range(1, NV):
                row = (slot * NV + i) * 8
                outs[slot][i, g * 8 : (g + 1) * 8, :] = (
                    points[slot][i, g * 8 : (g + 1) * 8, :] + change[row : row + 8, cols(g)]
                )


def merge_kernel(place_ref, *rest):
    pieces = rest[:8]
    out = rest[8]
    x = place_ref[1]
    core = place_ref[2]
    for slot, (dx, dc) in enumerate(SLOTS):
        col = pl.multiple_of(((x + dx) & 3) * LANE, LANE)
        row = pl.multiple_of((core ^ dc) * 32, 32)
        for v in range(NV):
            out[v, pl.ds(row, 32), pl.ds(col, LANE)] = pieces[slot][v]


def vmem():
    return pl.BlockSpec(memory_space=pltpu.VMEM)


def smem():
    return pl.BlockSpec(memory_space=pltpu.SMEM)


def call(kernel, name, scalars, args, outs, scratch=()):
    return pl.pallas_call(
        kernel,
        out_shape=tuple(jax.ShapeDtypeStruct(shape, dtype) for shape, dtype in outs),
        in_specs=[smem() for _ in scalars] + [vmem() for _ in args],
        out_specs=tuple(vmem() for _ in outs),
        scratch_shapes=[pltpu.VMEM(shape, dtype) for shape, dtype in scratch],
        compiler_params=pltpu.CompilerParams(vmem_limit_bytes=32 << 20),
        name=name,
    )(*scalars, *args)


def per_device(history, adjacency, volume_op, face_lift, schmid_map, hardening):
    count = lax.axis_size("zone")
    flat = history.reshape(ROWS, NZ)
    forward, backward = call(
        pack_kernel, "pack", (), (flat, adjacency), [((584, LANE), F32)] * 2
    )
    low = lax.ppermute(forward, "zone", [(i, i + 1) for i in range(count - 1)])
    high = lax.ppermute(backward, "zone", [(i + 1, i) for i in range(count - 1)])
    var = lax.axis_index("var")
    where = jnp.stack([lax.axis_index("zone") * NZ - 192, var >> 1, var & 1]).astype(jnp.int32)
    weights, mixing, renewing = call(
        table_kernel,
        "tables",
        (where,),
        (volume_op, face_lift.reshape(NFACE * NP, NP), schmid_map, hardening),
        [((2 * NP, KDIM), BF16), ((192, ROWS), BF16), ((ROWS, 288), BF16)],
    )
    inner = call(
        inner_kernel,
        "inner",
        (where,),
        (flat, adjacency, weights),
        [
            ((ROWS, 640), F32),
            ((2 * ROWS, 384), BF16),
            ((7, 256, MATMUL_FACES * LANE), BF16),
            ((ROWS, 256), F32),
            ((2 * ROWS, 256), BF16),
            ((ROWS, LANE), F32),
            ((2 * ROWS, LANE), BF16),
        ],
        [((2, KDIM, NV * LANE), BF16)] * 2,
    )
    advected = call(
        outer_kernel,
        "outer",
        (where,),
        (flat, adjacency, low, high, weights, *inner),
        [((NV, 32, LANE), F32)] * 8,
        [
            ((ROWS, 896), F32),
            ((2 * ROWS, 896), BF16),
            ((4, 256, MATMUL_FACES * LANE), BF16),
            ((ROWS, 768), F32),
            ((2 * ROWS, 768), BF16),
            ((ROWS, 640), F32),
            ((2 * ROWS, 640), BF16),
            ((2, KDIM, NV * LANE), BF16),
            ((2, KDIM, NV * LANE), BF16),
        ],
    )

    def exchange(piece, dx, dc):
        if dx == 0 and dc == 0:
            return piece
        pairs = [(v, ((v // 2 + dx) % 4) * 2 + ((v % 2) ^ dc)) for v in range(8)]
        return lax.ppermute(piece, "var", pairs)

    points = [exchange(piece, dx, dc) for piece, (dx, dc) in zip(advected, SLOTS)]
    renewed = call(
        point_kernel,
        "points",
        (where,),
        (mixing, renewing, *points),
        [((NV, 32, LANE), F32)] * 8,
        [((ROWS, 512), BF16), ((ROWS, 512), BF16), ((288, 512), BF16)],
    )
    returned = [exchange(piece, (4 - dx) % 4, dc) for piece, (dx, dc) in zip(renewed, SLOTS)]
    return call(merge_kernel, "merge", (where,), returned, [((NV, NP, NZ), F32)])[0]


def solution(mesh):
    in_specs = (P("var", None, "zone"), P(None, "zone"), P(), P(), P(), P())
    out_specs = P("var", None, "zone")
    return jax.shard_map(
        per_device, mesh=mesh, in_specs=in_specs, out_specs=out_specs, check_vma=False
    )
```

```python
import jax
import jax.numpy as jnp
from jax import lax
from jax.experimental import pallas as pl
from jax.experimental.pallas import tpu as pltpu
from jax.sharding import PartitionSpec as P


F32 = jnp.float32
BF16 = jnp.bfloat16
NV = 6
NP = 64
NZ = 512
ROWS = NV * NP
LANE = 128
HALF = 64
NFACE = 6
MATMUL_FACES = 4
KDIM = (NFACE + 1) * NP
SLOTS = [(0, 0), (2, 0), (2, 1), (1, 0), (1, 1), (3, 0), (3, 1), (0, 1)]


def first_half(rows):
    return lax.broadcasted_iota(jnp.int32, (rows, LANE), 1) < HALF


def swap(x):
    return pltpu.roll(x, HALF, 1)


def straddle(left, right):
    return jnp.where(first_half(left.shape[0]), swap(left), swap(right))


def split(x):
    high = x.astype(BF16)
    low = (x - high.astype(F32)).astype(BF16)
    return high, low


def cols(b, n=1):
    return slice(b * LANE, (b + n) * LANE)


def put_parts(parts, where, x):
    high, low = split(x)
    parts[0:ROWS, where] = high
    parts[ROWS:, where] = low


def fetch(pairs, sems):
    copies = [pltpu.make_async_copy(source, target, sems.at[i]) for i, (source, target) in enumerate(pairs)]
    for copy in copies:
        copy.start()
    return copies


def pack_kernel(history_hbm, adjacency_hbm, forward, backward, history, adjacency, sems):
    half = ROWS // 2
    first = first_half(half)
    copies = fetch(
        [(history_hbm.at[:, cols(c)], history.at[:, cols(c)]) for c in (2, 3, 0, 1)] + [(adjacency_hbm, adjacency)],
        sems,
    )
    copies[0].wait()
    copies[1].wait()
    forward[0:ROWS, :] = history[:, 384:512]
    forward[ROWS : ROWS + half, :] = jnp.where(first, swap(history[0:half, 256:384]), history[half:, 256:384])
    copies[2].wait()
    copies[3].wait()
    backward[0:ROWS, :] = history[:, 0:128]
    backward[ROWS : ROWS + half, :] = jnp.where(first, history[0:half, 128:256], swap(history[half:, 128:256]))
    copies[4].wait()
    for target, lanes in ((forward, slice(384, 512)), (backward, slice(0, 128))):
        target[576:584, :] = jnp.zeros((8, LANE), F32)
        target[576 : 576 + NFACE, :] = adjacency[:, lanes].astype(F32)


def place(adjacency, start):
    return jnp.where(adjacency < 0, 1000, adjacency - start)


def write_onehots(onehots, slot, rel):
    position = lax.broadcasted_iota(jnp.int32, (2 * LANE, LANE), 0)
    for face in range(MATMUL_FACES):
        hit = position == rel[face : face + 1, :]
        onehots[slot, :, cols(face)] = jnp.where(hit, 1.0, 0.0).astype(BF16)


def apply_block(source, parts, col, onehots, slot, rel, own, gathered, weights):
    for pair in range(MATMUL_FACES // 2):
        picked = jnp.dot(
            parts[:, pl.ds(col, 2 * LANE)], onehots[slot, :, cols(2 * pair, 2)], preferred_element_type=F32
        ).astype(BF16)
        for part in range(2):
            for v in range(NV):
                row = part * ROWS + v * NP
                for k in range(2):
                    face = 2 * pair + k
                    gathered[part, face * NP : (face + 1) * NP, cols(v)] = picked[row : row + NP, cols(k)]
    for face in range(MATMUL_FACES, NFACE):
        index = jnp.broadcast_to(rel[face : face + 1, :], (ROWS, LANE))
        lane = index & (LANE - 1)
        near = jnp.take_along_axis(source[:, pl.ds(col, LANE)], lane, axis=1)
        far = jnp.take_along_axis(source[:, pl.ds(col + LANE, LANE)], lane, axis=1)
        value = jnp.where(index >= 2 * LANE, 0.0, jnp.where(index >= LANE, far, near))
        for part, piece in enumerate(split(value)):
            for v in range(NV):
                gathered[part, face * NP : (face + 1) * NP, cols(v)] = piece[v * NP : (v + 1) * NP]
    for part, piece in enumerate(split(own)):
        for v in range(NV):
            gathered[part, NFACE * NP :, cols(v)] = piece[v * NP : (v + 1) * NP]
    both = jnp.dot(weights[...], gathered[0], preferred_element_type=F32)
    rest = jnp.dot(weights[0:NP, :], gathered[1], preferred_element_type=F32)
    value = both[0:NP] + (both[NP:] + rest)
    return [value[:, cols(v)] for v in range(NV)]


def finish(values, base, scale, target, parts, where):
    for v in range(NV):
        rows = slice(v * NP, (v + 1) * NP)
        result = base[rows] + values[v] * scale
        target[rows, where] = result
        high, low = split(result)
        parts[rows, where] = high
        parts[ROWS + v * NP : ROWS + (v + 1) * NP, where] = low


def inner_kernel(place_ref, history, adjacency, weights, u0, parts, onehots, t1, parts2, t2, parts3, gat_a, gat_b):
    origin = place_ref[0]
    zero = jnp.zeros((ROWS, LANE), F32)
    blocks = [history[:, cols(b)] for b in range(4)]
    padded = [zero] + blocks + [zero]
    for c in range(5):
        u0[:, cols(c)] = straddle(padded[c], padded[c + 1])
    for c in range(1, 4):
        put_parts(parts, cols(c - 1), u0[:, cols(c)])
    for b in range(4):
        write_onehots(onehots, b, place(adjacency[:, cols(b)], origin + (128 * b + 128)))
    near = [
        jnp.where(first_half(NFACE), pltpu.roll(adjacency[:, cols(b)], HALF, 1), pltpu.roll(adjacency[:, cols(b + 1)], HALF, 1))
        for b in range(3)
    ]
    for b in range(3):
        write_onehots(onehots, 4 + b, place(near[b], origin + (128 * b + 192)))
    for b, gathered in ((2, gat_a), (3, gat_b)):
        rel = place(adjacency[:, cols(b - 1)], origin + 128 * b)
        values = apply_block(
            u0.at[:, 128:512], parts, (b - 2) * LANE, onehots, b - 1, rel, blocks[b - 1], gathered, weights
        )
        finish(values, history[:, cols(b - 1)], 1.0 / 3.0, t1, parts2, cols(b - 2))
    rel = place(near[1], origin + 320)
    own = straddle(t1[:, cols(0)], t1[:, cols(1)])
    values = apply_block(t1, parts2, 0, onehots, 5, rel, own, gat_a, weights)
    finish(values, u0[:, cols(2)], 0.5, t2, parts3, cols(0))


def outer_kernel(
    place_ref, history, adjacency, low, high, weights, u0m, partsm, onehots, t1m, parts2m, t2m, parts3m,
    *rest,
):
    outs = rest[:2]
    t2, parts3, u0, parts, edge, t1, parts2, gat_a, gat_b = rest[2:]
    origin = place_ref[0]
    half = ROWS // 2
    first = first_half(half)
    whole = first_half(ROWS)
    low_far = low[ROWS : ROWS + half, :]
    high_far = high[ROWS : ROWS + half, :]
    near_low = swap(low[0:ROWS, :])
    near_high = swap(high[0:ROWS, :])
    u0[0:half, cols(0)] = jnp.where(first, low_far, near_low[0:half])
    u0[half:, cols(0)] = jnp.where(first, swap(low_far), near_low[half:])
    u0[:, cols(1)] = jnp.where(whole, near_low, u0m[:, cols(0)])
    u0[:, cols(2, 3)] = u0m[:, cols(1, 3)]
    u0[:, cols(5)] = jnp.where(whole, u0m[:, cols(4)], near_high)
    u0[0:half, cols(6)] = jnp.where(first, near_high[0:half], swap(high_far))
    u0[half:, cols(6)] = jnp.where(first, near_high[half:], high_far)
    parts[:, cols(2)] = partsm[:, cols(0)]
    parts[:, cols(4)] = partsm[:, cols(2)]
    for c in (0, 1, 5, 6):
        put_parts(parts, cols(c), u0[:, cols(c)])
    t1[:, cols(2, 2)] = t1m[...]
    parts2[:, cols(2, 2)] = parts2m[...]
    t2[:, cols(2)] = t2m[...]
    parts3[:, cols(2)] = parts3m[...]
    low_adj = low[576:584, :].astype(jnp.int32)[0:NFACE]
    high_adj = high[576:584, :].astype(jnp.int32)[0:NFACE]

    def mix(left, right):
        return jnp.where(first_half(NFACE), pltpu.roll(left, HALF, 1), pltpu.roll(right, HALF, 1))

    adj = [low_adj] + [adjacency[:, cols(b)] for b in range(4)] + [high_adj]
    edges = {}
    for slot, (section, b) in enumerate(((1, 0), (1, 5), (2, 0), (2, 4))):
        if section == 1:
            rel = place(adj[b], origin + 128 * b)
        else:
            rel = place(mix(adj[b], adj[b + 1]), origin + (128 * b + 64))
        write_onehots(edge, slot, rel)
        edges[section, b] = slot

    def base_block(b):
        if b == 0:
            return low[0:ROWS, :]
        if b == 5:
            return high[0:ROWS, :]
        return history[:, cols(b - 1)]

    for b, gathered in ((1, gat_a), (4, gat_b), (0, gat_a), (5, gat_b)):
        rel = place(adj[b], origin + 128 * b)
        table, slot = (edge, edges[1, b]) if (1, b) in edges else (onehots, b - 1)
        values = apply_block(u0, parts, b * LANE, table, slot, rel, base_block(b), gathered, weights)
        finish(values, base_block(b), 1.0 / 3.0, t1, parts2, cols(b))
    for b, gathered in ((1, gat_a), (3, gat_b), (0, gat_a), (4, gat_b)):
        rel = place(mix(adj[b], adj[b + 1]), origin + (128 * b + 64))
        table, slot = (edge, edges[2, b]) if (2, b) in edges else (onehots, 3 + b)
        own = straddle(t1[:, cols(b)], t1[:, cols(b + 1)])
        values = apply_block(t1, parts2, b * LANE, table, slot, rel, own, gathered, weights)
        finish(values, u0[:, cols(b + 1)], 0.5, t2, parts3, cols(b))
    last_block(place_ref, 2, history, adjacency, weights, onehots, t2, parts3, gat_a, outs)


def last_block(place_ref, dx, history, adjacency, weights, onehots, t2, parts3, gathered, outs):
    col = pl.multiple_of(((place_ref[1] + dx) & 3) * LANE, LANE)
    rel = place(adjacency[:, pl.ds(col, LANE)], place_ref[0] + 128 + col)
    own = straddle(t2[:, pl.ds(col, LANE)], t2[:, pl.ds(col + LANE, LANE)])
    values = apply_block(t2, parts3, col, onehots, (place_ref[1] + dx) & 3, rel, own, gathered, weights)
    upper = place_ref[2] == 1
    for v in range(NV):
        result = history[v * NP : (v + 1) * NP, pl.ds(col, LANE)] + values[v]
        below, above = result[0:32], result[32:64]
        outs[0][v] = jnp.where(upper, above, below)
        outs[1][v] = jnp.where(upper, below, above)


def last_kernel(dx):
    def kernel(place_ref, history, adjacency, weights, onehots, t2, parts3, kept, crossed, gathered):
        last_block(place_ref, dx, history, adjacency, weights, onehots, t2, parts3, gathered, (kept, crossed))

    return kernel


def source_of(x, core, slot):
    dx, dc = SLOTS[slot]
    return ((x - dx) & 3) * 2 + (core ^ dc)


def table_kernel(
    place_ref, volume_hbm, face_hbm, schmid_hbm, hardening_hbm, weights, mixing, renewing,
    volume_op, face_lift, schmid_map, hardening, sems,
):
    x = place_ref[1]
    core = place_ref[2]
    copies = fetch(
        [(volume_hbm, volume_op), (face_hbm, face_lift), (schmid_hbm, schmid_map), (hardening_hbm, hardening)], sems
    )
    for copy in copies:
        copy.wait()
    for lanes, matrix in ((slice(0, 384), face_lift[...].T), (slice(384, 448), volume_op[...].T)):
        high, low = split(matrix)
        weights[0:NP, lanes] = high
        weights[NP:, lanes] = low

    def variable(index):
        total = jnp.zeros(index.shape, jnp.int32)
        for slot in range(8):
            inside = (index >= slot * 48) & (index < slot * 48 + 48)
            total = jnp.where(inside, source_of(x, core, slot) * NV + ((index - slot * 48) >> 3), total)
        return total

    def onehot(hit):
        return jnp.where(hit, 1.0, 0.0).astype(BF16)

    def iota(shape, axis):
        return lax.broadcasted_iota(jnp.int32, shape, axis)

    columns = onehot(iota((48, ROWS), 0) == variable(iota((48, ROWS), 1)))
    rows = onehot(iota((ROWS, 48), 1) == variable(iota((ROWS, 48), 0)))
    slips = onehot(iota((96, 12), 1) == (iota((96, 12), 0) >> 3))
    spread = onehot(iota((12, 96), 0) == (iota((12, 96), 1) >> 3))
    wide = onehot((iota((96, ROWS), 0) & 7) == (iota((96, ROWS), 1) & 7)).astype(F32)
    tall = onehot((iota((ROWS, 96), 0) & 7) == (iota((ROWS, 96), 1) & 7)).astype(F32)
    second = (((1,), (1,)), ((), ()))
    for part, piece in enumerate(split(schmid_map[...])):
        picked = jnp.dot(slips, piece, preferred_element_type=F32).astype(BF16)
        picked = jnp.dot(picked, columns, preferred_element_type=F32) * wide
        mixing[part * 96 : (part + 1) * 96, :] = picked.astype(BF16)
    for part, piece in enumerate(split(hardening[...])):
        picked = lax.dot_general(rows, piece, second, preferred_element_type=F32).astype(BF16)
        picked = (jnp.dot(picked, spread, preferred_element_type=F32) * tall).astype(BF16)
        if part == 0:
            renewing[:, 0:96] = picked
            renewing[:, 96:192] = picked
        else:
            renewing[:, 192:288] = picked


def point_kernel(place_ref, mixing, renewing, *rest):
    own = [source_of(place_ref[1], place_ref[2], slot) < 4 for slot in range(8)]
    points = rest[:8]
    outs = rest[8:16]
    highs, lows, rate_parts = rest[16:]
    for slot in range(8):
        for i in range(NV):
            row = (slot * NV + i) * 8
            for g in range(4):
                high, low = split(points[slot][i, g * 8 : (g + 1) * 8, :])
                highs[row : row + 8, cols(g)] = high
                lows[row : row + 8, cols(g)] = low
    both = jnp.dot(mixing[...], highs[...], preferred_element_type=F32)
    rest_ = jnp.dot(mixing[0:96, :], lows[...], preferred_element_type=F32)
    rates = jnp.tanh(both[0:96] + (both[96:] + rest_))
    high, low = split(rates)
    rate_parts[0:96, :] = high
    rate_parts[96:192, :] = low
    rate_parts[192:288, :] = high
    change = jnp.dot(renewing[...], rate_parts[...], preferred_element_type=F32)
    for g in range(4):
        rows = [points[slot][0, g * 8 : (g + 1) * 8, :] + change[slot * 48 : slot * 48 + 8, cols(g)] for slot in range(8)]
        square = jnp.zeros((8, LANE), F32)
        for slot in range(8):
            square = square + jnp.where(own[slot], rows[slot] * rows[slot], 0.0)
        factor = 1.0 / jnp.maximum(jnp.sqrt(square), 1.0)
        for slot in range(8):
            outs[slot][0, g * 8 : (g + 1) * 8, :] = jnp.where(own[slot], rows[slot] * factor, rows[slot])
            for i in range(1, NV):
                row = (slot * NV + i) * 8
                outs[slot][i, g * 8 : (g + 1) * 8, :] = (
                    points[slot][i, g * 8 : (g + 1) * 8, :] + change[row : row + 8, cols(g)]
                )


def merge_kernel(place_ref, *rest):
    pieces = rest[:8]
    out, sems = rest[8:]
    x = place_ref[1]
    core = place_ref[2]
    pairs = []
    for slot, (dx, dc) in enumerate(SLOTS):
        col = pl.multiple_of(((x + dx) & 3) * LANE, LANE)
        row = pl.multiple_of((core ^ dc) * 32, 32)
        pairs.append((pieces[slot], out.at[:, pl.ds(row, 32), pl.ds(col, LANE)]))
    for copy in fetch(pairs, sems):
        copy.wait()


def vmem():
    return pl.BlockSpec(memory_space=pltpu.VMEM)


def smem():
    return pl.BlockSpec(memory_space=pltpu.SMEM)


def anywhere():
    return pl.BlockSpec(memory_space=pltpu.MemorySpace.HBM)


def call(kernel, scalars, args, outs, scratch=(), copies=0, spaces=(vmem, vmem)):
    return pl.pallas_call(
        kernel,
        out_shape=tuple(jax.ShapeDtypeStruct(shape, dtype) for shape, dtype in outs),
        in_specs=[smem() for _ in scalars] + [spaces[0]() for _ in args],
        out_specs=tuple(spaces[1]() for _ in outs),
        scratch_shapes=[pltpu.VMEM(shape, dtype) for shape, dtype in scratch]
        + ([pltpu.SemaphoreType.DMA((copies,))] if copies else []),
        compiler_params=pltpu.CompilerParams(vmem_limit_bytes=32 << 20),
    )(*scalars, *(pltpu.with_memory_space_constraint(a, pltpu.MemorySpace.HBM) if spaces[0] is anywhere else a for a in args))


def per_device(history, adjacency, volume_op, face_lift, schmid_map, hardening):
    count = lax.axis_size("zone")
    flat = history.reshape(ROWS, NZ)
    payload = ((584, LANE), F32)
    forward, backward, local, faces = call(
        pack_kernel,
        (),
        (flat, adjacency),
        [payload, payload, ((ROWS, NZ), F32), ((NFACE, NZ), jnp.int32)],
        copies=5,
        spaces=(anywhere, vmem),
    )
    low = lax.ppermute(forward, "zone", [(i, (i + 1) % count) for i in range(count)])
    high = lax.ppermute(backward, "zone", [((i + 1) % count, i) for i in range(count)])
    var = lax.axis_index("var")
    where = jnp.stack([lax.axis_index("zone") * NZ - 192, var >> 1, var & 1]).astype(jnp.int32)
    weights, mixing, renewing = call(
        table_kernel,
        (where,),
        (volume_op, face_lift.reshape(NFACE * NP, NP), schmid_map.T, hardening),
        [((2 * NP, KDIM), BF16), ((192, ROWS), BF16), ((ROWS, 288), BF16)],
        [((NP, NP), F32), ((NFACE * NP, NP), F32), ((12, 48), F32), ((12, 48), F32)],
        copies=4,
        spaces=(anywhere, vmem),
    )
    buffer = ((2, KDIM, NV * LANE), BF16)
    inner = call(
        inner_kernel,
        (where,),
        (local, faces, weights),
        [
            ((ROWS, 640), F32),
            ((2 * ROWS, 384), BF16),
            ((7, 256, MATMUL_FACES * LANE), BF16),
            ((ROWS, 256), F32),
            ((2 * ROWS, 256), BF16),
            ((ROWS, LANE), F32),
            ((2 * ROWS, LANE), BF16),
        ],
        [buffer] * 2,
    )
    piece = ((NV, 32, LANE), F32)
    *ahead, t2, parts3 = call(
        outer_kernel,
        (where,),
        (local, faces, low, high, weights, *inner),
        [piece, piece, ((ROWS, 640), F32), ((2 * ROWS, 640), BF16)],
        [
            ((ROWS, 896), F32),
            ((2 * ROWS, 896), BF16),
            ((4, 256, MATMUL_FACES * LANE), BF16),
            ((ROWS, 768), F32),
            ((2 * ROWS, 768), BF16),
            buffer,
            buffer,
        ],
    )
    advected = {(2, 0): ahead[0], (2, 1): ahead[1]}
    for dx in (1, 3, 0):
        advected[dx, 0], advected[dx, 1] = call(
            last_kernel(dx), (where,), (local, faces, weights, inner[2], t2, parts3), [piece, piece], [buffer]
        )

    def exchange(piece, dx, dc):
        if dx == 0 and dc == 0:
            return piece
        pairs = [(v, ((v // 2 + dx) % 4) * 2 + ((v % 2) ^ dc)) for v in range(8)]
        return lax.ppermute(piece, "var", pairs)

    points = [exchange(advected[dx, dc], dx, dc) for dx, dc in SLOTS]
    renewed = call(
        point_kernel,
        (where,),
        (mixing, renewing, *points),
        [((NV, 32, LANE), F32)] * 8,
        [((ROWS, 512), BF16), ((ROWS, 512), BF16), ((288, 512), BF16)],
    )
    returned = [exchange(piece, (4 - dx) % 4, dc) for piece, (dx, dc) in zip(renewed, SLOTS)]
    return call(merge_kernel, (where,), returned, [((NV, NP, NZ), F32)], copies=8, spaces=(vmem, anywhere))[0]


def solution(mesh):
    in_specs = (P("var", None, "zone"), P(None, "zone"), P(), P(), P(), P())
    out_specs = P("var", None, "zone")

    return jax.shard_map(per_device, mesh=mesh, in_specs=in_specs, out_specs=out_specs, check_vma=False)
```

```python
import jax
import jax.numpy as jnp
from jax import lax
from jax.experimental import pallas as pl
from jax.experimental.pallas import tpu as pltpu
from jax.sharding import PartitionSpec as P


F32 = jnp.float32
BF16 = jnp.bfloat16
NV = 6
NP = 64
NZ = 512
ROWS = NV * NP
LANE = 128
HALF = 64
NFACE = 6
MATMUL_FACES = 4
KDIM = (NFACE + 1) * NP
SLOTS = [(0, 0), (2, 0), (2, 1), (1, 0), (3, 0), (1, 1), (3, 1), (0, 1)]
EARLY = (0, 1, 2, 7)
LATE = (3, 4, 5, 6)


def first_half(rows):
    return lax.broadcasted_iota(jnp.int32, (rows, LANE), 1) < HALF


def swap(x):
    return pltpu.roll(x, HALF, 1)


def straddle(left, right):
    return jnp.where(first_half(left.shape[0]), swap(left), swap(right))


def split(x):
    high = x.astype(BF16)
    low = (x - high.astype(F32)).astype(BF16)
    return high, low


def cols(b, n=1):
    return slice(b * LANE, (b + n) * LANE)


def put_parts(parts, where, x):
    high, low = split(x)
    parts[0:ROWS, where] = high
    parts[ROWS:, where] = low


def fetch(pairs, sems):
    copies = [pltpu.make_async_copy(source, target, sems.at[i]) for i, (source, target) in enumerate(pairs)]
    for copy in copies:
        copy.start()
    return copies


def pack_kernel(
    place_ref, history_hbm, adjacency_hbm, near_one, near_two, far_one, far_two, history, adjacency, sems
):
    half = ROWS // 2
    first = first_half(half)
    odd = place_ref[3] == 1
    copies = fetch(
        [(history_hbm.at[:, cols(c)], history.at[:, cols(c)]) for c in (0, 3, 1, 2)] + [(adjacency_hbm, adjacency)],
        sems,
    )

    def put(one, two, rows, forward, backward):
        one[rows, :] = jnp.where(odd, forward, backward)
        two[rows, :] = jnp.where(odd, backward, forward)

    copies[0].wait()
    copies[1].wait()
    forward = jnp.where(first, swap(history[0:half, cols(3)]), history[half:, cols(3)])
    backward = jnp.where(first, history[0:half, cols(0)], swap(history[half:, cols(0)]))
    put(near_one, near_two, slice(0, half), forward, backward)
    copies[2].wait()
    copies[3].wait()
    forward = straddle(history[:, cols(2)], history[:, cols(3)])
    backward = straddle(history[:, cols(0)], history[:, cols(1)])
    put(far_one, far_two, slice(0, ROWS), forward, backward)
    copies[4].wait()
    for target in (far_one, far_two):
        target[ROWS:, :] = jnp.zeros((8, LANE), F32)
    put(
        far_one, far_two, slice(ROWS, ROWS + NFACE), adjacency[:, cols(3)].astype(F32), adjacency[:, cols(0)].astype(F32)
    )


def place(adjacency, start):
    return jnp.where(adjacency < 0, 1000, adjacency - start)


def write_onehots(onehots, slot, rel):
    position = lax.broadcasted_iota(jnp.int32, (2 * LANE, LANE), 0)
    for face in range(MATMUL_FACES):
        hit = position == rel[face : face + 1, :]
        onehots[slot, :, cols(face)] = jnp.where(hit, 1.0, 0.0).astype(BF16)


def apply_block(close, beyond, parts, col, onehots, slot, rel, own, gathered, weights):
    for pair in range(MATMUL_FACES // 2):
        picked = jnp.dot(
            parts[:, pl.ds(col, 2 * LANE)], onehots[slot, :, cols(2 * pair, 2)], preferred_element_type=F32
        ).astype(BF16)
        for part in range(2):
            for v in range(NV):
                row = part * ROWS + v * NP
                for k in range(2):
                    face = 2 * pair + k
                    gathered[part, face * NP : (face + 1) * NP, cols(v)] = picked[row : row + NP, cols(k)]
    for face in range(MATMUL_FACES, NFACE):
        index = jnp.broadcast_to(rel[face : face + 1, :], (ROWS, LANE))
        lane = index & (LANE - 1)
        near = jnp.take_along_axis(close, lane, axis=1)
        far = jnp.take_along_axis(beyond, lane, axis=1)
        value = jnp.where(index >= 2 * LANE, 0.0, jnp.where(index >= LANE, far, near))
        for part, piece in enumerate(split(value)):
            for v in range(NV):
                gathered[part, face * NP : (face + 1) * NP, cols(v)] = piece[v * NP : (v + 1) * NP]
    for part, piece in enumerate(split(own)):
        for v in range(NV):
            gathered[part, NFACE * NP :, cols(v)] = piece[v * NP : (v + 1) * NP]
    both = jnp.dot(weights[...], gathered[0], preferred_element_type=F32)
    rest = jnp.dot(weights[0:NP, :], gathered[1], preferred_element_type=F32)
    value = both[0:NP] + (both[NP:] + rest)
    return [value[:, cols(v)] for v in range(NV)]


def finish(values, base, scale, target, parts, where):
    for v in range(NV):
        rows = slice(v * NP, (v + 1) * NP)
        result = base[rows] + values[v] * scale
        target[rows, where] = result
        high, low = split(result)
        parts[rows, where] = high
        parts[ROWS + v * NP : ROWS + (v + 1) * NP, where] = low


def mix(left, right):
    return jnp.where(first_half(NFACE), pltpu.roll(left, HALF, 1), pltpu.roll(right, HALF, 1))


def inner_kernel(
    place_ref, history, adjacency, volume_hbm, face_hbm,
    u0, parts, onehots, t1, parts2, t2, parts3, weights,
    gat_a, gat_b, volume_op, face_lift, sems,
):
    copies = fetch([(volume_hbm, volume_op), (face_hbm, face_lift)], sems)
    origin = place_ref[0]
    zero = jnp.zeros((ROWS, LANE), F32)
    blocks = [history[:, cols(b)] for b in range(4)]
    padded = [zero] + blocks + [zero]
    for c in range(5):
        u0[:, cols(c)] = straddle(padded[c], padded[c + 1])
    for c in range(1, 4):
        put_parts(parts, cols(c - 1), u0[:, cols(c)])
    for b in range(4):
        write_onehots(onehots, b, place(adjacency[:, cols(b)], origin + (128 * b + 128)))
    near = [mix(adjacency[:, cols(b)], adjacency[:, cols(b + 1)]) for b in range(3)]
    for b in range(3):
        write_onehots(onehots, 4 + b, place(near[b], origin + (128 * b + 192)))
    for copy in copies:
        copy.wait()
    for lanes, matrix in ((slice(0, 384), face_lift[...].T), (slice(384, 448), volume_op[...].T)):
        high, low = split(matrix)
        weights[0:NP, lanes] = high
        weights[NP:, lanes] = low
    for b, gathered in ((2, gat_a), (3, gat_b)):
        rel = place(adjacency[:, cols(b - 1)], origin + 128 * b)
        values = apply_block(
            u0[:, cols(b - 1)], u0[:, cols(b)], parts, (b - 2) * LANE, onehots, b - 1, rel, blocks[b - 1], gathered, weights
        )
        finish(values, blocks[b - 1], 1.0 / 3.0, t1, parts2, cols(b - 2))
    rel = place(near[1], origin + 320)
    own = straddle(t1[:, cols(0)], t1[:, cols(1)])
    values = apply_block(t1[:, cols(0)], t1[:, cols(1)], parts2, 0, onehots, 5, rel, own, gat_a, weights)
    finish(values, u0[:, cols(2)], 0.5, t2, parts3, cols(0))


def middle_kernel(
    place_ref, history, adjacency, near_one, near_two, u0m, partsm, onehots, t1m, parts2m, t2m, parts3m, weights,
    ends, end_parts, rim, rim_parts, t2, parts3,
    left, right, t1, parts2, gat_a, gat_b,
):
    origin = place_ref[0]
    odd = place_ref[3] == 1
    half = ROWS // 2
    first = first_half(half)
    low = jnp.where(odd, near_two[...], near_one[...])
    high = jnp.where(odd, near_one[...], near_two[...])
    ends[0:half, cols(0)] = jnp.where(first, low, u0m[0:half, cols(0)])
    ends[half:, cols(0)] = jnp.where(first, swap(low), u0m[half:, cols(0)])
    ends[0:half, cols(1)] = jnp.where(first, u0m[0:half, cols(4)], swap(high))
    ends[half:, cols(1)] = jnp.where(first, u0m[half:, cols(4)], high)
    put_parts(end_parts, cols(0), ends[:, cols(0)])
    put_parts(end_parts, cols(1), ends[:, cols(1)])
    left[:, cols(0)] = end_parts[:, cols(0)]
    left[:, cols(1)] = partsm[:, cols(0)]
    right[:, cols(0)] = partsm[:, cols(2)]
    right[:, cols(1)] = end_parts[:, cols(1)]
    t1[:, cols(1, 2)] = t1m[...]
    parts2[:, cols(1, 2)] = parts2m[...]
    t2[:, cols(1)] = t2m[...]
    parts3[:, cols(1)] = parts3m[...]
    rel = place(adjacency[:, cols(0)], origin + 128)
    base = history[:, cols(0)]
    values = apply_block(ends[:, cols(0)], u0m[:, cols(1)], left, 0, onehots, 0, rel, base, gat_a, weights)
    finish(values, base, 1.0 / 3.0, t1, parts2, cols(0))
    rel = place(adjacency[:, cols(3)], origin + 512)
    base = history[:, cols(3)]
    values = apply_block(u0m[:, cols(3)], ends[:, cols(1)], right, 0, onehots, 3, rel, base, gat_b, weights)
    finish(values, base, 1.0 / 3.0, t1, parts2, cols(3))
    for b, gathered in ((0, gat_a), (2, gat_b)):
        rel = place(mix(adjacency[:, cols(b)], adjacency[:, cols(b + 1)]), origin + (128 * b + 192))
        close, beyond = t1[:, cols(b)], t1[:, cols(b + 1)]
        values = apply_block(
            close, beyond, parts2, b * LANE, onehots, 4 + b, rel, straddle(close, beyond), gathered, weights
        )
        finish(values, u0m[:, cols(b + 1)], 0.5, t2, parts3, cols(b))
    for i, c in ((0, 0), (1, 3)):
        rim[:, cols(i)] = t1[:, cols(c)]
        rim_parts[:, cols(i)] = parts2[:, cols(c)]


def edge_kernel(
    place_ref, history, adjacency, far_one, far_two, onehots, weights, ends, end_parts, rim, rim_parts, t2m, parts3m,
    *rest,
):
    outs = rest[:8]
    low, high, left, right, left2, right2, edge, tips, t2, parts3, gat_a, gat_b = rest[8:]
    origin = place_ref[0]
    x = place_ref[1]
    odd = place_ref[3] == 1
    upper = place_ref[2] == 1
    low[...] = jnp.where(odd, far_two[...], far_one[...])
    high[...] = jnp.where(odd, far_one[...], far_two[...])
    low_adj = low[ROWS:, :].astype(jnp.int32)[0:NFACE]
    high_adj = high[ROWS:, :].astype(jnp.int32)[0:NFACE]
    rels = [
        place(low_adj, origin),
        place(high_adj, origin + 640),
        place(mix(low_adj, adjacency[:, cols(0)]), origin + 64),
        place(mix(adjacency[:, cols(3)], high_adj), origin + 576),
    ]
    for slot, rel in enumerate(rels):
        write_onehots(edge, slot, rel)
    put_parts(left, cols(0), low[0:ROWS, :])
    left[:, cols(1)] = end_parts[:, cols(0)]
    right[:, cols(0)] = end_parts[:, cols(1)]
    put_parts(right, cols(1), high[0:ROWS, :])
    left2[:, cols(1)] = rim_parts[:, cols(0)]
    right2[:, cols(0)] = rim_parts[:, cols(1)]
    t2[:, cols(1, 3)] = t2m[...]
    parts3[:, cols(1, 3)] = parts3m[...]
    close, beyond = low[0:ROWS, :], ends[:, cols(0)]
    base = straddle(close, beyond)
    values = apply_block(close, beyond, left, 0, edge, 0, rels[0], base, gat_a, weights)
    finish(values, base, 1.0 / 3.0, tips, left2, cols(0))
    close, beyond = ends[:, cols(1)], high[0:ROWS, :]
    base = straddle(close, beyond)
    values = apply_block(close, beyond, right, 0, edge, 1, rels[1], base, gat_b, weights)
    finish(values, base, 1.0 / 3.0, tips, right2, cols(1))
    close, beyond = tips[:, cols(0)], rim[:, cols(0)]
    values = apply_block(close, beyond, left2, 0, edge, 2, rels[2], straddle(close, beyond), gat_a, weights)
    finish(values, ends[:, cols(0)], 0.5, t2, parts3, cols(0))
    close, beyond = rim[:, cols(1)], tips[:, cols(1)]
    values = apply_block(close, beyond, right2, 0, edge, 3, rels[3], straddle(close, beyond), gat_b, weights)
    finish(values, ends[:, cols(1)], 0.5, t2, parts3, cols(4))
    for dx, gathered in ((2, gat_a), (1, gat_b), (3, gat_a), (0, gat_b)):
        b = (x + dx) & 3
        col = pl.multiple_of(b * LANE, LANE)
        rel = place(adjacency[:, pl.ds(col, LANE)], origin + 128 + col)
        close, beyond = t2[:, pl.ds(col, LANE)], t2[:, pl.ds(col + LANE, LANE)]
        values = apply_block(
            close, beyond, parts3, col, onehots, b, rel, straddle(close, beyond), gathered, weights
        )
        for v in range(NV):
            result = history[v * NP : (v + 1) * NP, pl.ds(col, LANE)] + values[v]
            below, above = result[0:32], result[32:64]
            outs[SLOTS.index((dx, 0))][v] = jnp.where(upper, above, below)
            outs[SLOTS.index((dx, 1))][v] = jnp.where(upper, below, above)


def source_of(x, core, slot):
    dx, dc = SLOTS[slot]
    return ((x - dx) & 3) * 2 + (core ^ dc)


def table_kernel(place_ref, schmid_hbm, hardening_hbm, mixing, renewing, schmid_map, hardening, sems):
    x = place_ref[1]
    core = place_ref[2]
    for copy in fetch([(schmid_hbm, schmid_map), (hardening_hbm, hardening)], sems):
        copy.wait()

    def variable(index):
        total = jnp.zeros(index.shape, jnp.int32)
        for slot in range(8):
            inside = (index >= slot * 48) & (index < slot * 48 + 48)
            total = jnp.where(inside, source_of(x, core, slot) * NV + ((index - slot * 48) >> 3), total)
        return total

    def onehot(hit):
        return jnp.where(hit, 1.0, 0.0).astype(BF16)

    def iota(shape, axis):
        return lax.broadcasted_iota(jnp.int32, shape, axis)

    columns = onehot(iota((48, ROWS), 0) == variable(iota((48, ROWS), 1)))
    rows = onehot(iota((ROWS, 48), 1) == variable(iota((ROWS, 48), 0)))
    slips = onehot(iota((96, 12), 1) == (iota((96, 12), 0) >> 3))
    spread = onehot(iota((12, 96), 0) == (iota((12, 96), 1) >> 3))
    wide = onehot((iota((96, ROWS), 0) & 7) == (iota((96, ROWS), 1) & 7)).astype(F32)
    tall = onehot((iota((ROWS, 96), 0) & 7) == (iota((ROWS, 96), 1) & 7)).astype(F32)
    second = (((1,), (1,)), ((), ()))
    for part, piece in enumerate(split(schmid_map[...])):
        picked = jnp.dot(slips, piece, preferred_element_type=F32).astype(BF16)
        picked = jnp.dot(picked, columns, preferred_element_type=F32) * wide
        mixing[part * 96 : (part + 1) * 96, :] = picked.astype(BF16)
    for part, piece in enumerate(split(hardening[...])):
        picked = lax.dot_general(rows, piece, second, preferred_element_type=F32).astype(BF16)
        picked = (jnp.dot(picked, spread, preferred_element_type=F32) * tall).astype(BF16)
        if part == 0:
            renewing[:, 0:96] = picked
            renewing[:, 96:192] = picked
        else:
            renewing[:, 192:288] = picked


def point_kernel(place_ref, mixing, renewing, *rest):
    own = [source_of(place_ref[1], place_ref[2], slot) < 4 for slot in range(8)]
    points = rest[:8]
    outs = rest[8:16]
    highs, lows, rate_parts = rest[16:]
    for slot in range(8):
        for i in range(NV):
            row = (slot * NV + i) * 8
            for g in range(4):
                high, low = split(points[slot][i, g * 8 : (g + 1) * 8, :])
                highs[row : row + 8, cols(g)] = high
                lows[row : row + 8, cols(g)] = low
    both = jnp.dot(mixing[...], highs[...], preferred_element_type=F32)
    rest_ = jnp.dot(mixing[0:96, :], lows[...], preferred_element_type=F32)
    rates = jnp.tanh(both[0:96] + (both[96:] + rest_))
    high, low = split(rates)
    rate_parts[0:96, :] = high
    rate_parts[96:192, :] = low
    rate_parts[192:288, :] = high
    change = jnp.dot(renewing[...], rate_parts[...], preferred_element_type=F32)
    for g in range(4):
        rows = [points[slot][0, g * 8 : (g + 1) * 8, :] + change[slot * 48 : slot * 48 + 8, cols(g)] for slot in range(8)]
        square = jnp.zeros((8, LANE), F32)
        for slot in range(8):
            square = square + jnp.where(own[slot], rows[slot] * rows[slot], 0.0)
        factor = 1.0 / jnp.maximum(jnp.sqrt(square), 1.0)
        for slot in range(8):
            outs[slot][0, g * 8 : (g + 1) * 8, :] = jnp.where(own[slot], rows[slot] * factor, rows[slot])
            for i in range(1, NV):
                row = (slot * NV + i) * 8
                outs[slot][i, g * 8 : (g + 1) * 8, :] = (
                    points[slot][i, g * 8 : (g + 1) * 8, :] + change[row : row + 8, cols(g)]
                )


def merge_kernel(slots):
    def kernel(place_ref, *rest):
        pieces = rest[: len(slots)]
        out, sems = rest[-2:]
        x = place_ref[1]
        core = place_ref[2]
        pairs = []
        for piece, slot in zip(pieces, slots):
            dx, dc = SLOTS[slot]
            col = pl.multiple_of(((x + dx) & 3) * LANE, LANE)
            row = pl.multiple_of((core ^ dc) * 32, 32)
            pairs.append((piece, out.at[:, pl.ds(row, 32), pl.ds(col, LANE)]))
        for copy in fetch(pairs, sems):
            copy.wait()

    return kernel


def vmem():
    return pl.BlockSpec(memory_space=pltpu.VMEM)


def smem():
    return pl.BlockSpec(memory_space=pltpu.SMEM)


def anywhere():
    return pl.BlockSpec(memory_space=pltpu.MemorySpace.HBM)


def call(kernel, where, args, outs, scratch=(), far_args=(), copies=0, hbm_out=False, aliases=None):
    space = anywhere if hbm_out else vmem
    far_args = [pltpu.with_memory_space_constraint(a, pltpu.MemorySpace.HBM) for a in far_args]
    return pl.pallas_call(
        kernel,
        out_shape=tuple(jax.ShapeDtypeStruct(shape, dtype) for shape, dtype in outs),
        in_specs=[smem()] + [vmem() for _ in args] + [anywhere() for _ in far_args],
        out_specs=tuple(space() for _ in outs),
        scratch_shapes=[pltpu.VMEM(shape, dtype) for shape, dtype in scratch]
        + ([pltpu.SemaphoreType.DMA((copies,))] if copies else []),
        input_output_aliases=aliases or {},
        compiler_params=pltpu.CompilerParams(vmem_limit_bytes=32 << 20),
    )(where, *args, *far_args)


def per_device(history, adjacency, volume_op, face_lift, schmid_map, hardening):
    count = lax.axis_size("zone")
    groups = lax.axis_size("var")
    flat = history.reshape(ROWS, NZ)
    zone = lax.axis_index("zone")
    var = lax.axis_index("var")
    where = jnp.stack([zone * NZ - 192, var >> 1, var & 1, zone & 1]).astype(jnp.int32)
    near = ((ROWS // 2, LANE), F32)
    far = ((ROWS + 8, LANE), F32)
    near_one, near_two, far_one, far_two, local, faces = call(
        pack_kernel,
        where,
        (),
        [near, near, far, far, ((ROWS, NZ), F32), ((NFACE, NZ), jnp.int32)],
        far_args=(flat, adjacency),
        copies=5,
    )

    def swap_pairs(shift):
        pairs = []
        for z in range(count):
            other = ((z + shift) ^ 1) - shift
            for v in range(groups):
                target = other * groups + v if 0 <= other < count else z * groups + (v ^ 1)
                pairs.append((z * groups + v, target))
        return pairs

    one, two = swap_pairs(1), swap_pairs(0)
    axes = ("zone", "var")
    near_one = lax.ppermute(near_one, axes, one)
    near_two = lax.ppermute(near_two, axes, two)
    far_one = lax.ppermute(far_one, axes, one)
    far_two = lax.ppermute(far_two, axes, two)
    buffer = ((2, KDIM, NV * LANE), BF16)
    wide = lambda n: ((ROWS, n * LANE), F32)
    pair = lambda n: ((2 * ROWS, n * LANE), BF16)
    *inner, weights = call(
        inner_kernel,
        where,
        (local, faces),
        [
            wide(5), pair(3), ((7, 256, MATMUL_FACES * LANE), BF16),
            wide(2), pair(2), wide(1), pair(1), ((2 * NP, KDIM), BF16),
        ],
        [buffer, buffer, ((NP, NP), F32), ((NFACE * NP, NP), F32)],
        far_args=(volume_op, face_lift.reshape(NFACE * NP, NP)),
        copies=2,
    )
    onehots = inner[2]
    middle = call(
        middle_kernel,
        where,
        (local, faces, near_one, near_two, *inner, weights),
        [wide(2), pair(2), wide(2), pair(2), wide(3), pair(3)],
        [pair(2), pair(2), wide(4), pair(4), buffer, buffer],
    )
    piece = ((NV, 32, LANE), F32)
    advected = call(
        edge_kernel,
        where,
        (local, faces, far_one, far_two, onehots, weights, *middle),
        [piece] * 8,
        [
            far, far, pair(2), pair(2), pair(2), pair(2), ((4, 256, MATMUL_FACES * LANE), BF16),
            wide(2), wide(5), pair(5), buffer, buffer,
        ],
    )

    def exchange(piece, dx, dc):
        if dx == 0 and dc == 0:
            return piece
        pairs = [(v, ((v // 2 + dx) % 4) * 2 + ((v % 2) ^ dc)) for v in range(8)]
        return lax.ppermute(piece, "var", pairs)

    points = [exchange(piece, dx, dc) for piece, (dx, dc) in zip(advected, SLOTS)]
    mixing, renewing = call(
        table_kernel,
        where,
        (),
        [((192, ROWS), BF16), ((ROWS, 288), BF16)],
        [((12, 48), F32), ((12, 48), F32)],
        far_args=(schmid_map.T, hardening),
        copies=2,
    )
    renewed = call(
        point_kernel,
        where,
        (mixing, renewing, *points),
        [piece] * 8,
        [((ROWS, 512), BF16), ((ROWS, 512), BF16), ((288, 512), BF16)],
    )
    returned = [exchange(piece, (4 - dx) % 4, dc) for piece, (dx, dc) in zip(renewed, SLOTS)]
    out = call(
        merge_kernel(EARLY), where, [returned[i] for i in EARLY], [((NV, NP, NZ), F32)],
        copies=len(EARLY), hbm_out=True,
    )[0]
    return call(
        merge_kernel(LATE), where, [returned[i] for i in LATE], [((NV, NP, NZ), F32)],
        far_args=(out,), copies=len(LATE), hbm_out=True, aliases={1 + len(LATE): 0},
    )[0]


def solution(mesh):
    in_specs = (P("var", None, "zone"), P(None, "zone"), P(), P(), P(), P())
    out_specs = P("var", None, "zone")

    return jax.shard_map(per_device, mesh=mesh, in_specs=in_specs, out_specs=out_specs, check_vma=False)
```

```python
import jax
import jax.numpy as jnp
from jax import lax
from jax.experimental import pallas as pl
from jax.experimental.pallas import tpu as pltpu
from jax.sharding import PartitionSpec as P


F32 = jnp.float32
BF16 = jnp.bfloat16
NV = 6
NP = 64
NZ = 512
ROWS = NV * NP
LANE = 128
HALF = 64
NFACE = 6
MATMUL_FACES = 4
KDIM = (NFACE + 1) * NP
SLOTS = [(0, 0), (2, 0), (2, 1), (1, 0), (3, 0), (1, 1), (3, 1), (0, 1)]
EARLY = (0, 1, 2, 7)
LATE = (3, 4, 5, 6)


def first_half(rows):
    return lax.broadcasted_iota(jnp.int32, (rows, LANE), 1) < HALF


def swap(x):
    return pltpu.roll(x, HALF, 1)


def straddle(left, right):
    return jnp.where(first_half(left.shape[0]), swap(left), swap(right))


def split(x):
    high = x.astype(BF16)
    low = (x - high.astype(F32)).astype(BF16)
    return high, low


def cols(b, n=1):
    return slice(b * LANE, (b + n) * LANE)


def put_parts(parts, where, x):
    high, low = split(x)
    parts[0:ROWS, where] = high
    parts[ROWS:, where] = low


def fetch(pairs, sems):
    copies = [pltpu.make_async_copy(source, target, sems.at[i]) for i, (source, target) in enumerate(pairs)]
    for copy in copies:
        copy.start()
    return copies


def pack_kernel(
    place_ref, history_hbm, adjacency_hbm, volume_hbm, face_hbm,
    near_one, near_two, far_one, far_two, history, adjacency, volume_op, face_lift, sems,
):
    half = ROWS // 2
    first = first_half(half)
    copies = fetch(
        [(history_hbm.at[:, cols(c)], history.at[:, cols(c)]) for c in (0, 3, 1, 2)]
        + [(adjacency_hbm, adjacency), (volume_hbm, volume_op), (face_hbm, face_lift)],
        sems,
    )
    for copy in copies:
        copy.wait()

    def put(near_up, near_down, far_up, far_down):
        near_up[...] = jnp.where(first, swap(history[0:half, cols(3)]), history[half:, cols(3)])
        near_down[...] = jnp.where(first, history[0:half, cols(0)], swap(history[half:, cols(0)]))
        far_up[0:ROWS, :] = straddle(history[:, cols(2)], history[:, cols(3)])
        far_down[0:ROWS, :] = straddle(history[:, cols(0)], history[:, cols(1)])
        for target, c in ((far_up, 3), (far_down, 0)):
            target[ROWS:, :] = jnp.zeros((8, LANE), F32)
            target[ROWS : ROWS + NFACE, :] = adjacency[:, cols(c)].astype(F32)

    @pl.when(place_ref[3] == 1)
    def _():
        put(near_one, near_two, far_one, far_two)

    @pl.when(place_ref[3] == 0)
    def _():
        put(near_two, near_one, far_two, far_one)


def place(adjacency, start):
    return jnp.where(adjacency < 0, 1000, adjacency - start)


def write_onehots(onehots, slot, rel):
    position = lax.broadcasted_iota(jnp.int32, (2 * LANE, LANE), 0)
    for face in range(MATMUL_FACES):
        hit = position == rel[face : face + 1, :]
        onehots[slot, :, cols(face)] = jnp.where(hit, 1.0, 0.0).astype(BF16)


def apply_block(close, beyond, parts, col, onehots, slot, rel, own, gathered, weights):
    for pair in range(MATMUL_FACES // 2):
        picked = jnp.dot(
            parts[:, pl.ds(col, 2 * LANE)], onehots[slot, :, cols(2 * pair, 2)], preferred_element_type=F32
        ).astype(BF16)
        for part in range(2):
            for v in range(NV):
                row = part * ROWS + v * NP
                for k in range(2):
                    face = 2 * pair + k
                    gathered[part, face * NP : (face + 1) * NP, cols(v)] = picked[row : row + NP, cols(k)]
    for face in range(MATMUL_FACES, NFACE):
        index = jnp.broadcast_to(rel[face : face + 1, :], (ROWS, LANE))
        lane = index & (LANE - 1)
        near = jnp.take_along_axis(close, lane, axis=1)
        far = jnp.take_along_axis(beyond, lane, axis=1)
        value = jnp.where(index >= 2 * LANE, 0.0, jnp.where(index >= LANE, far, near))
        for part, piece in enumerate(split(value)):
            for v in range(NV):
                gathered[part, face * NP : (face + 1) * NP, cols(v)] = piece[v * NP : (v + 1) * NP]
    for part, piece in enumerate(split(own)):
        for v in range(NV):
            gathered[part, NFACE * NP :, cols(v)] = piece[v * NP : (v + 1) * NP]
    both = jnp.dot(weights[...], gathered[0], preferred_element_type=F32)
    rest = jnp.dot(weights[0:NP, :], gathered[1], preferred_element_type=F32)
    value = both[0:NP] + (both[NP:] + rest)
    return [value[:, cols(v)] for v in range(NV)]


def finish(values, base, scale, target, parts, where):
    for v in range(NV):
        rows = slice(v * NP, (v + 1) * NP)
        result = base[rows] + values[v] * scale
        target[rows, where] = result
        high, low = split(result)
        parts[rows, where] = high
        parts[ROWS + v * NP : ROWS + (v + 1) * NP, where] = low


def mix(left, right):
    return jnp.where(first_half(NFACE), pltpu.roll(left, HALF, 1), pltpu.roll(right, HALF, 1))


def inner_kernel(
    place_ref, history, adjacency, volume_op, face_lift,
    u0, parts, onehots, t1, parts2, t2, parts3, weights,
    gat_a, gat_b,
):
    origin = place_ref[0]
    zero = jnp.zeros((ROWS, LANE), F32)
    blocks = [history[:, cols(b)] for b in range(4)]
    padded = [zero] + blocks + [zero]
    for c in range(5):
        u0[:, cols(c)] = straddle(padded[c], padded[c + 1])
    for c in range(1, 4):
        put_parts(parts, cols(c - 1), u0[:, cols(c)])
    for b in range(4):
        write_onehots(onehots, b, place(adjacency[:, cols(b)], origin + (128 * b + 128)))
    near = [mix(adjacency[:, cols(b)], adjacency[:, cols(b + 1)]) for b in range(3)]
    for b in range(3):
        write_onehots(onehots, 4 + b, place(near[b], origin + (128 * b + 192)))
    for lanes, matrix in ((slice(0, 384), face_lift[...].T), (slice(384, 448), volume_op[...].T)):
        high, low = split(matrix)
        weights[0:NP, lanes] = high
        weights[NP:, lanes] = low
    for b, gathered in ((2, gat_a), (3, gat_b)):
        rel = place(adjacency[:, cols(b - 1)], origin + 128 * b)
        values = apply_block(
            u0[:, cols(b - 1)], u0[:, cols(b)], parts, (b - 2) * LANE, onehots, b - 1, rel, blocks[b - 1], gathered, weights
        )
        finish(values, blocks[b - 1], 1.0 / 3.0, t1, parts2, cols(b - 2))
    rel = place(near[1], origin + 320)
    own = straddle(t1[:, cols(0)], t1[:, cols(1)])
    values = apply_block(t1[:, cols(0)], t1[:, cols(1)], parts2, 0, onehots, 5, rel, own, gat_a, weights)
    finish(values, u0[:, cols(2)], 0.5, t2, parts3, cols(0))


def middle_kernel(
    place_ref, history, adjacency, near_one, near_two, u0m, partsm, onehots, t1m, parts2m, t2m, parts3m, weights,
    ends, end_parts, rim, rim_parts, t2, parts3,
    left, right, t1, parts2, gat_a, gat_b,
):
    origin = place_ref[0]
    odd = place_ref[3] == 1
    half = ROWS // 2
    first = first_half(half)
    low = jnp.where(odd, near_two[...], near_one[...])
    high = jnp.where(odd, near_one[...], near_two[...])
    ends[0:half, cols(0)] = jnp.where(first, low, u0m[0:half, cols(0)])
    ends[half:, cols(0)] = jnp.where(first, swap(low), u0m[half:, cols(0)])
    ends[0:half, cols(1)] = jnp.where(first, u0m[0:half, cols(4)], swap(high))
    ends[half:, cols(1)] = jnp.where(first, u0m[half:, cols(4)], high)
    put_parts(end_parts, cols(0), ends[:, cols(0)])
    put_parts(end_parts, cols(1), ends[:, cols(1)])
    left[:, cols(0)] = end_parts[:, cols(0)]
    left[:, cols(1)] = partsm[:, cols(0)]
    right[:, cols(0)] = partsm[:, cols(2)]
    right[:, cols(1)] = end_parts[:, cols(1)]
    t1[:, cols(1, 2)] = t1m[...]
    parts2[:, cols(1, 2)] = parts2m[...]
    t2[:, cols(1)] = t2m[...]
    parts3[:, cols(1)] = parts3m[...]
    rel = place(adjacency[:, cols(0)], origin + 128)
    base = history[:, cols(0)]
    values = apply_block(ends[:, cols(0)], u0m[:, cols(1)], left, 0, onehots, 0, rel, base, gat_a, weights)
    finish(values, base, 1.0 / 3.0, t1, parts2, cols(0))
    rel = place(adjacency[:, cols(3)], origin + 512)
    base = history[:, cols(3)]
    values = apply_block(u0m[:, cols(3)], ends[:, cols(1)], right, 0, onehots, 3, rel, base, gat_b, weights)
    finish(values, base, 1.0 / 3.0, t1, parts2, cols(3))
    for b, gathered in ((0, gat_a), (2, gat_b)):
        rel = place(mix(adjacency[:, cols(b)], adjacency[:, cols(b + 1)]), origin + (128 * b + 192))
        close, beyond = t1[:, cols(b)], t1[:, cols(b + 1)]
        values = apply_block(
            close, beyond, parts2, b * LANE, onehots, 4 + b, rel, straddle(close, beyond), gathered, weights
        )
        finish(values, u0m[:, cols(b + 1)], 0.5, t2, parts3, cols(b))
    for i, c in ((0, 0), (1, 3)):
        rim[:, cols(i)] = t1[:, cols(c)]
        rim_parts[:, cols(i)] = parts2[:, cols(c)]


def edge_kernel(
    place_ref, history, adjacency, far_one, far_two, onehots, weights, ends, end_parts, rim, rim_parts, t2m, parts3m,
    *rest,
):
    outs = rest[:8]
    low, high, left, right, left2, right2, edge, tips, t2, parts3, gat_a, gat_b = rest[8:]
    origin = place_ref[0]
    x = place_ref[1]
    odd = place_ref[3] == 1
    upper = place_ref[2] == 1
    low[...] = jnp.where(odd, far_two[...], far_one[...])
    high[...] = jnp.where(odd, far_one[...], far_two[...])
    low_adj = low[ROWS:, :].astype(jnp.int32)[0:NFACE]
    high_adj = high[ROWS:, :].astype(jnp.int32)[0:NFACE]
    rels = [
        place(low_adj, origin),
        place(high_adj, origin + 640),
        place(mix(low_adj, adjacency[:, cols(0)]), origin + 64),
        place(mix(adjacency[:, cols(3)], high_adj), origin + 576),
    ]
    for slot, rel in enumerate(rels):
        write_onehots(edge, slot, rel)
    put_parts(left, cols(0), low[0:ROWS, :])
    left[:, cols(1)] = end_parts[:, cols(0)]
    right[:, cols(0)] = end_parts[:, cols(1)]
    put_parts(right, cols(1), high[0:ROWS, :])
    left2[:, cols(1)] = rim_parts[:, cols(0)]
    right2[:, cols(0)] = rim_parts[:, cols(1)]
    t2[:, cols(1, 3)] = t2m[...]
    parts3[:, cols(1, 3)] = parts3m[...]
    close, beyond = low[0:ROWS, :], ends[:, cols(0)]
    base = straddle(close, beyond)
    values = apply_block(close, beyond, left, 0, edge, 0, rels[0], base, gat_a, weights)
    finish(values, base, 1.0 / 3.0, tips, left2, cols(0))
    close, beyond = ends[:, cols(1)], high[0:ROWS, :]
    base = straddle(close, beyond)
    values = apply_block(close, beyond, right, 0, edge, 1, rels[1], base, gat_b, weights)
    finish(values, base, 1.0 / 3.0, tips, right2, cols(1))
    close, beyond = tips[:, cols(0)], rim[:, cols(0)]
    values = apply_block(close, beyond, left2, 0, edge, 2, rels[2], straddle(close, beyond), gat_a, weights)
    finish(values, ends[:, cols(0)], 0.5, t2, parts3, cols(0))
    close, beyond = rim[:, cols(1)], tips[:, cols(1)]
    values = apply_block(close, beyond, right2, 0, edge, 3, rels[3], straddle(close, beyond), gat_b, weights)
    finish(values, ends[:, cols(1)], 0.5, t2, parts3, cols(4))
    for dx, gathered in ((2, gat_a), (1, gat_b), (3, gat_a), (0, gat_b)):
        b = (x + dx) & 3
        col = pl.multiple_of(b * LANE, LANE)
        rel = place(adjacency[:, pl.ds(col, LANE)], origin + 128 + col)
        close, beyond = t2[:, pl.ds(col, LANE)], t2[:, pl.ds(col + LANE, LANE)]
        values = apply_block(
            close, beyond, parts3, col, onehots, b, rel, straddle(close, beyond), gathered, weights
        )
        for v in range(NV):
            result = history[v * NP : (v + 1) * NP, pl.ds(col, LANE)] + values[v]
            below, above = result[0:32], result[32:64]
            outs[SLOTS.index((dx, 0))][v] = jnp.where(upper, above, below)
            outs[SLOTS.index((dx, 1))][v] = jnp.where(upper, below, above)


def source_of(x, core, slot):
    dx, dc = SLOTS[slot]
    return ((x - dx) & 3) * 2 + (core ^ dc)


def table_kernel(place_ref, schmid_hbm, hardening_hbm, mixing, renewing, schmid_map, hardening, sems):
    x = place_ref[1]
    core = place_ref[2]
    for copy in fetch([(schmid_hbm, schmid_map), (hardening_hbm, hardening)], sems):
        copy.wait()

    def variable(index):
        total = jnp.zeros(index.shape, jnp.int32)
        for slot in range(8):
            inside = (index >= slot * 48) & (index < slot * 48 + 48)
            total = jnp.where(inside, source_of(x, core, slot) * NV + ((index - slot * 48) >> 3), total)
        return total

    def onehot(hit):
        return jnp.where(hit, 1.0, 0.0).astype(BF16)

    def iota(shape, axis):
        return lax.broadcasted_iota(jnp.int32, shape, axis)

    columns = onehot(iota((48, ROWS), 0) == variable(iota((48, ROWS), 1)))
    rows = onehot(iota((ROWS, 48), 1) == variable(iota((ROWS, 48), 0)))
    slips = onehot(iota((96, 12), 1) == (iota((96, 12), 0) >> 3))
    spread = onehot(iota((12, 96), 0) == (iota((12, 96), 1) >> 3))
    wide = onehot((iota((96, ROWS), 0) & 7) == (iota((96, ROWS), 1) & 7)).astype(F32)
    tall = onehot((iota((ROWS, 96), 0) & 7) == (iota((ROWS, 96), 1) & 7)).astype(F32)
    second = (((1,), (1,)), ((), ()))
    for part, piece in enumerate(split(schmid_map[...])):
        picked = jnp.dot(slips, piece, preferred_element_type=F32).astype(BF16)
        picked = jnp.dot(picked, columns, preferred_element_type=F32) * wide
        mixing[part * 96 : (part + 1) * 96, :] = picked.astype(BF16)
    for part, piece in enumerate(split(hardening[...])):
        picked = lax.dot_general(rows, piece, second, preferred_element_type=F32).astype(BF16)
        picked = (jnp.dot(picked, spread, preferred_element_type=F32) * tall).astype(BF16)
        if part == 0:
            renewing[:, 0:96] = picked
            renewing[:, 96:192] = picked
        else:
            renewing[:, 192:288] = picked


def point_kernel(place_ref, mixing, renewing, *rest):
    own = [source_of(place_ref[1], place_ref[2], slot) < 4 for slot in range(8)]
    points = rest[:8]
    outs = rest[8:16]
    highs, lows, rate_parts = rest[16:]
    for slot in range(8):
        for i in range(NV):
            row = (slot * NV + i) * 8
            for g in range(4):
                high, low = split(points[slot][i, g * 8 : (g + 1) * 8, :])
                highs[row : row + 8, cols(g)] = high
                lows[row : row + 8, cols(g)] = low
    both = jnp.dot(mixing[...], highs[...], preferred_element_type=F32)
    rest_ = jnp.dot(mixing[0:96, :], lows[...], preferred_element_type=F32)
    rates = jnp.tanh(both[0:96] + (both[96:] + rest_))
    high, low = split(rates)
    rate_parts[0:96, :] = high
    rate_parts[96:192, :] = low
    rate_parts[192:288, :] = high
    change = jnp.dot(renewing[...], rate_parts[...], preferred_element_type=F32)
    for g in range(4):
        rows = [points[slot][0, g * 8 : (g + 1) * 8, :] + change[slot * 48 : slot * 48 + 8, cols(g)] for slot in range(8)]
        square = jnp.zeros((8, LANE), F32)
        for slot in range(8):
            square = square + jnp.where(own[slot], rows[slot] * rows[slot], 0.0)
        factor = 1.0 / jnp.maximum(jnp.sqrt(square), 1.0)
        for slot in range(8):
            outs[slot][0, g * 8 : (g + 1) * 8, :] = jnp.where(own[slot], rows[slot] * factor, rows[slot])
            for i in range(1, NV):
                row = (slot * NV + i) * 8
                outs[slot][i, g * 8 : (g + 1) * 8, :] = (
                    points[slot][i, g * 8 : (g + 1) * 8, :] + change[row : row + 8, cols(g)]
                )


def merge_kernel(slots):
    def kernel(place_ref, *rest):
        pieces = rest[: len(slots)]
        out, sems = rest[-2:]
        x = place_ref[1]
        core = place_ref[2]
        pairs = []
        for piece, slot in zip(pieces, slots):
            dx, dc = SLOTS[slot]
            col = pl.multiple_of(((x + dx) & 3) * LANE, LANE)
            row = pl.multiple_of((core ^ dc) * 32, 32)
            pairs.append((piece, out.at[:, pl.ds(row, 32), pl.ds(col, LANE)]))
        for copy in fetch(pairs, sems):
            copy.wait()

    return kernel


def vmem():
    return pl.BlockSpec(memory_space=pltpu.VMEM)


def anywhere():
    return pl.BlockSpec(memory_space=pltpu.MemorySpace.HBM)


def position():
    zone = lax.axis_index("zone")
    var = lax.axis_index("var")
    return zone * NZ - 192, var >> 1, var & 1, zone & 1


def call(kernel, args, outs, scratch=(), far_args=(), copies=0, hbm_out=False, aliases=None):
    space = anywhere if hbm_out else vmem
    far_args = [pltpu.with_memory_space_constraint(a, pltpu.MemorySpace.HBM) for a in far_args]


    def placed(*refs):
        kernel(position(), *refs)

    return pl.pallas_call(
        placed,
        out_shape=tuple(jax.ShapeDtypeStruct(shape, dtype) for shape, dtype in outs),
        in_specs=[vmem() for _ in args] + [anywhere() for _ in far_args],
        out_specs=tuple(space() for _ in outs),
        scratch_shapes=[pltpu.VMEM(shape, dtype) for shape, dtype in scratch]
        + ([pltpu.SemaphoreType.DMA((copies,))] if copies else []),
        input_output_aliases=aliases or {},
        compiler_params=pltpu.CompilerParams(vmem_limit_bytes=32 << 20),
    )(*args, *far_args)


def per_device(history, adjacency, volume_op, face_lift, schmid_map, hardening):
    count = lax.axis_size("zone")
    groups = lax.axis_size("var")
    flat = history.reshape(ROWS, NZ)
    near = ((ROWS // 2, LANE), F32)
    far = ((ROWS + 8, LANE), F32)
    near_one, near_two, far_one, far_two, local, faces, volume, lifts = call(
        pack_kernel,
        (),
        [
            near, near, far, far, ((ROWS, NZ), F32), ((NFACE, NZ), jnp.int32), ((NP, NP), F32), ((NFACE * NP, NP), F32),
        ],
        far_args=(flat, adjacency, volume_op, face_lift.reshape(NFACE * NP, NP)),
        copies=7,
    )

    def swap_pairs(shift):
        pairs = []
        for z in range(count):
            other = ((z + shift) ^ 1) - shift
            for v in range(groups):
                target = other * groups + v if 0 <= other < count else z * groups + (v ^ 1)
                pairs.append((z * groups + v, target))
        return pairs

    one, two = swap_pairs(1), swap_pairs(0)
    axes = ("zone", "var")
    near_one = lax.ppermute(near_one, axes, one)
    near_two = lax.ppermute(near_two, axes, two)
    far_one = lax.ppermute(far_one, axes, one)
    far_two = lax.ppermute(far_two, axes, two)
    buffer = ((2, KDIM, NV * LANE), BF16)
    wide = lambda n: ((ROWS, n * LANE), F32)
    pair = lambda n: ((2 * ROWS, n * LANE), BF16)
    *inner, weights = call(
        inner_kernel,
        (local, faces, volume, lifts),
        [
            wide(5), pair(3), ((7, 256, MATMUL_FACES * LANE), BF16),
            wide(2), pair(2), wide(1), pair(1), ((2 * NP, KDIM), BF16),
        ],
        [buffer, buffer],
    )
    onehots = inner[2]
    middle = call(
        middle_kernel,
        (local, faces, near_one, near_two, *inner, weights),
        [wide(2), pair(2), wide(2), pair(2), wide(3), pair(3)],
        [pair(2), pair(2), wide(4), pair(4), buffer, buffer],
    )
    piece = ((NV, 32, LANE), F32)
    advected = call(
        edge_kernel,
        (local, faces, far_one, far_two, onehots, weights, *middle),
        [piece] * 8,
        [
            far, far, pair(2), pair(2), pair(2), pair(2), ((4, 256, MATMUL_FACES * LANE), BF16),
            wide(2), wide(5), pair(5), buffer, buffer,
        ],
    )

    def exchange(piece, dx, dc):
        if dx == 0 and dc == 0:
            return piece
        pairs = [(v, ((v // 2 + dx) % 4) * 2 + ((v % 2) ^ dc)) for v in range(8)]
        return lax.ppermute(piece, "var", pairs)

    points = [exchange(piece, dx, dc) for piece, (dx, dc) in zip(advected, SLOTS)]
    mixing, renewing = call(
        table_kernel,
        (),
        [((192, ROWS), BF16), ((ROWS, 288), BF16)],
        [((12, 48), F32), ((12, 48), F32)],
        far_args=(schmid_map.T, hardening),
        copies=2,
    )
    renewed = call(
        point_kernel,
        (mixing, renewing, *points),
        [piece] * 8,
        [((ROWS, 512), BF16), ((ROWS, 512), BF16), ((288, 512), BF16)],
    )
    returned = [exchange(piece, (4 - dx) % 4, dc) for piece, (dx, dc) in zip(renewed, SLOTS)]
    out = call(
        merge_kernel(EARLY), [returned[i] for i in EARLY], [((NV, NP, NZ), F32)],
        copies=len(EARLY), hbm_out=True,
    )[0]
    return call(
        merge_kernel(LATE), [returned[i] for i in LATE], [((NV, NP, NZ), F32)],
        far_args=(out,), copies=len(LATE), hbm_out=True, aliases={len(LATE): 0},
    )[0]


def solution(mesh):
    in_specs = (P("var", None, "zone"), P(None, "zone"), P(), P(), P(), P())
    out_specs = P("var", None, "zone")

    return jax.shard_map(per_device, mesh=mesh, in_specs=in_specs, out_specs=out_specs, check_vma=False)
```

```python
import jax
import jax.numpy as jnp
from jax import lax
from jax.experimental import pallas as pl
from jax.experimental.pallas import tpu as pltpu
from jax.sharding import PartitionSpec as P


F32 = jnp.float32
BF16 = jnp.bfloat16
NV = 6
NP = 64
NZ = 512
ROWS = NV * NP
LANE = 128
HALF = 64
NFACE = 6
MATMUL_FACES = 4
KDIM = (NFACE + 1) * NP
SLOTS = [(0, 0), (2, 0), (2, 1), (1, 0), (3, 0), (1, 1), (3, 1), (0, 1)]
EARLY = (0, 1, 2, 7)
LATE = (3, 4, 5, 6)


def first_half(rows):
    return lax.broadcasted_iota(jnp.int32, (rows, LANE), 1) < HALF


def swap(x):
    return pltpu.roll(x, HALF, 1)


def straddle(left, right):
    return jnp.where(first_half(left.shape[0]), swap(left), swap(right))


def split(x):
    high = x.astype(BF16)
    low = (x - high.astype(F32)).astype(BF16)
    return high, low


def cols(b, n=1):
    return slice(b * LANE, (b + n) * LANE)


def put_parts(parts, where, x):
    high, low = split(x)
    parts[0:ROWS, where] = high
    parts[ROWS:, where] = low


def fetch(pairs, sems):
    copies = [pltpu.make_async_copy(source, target, sems.at[i]) for i, (source, target) in enumerate(pairs)]
    for copy in copies:
        copy.start()
    return copies


def pack_kernel(
    place_ref, history_hbm, adjacency_hbm, volume_hbm, face_hbm,
    near_one, near_two, far_one, far_two, history, adjacency, volume_op, face_lift, sems,
):
    half = ROWS // 2
    first = first_half(half)
    copies = fetch(
        [(history_hbm.at[:, cols(c)], history.at[:, cols(c)]) for c in (0, 3, 1, 2)]
        + [(adjacency_hbm, adjacency), (volume_hbm, volume_op), (face_hbm, face_lift)],
        sems,
    )
    for copy in copies:
        copy.wait()

    def put(near_up, near_down, far_up, far_down):
        near_up[...] = jnp.where(first, swap(history[0:half, cols(3)]), history[half:, cols(3)])
        near_down[...] = jnp.where(first, history[0:half, cols(0)], swap(history[half:, cols(0)]))
        far_up[0:ROWS, :] = straddle(history[:, cols(2)], history[:, cols(3)])
        far_down[0:ROWS, :] = straddle(history[:, cols(0)], history[:, cols(1)])
        for target, c in ((far_up, 3), (far_down, 0)):
            target[ROWS:, :] = jnp.zeros((8, LANE), F32)
            target[ROWS : ROWS + NFACE, :] = adjacency[:, cols(c)].astype(F32)

    @pl.when(place_ref[3] == 1)
    def _():
        put(near_one, near_two, far_one, far_two)

    @pl.when(place_ref[3] == 0)
    def _():
        put(near_two, near_one, far_two, far_one)


def place(adjacency, start):
    return jnp.where(adjacency < 0, 1000, adjacency - start)


def write_onehots(onehots, slot, rel):
    position = lax.broadcasted_iota(jnp.int32, (2 * LANE, LANE), 0)
    for face in range(MATMUL_FACES):
        hit = position == rel[face : face + 1, :]
        onehots[slot, :, cols(face)] = jnp.where(hit, 1.0, 0.0).astype(BF16)


def apply_block(close, beyond, parts, col, onehots, slot, rel, own, gathered, weights):
    for pair in range(MATMUL_FACES // 2):
        picked = jnp.dot(
            parts[:, pl.ds(col, 2 * LANE)], onehots[slot, :, cols(2 * pair, 2)], preferred_element_type=F32
        ).astype(BF16)
        for part in range(2):
            for v in range(NV):
                row = part * ROWS + v * NP
                for k in range(2):
                    face = 2 * pair + k
                    gathered[part, face * NP : (face + 1) * NP, cols(v)] = picked[row : row + NP, cols(k)]
    for face in range(MATMUL_FACES, NFACE):
        index = jnp.broadcast_to(rel[face : face + 1, :], (ROWS, LANE))
        lane = index & (LANE - 1)
        near = jnp.take_along_axis(close, lane, axis=1)
        far = jnp.take_along_axis(beyond, lane, axis=1)
        value = jnp.where(index >= 2 * LANE, 0.0, jnp.where(index >= LANE, far, near))
        for part, piece in enumerate(split(value)):
            for v in range(NV):
                gathered[part, face * NP : (face + 1) * NP, cols(v)] = piece[v * NP : (v + 1) * NP]
    for part, piece in enumerate(split(own)):
        for v in range(NV):
            gathered[part, NFACE * NP :, cols(v)] = piece[v * NP : (v + 1) * NP]
    both = jnp.dot(weights[...], gathered[0], preferred_element_type=F32)
    rest = jnp.dot(weights[0:NP, :], gathered[1], preferred_element_type=F32)
    value = both[0:NP] + (both[NP:] + rest)
    return [value[:, cols(v)] for v in range(NV)]


def finish(values, base, scale, target, parts, where):
    for v in range(NV):
        rows = slice(v * NP, (v + 1) * NP)
        result = base[rows] + values[v] * scale
        target[rows, where] = result
        high, low = split(result)
        parts[rows, where] = high
        parts[ROWS + v * NP : ROWS + (v + 1) * NP, where] = low


def mix(left, right):
    return jnp.where(first_half(NFACE), pltpu.roll(left, HALF, 1), pltpu.roll(right, HALF, 1))


def inner_kernel(
    place_ref, history, adjacency, volume_op, face_lift,
    u0, parts, onehots, t1, parts2, t2, parts3, weights,
    gat_a, gat_b,
):
    origin = place_ref[0]
    zero = jnp.zeros((ROWS, LANE), F32)
    blocks = [history[:, cols(b)] for b in range(4)]
    padded = [zero] + blocks + [zero]
    for c in range(5):
        u0[:, cols(c)] = straddle(padded[c], padded[c + 1])
    for c in range(1, 4):
        put_parts(parts, cols(c - 1), u0[:, cols(c)])
    for b in range(4):
        write_onehots(onehots, b, place(adjacency[:, cols(b)], origin + (128 * b + 128)))
    near = [mix(adjacency[:, cols(b)], adjacency[:, cols(b + 1)]) for b in range(3)]
    for b in range(3):
        write_onehots(onehots, 4 + b, place(near[b], origin + (128 * b + 192)))
    for lanes, matrix in ((slice(0, 384), face_lift[...].T), (slice(384, 448), volume_op[...].T)):
        high, low = split(matrix)
        weights[0:NP, lanes] = high
        weights[NP:, lanes] = low
    for b, gathered in ((2, gat_a), (3, gat_b)):
        rel = place(adjacency[:, cols(b - 1)], origin + 128 * b)
        values = apply_block(
            u0[:, cols(b - 1)], u0[:, cols(b)], parts, (b - 2) * LANE, onehots, b - 1, rel, blocks[b - 1], gathered, weights
        )
        finish(values, blocks[b - 1], 1.0 / 3.0, t1, parts2, cols(b - 2))
    rel = place(near[1], origin + 320)
    own = straddle(t1[:, cols(0)], t1[:, cols(1)])
    values = apply_block(t1[:, cols(0)], t1[:, cols(1)], parts2, 0, onehots, 5, rel, own, gat_a, weights)
    finish(values, u0[:, cols(2)], 0.5, t2, parts3, cols(0))


def middle_kernel(
    place_ref, history, adjacency, near_one, near_two, u0m, partsm, onehots, t1m, parts2m, t2m, parts3m, weights,
    ends, end_parts, rim, rim_parts, t2, parts3,
    left, right, t1, parts2, gat_a, gat_b,
):
    origin = place_ref[0]
    odd = place_ref[3] == 1
    half = ROWS // 2
    first = first_half(half)
    low = jnp.where(odd, near_two[...], near_one[...])
    high = jnp.where(odd, near_one[...], near_two[...])
    ends[0:half, cols(0)] = jnp.where(first, low, u0m[0:half, cols(0)])
    ends[half:, cols(0)] = jnp.where(first, swap(low), u0m[half:, cols(0)])
    ends[0:half, cols(1)] = jnp.where(first, u0m[0:half, cols(4)], swap(high))
    ends[half:, cols(1)] = jnp.where(first, u0m[half:, cols(4)], high)
    put_parts(end_parts, cols(0), ends[:, cols(0)])
    put_parts(end_parts, cols(1), ends[:, cols(1)])
    left[:, cols(0)] = end_parts[:, cols(0)]
    left[:, cols(1)] = partsm[:, cols(0)]
    right[:, cols(0)] = partsm[:, cols(2)]
    right[:, cols(1)] = end_parts[:, cols(1)]
    t1[:, cols(1, 2)] = t1m[...]
    parts2[:, cols(1, 2)] = parts2m[...]
    t2[:, cols(1)] = t2m[...]
    parts3[:, cols(1)] = parts3m[...]
    rel = place(adjacency[:, cols(0)], origin + 128)
    base = history[:, cols(0)]
    values = apply_block(ends[:, cols(0)], u0m[:, cols(1)], left, 0, onehots, 0, rel, base, gat_a, weights)
    finish(values, base, 1.0 / 3.0, t1, parts2, cols(0))
    rel = place(adjacency[:, cols(3)], origin + 512)
    base = history[:, cols(3)]
    values = apply_block(u0m[:, cols(3)], ends[:, cols(1)], right, 0, onehots, 3, rel, base, gat_b, weights)
    finish(values, base, 1.0 / 3.0, t1, parts2, cols(3))
    for b, gathered in ((0, gat_a), (2, gat_b)):
        rel = place(mix(adjacency[:, cols(b)], adjacency[:, cols(b + 1)]), origin + (128 * b + 192))
        close, beyond = t1[:, cols(b)], t1[:, cols(b + 1)]
        values = apply_block(
            close, beyond, parts2, b * LANE, onehots, 4 + b, rel, straddle(close, beyond), gathered, weights
        )
        finish(values, u0m[:, cols(b + 1)], 0.5, t2, parts3, cols(b))
    for i, c in ((0, 0), (1, 3)):
        rim[:, cols(i)] = t1[:, cols(c)]
        rim_parts[:, cols(i)] = parts2[:, cols(c)]


def edge_kernel(
    place_ref, history, adjacency, far_one, far_two, onehots, weights, ends, end_parts, rim, rim_parts, t2m, parts3m,
    *rest,
):
    outs = rest[:2]
    t2, parts3, low, high, left, right, left2, right2, edge, tips, gat_a, gat_b = rest[2:]
    origin = place_ref[0]
    odd = place_ref[3] == 1
    low[...] = jnp.where(odd, far_two[...], far_one[...])
    high[...] = jnp.where(odd, far_one[...], far_two[...])
    low_adj = low[ROWS:, :].astype(jnp.int32)[0:NFACE]
    high_adj = high[ROWS:, :].astype(jnp.int32)[0:NFACE]
    rels = [
        place(low_adj, origin),
        place(high_adj, origin + 640),
        place(mix(low_adj, adjacency[:, cols(0)]), origin + 64),
        place(mix(adjacency[:, cols(3)], high_adj), origin + 576),
    ]
    for slot, rel in enumerate(rels):
        write_onehots(edge, slot, rel)
    put_parts(left, cols(0), low[0:ROWS, :])
    left[:, cols(1)] = end_parts[:, cols(0)]
    right[:, cols(0)] = end_parts[:, cols(1)]
    put_parts(right, cols(1), high[0:ROWS, :])
    left2[:, cols(1)] = rim_parts[:, cols(0)]
    right2[:, cols(0)] = rim_parts[:, cols(1)]
    t2[:, cols(1, 3)] = t2m[...]
    parts3[:, cols(1, 3)] = parts3m[...]
    close, beyond = low[0:ROWS, :], ends[:, cols(0)]
    base = straddle(close, beyond)
    values = apply_block(close, beyond, left, 0, edge, 0, rels[0], base, gat_a, weights)
    finish(values, base, 1.0 / 3.0, tips, left2, cols(0))
    close, beyond = ends[:, cols(1)], high[0:ROWS, :]
    base = straddle(close, beyond)
    values = apply_block(close, beyond, right, 0, edge, 1, rels[1], base, gat_b, weights)
    finish(values, base, 1.0 / 3.0, tips, right2, cols(1))
    close, beyond = tips[:, cols(0)], rim[:, cols(0)]
    values = apply_block(close, beyond, left2, 0, edge, 2, rels[2], straddle(close, beyond), gat_a, weights)
    finish(values, ends[:, cols(0)], 0.5, t2, parts3, cols(0))
    close, beyond = rim[:, cols(1)], tips[:, cols(1)]
    values = apply_block(close, beyond, right2, 0, edge, 3, rels[3], straddle(close, beyond), gat_b, weights)
    finish(values, ends[:, cols(1)], 0.5, t2, parts3, cols(4))
    last_block(place_ref, 2, history, adjacency, weights, onehots, t2, parts3, gat_a, outs)


def last_block(place_ref, dx, history, adjacency, weights, onehots, t2, parts3, gathered, outs):
    b = (place_ref[1] + dx) & 3
    upper = place_ref[2] == 1
    col = pl.multiple_of(b * LANE, LANE)
    rel = place(adjacency[:, pl.ds(col, LANE)], place_ref[0] + 128 + col)
    close, beyond = t2[:, pl.ds(col, LANE)], t2[:, pl.ds(col + LANE, LANE)]
    values = apply_block(close, beyond, parts3, col, onehots, b, rel, straddle(close, beyond), gathered, weights)
    for v in range(NV):
        result = history[v * NP : (v + 1) * NP, pl.ds(col, LANE)] + values[v]
        below, above = result[0:32], result[32:64]
        outs[0][v] = jnp.where(upper, above, below)
        outs[1][v] = jnp.where(upper, below, above)


def last_kernel(dx):
    def kernel(place_ref, history, adjacency, weights, onehots, t2, parts3, kept, crossed, gathered):
        last_block(place_ref, dx, history, adjacency, weights, onehots, t2, parts3, gathered, (kept, crossed))

    return kernel


def source_of(x, core, slot):
    dx, dc = SLOTS[slot]
    return ((x - dx) & 3) * 2 + (core ^ dc)


def table_kernel(place_ref, schmid_hbm, hardening_hbm, mixing, renewing, schmid_map, hardening, sems):
    x = place_ref[1]
    core = place_ref[2]
    for copy in fetch([(schmid_hbm, schmid_map), (hardening_hbm, hardening)], sems):
        copy.wait()

    def variable(index):
        total = jnp.zeros(index.shape, jnp.int32)
        for slot in range(8):
            inside = (index >= slot * 48) & (index < slot * 48 + 48)
            total = jnp.where(inside, source_of(x, core, slot) * NV + ((index - slot * 48) >> 3), total)
        return total

    def onehot(hit):
        return jnp.where(hit, 1.0, 0.0).astype(BF16)

    def iota(shape, axis):
        return lax.broadcasted_iota(jnp.int32, shape, axis)

    columns = onehot(iota((48, ROWS), 0) == variable(iota((48, ROWS), 1)))
    rows = onehot(iota((ROWS, 48), 1) == variable(iota((ROWS, 48), 0)))
    slips = onehot(iota((96, 12), 1) == (iota((96, 12), 0) >> 3))
    spread = onehot(iota((12, 96), 0) == (iota((12, 96), 1) >> 3))
    wide = onehot((iota((96, ROWS), 0) & 7) == (iota((96, ROWS), 1) & 7)).astype(F32)
    tall = onehot((iota((ROWS, 96), 0) & 7) == (iota((ROWS, 96), 1) & 7)).astype(F32)
    second = (((1,), (1,)), ((), ()))
    for part, piece in enumerate(split(schmid_map[...])):
        picked = jnp.dot(slips, piece, preferred_element_type=F32).astype(BF16)
        picked = jnp.dot(picked, columns, preferred_element_type=F32) * wide
        mixing[part * 96 : (part + 1) * 96, :] = picked.astype(BF16)
    for part, piece in enumerate(split(hardening[...])):
        picked = lax.dot_general(rows, piece, second, preferred_element_type=F32).astype(BF16)
        picked = (jnp.dot(picked, spread, preferred_element_type=F32) * tall).astype(BF16)
        if part == 0:
            renewing[:, 0:96] = picked
            renewing[:, 96:192] = picked
        else:
            renewing[:, 192:288] = picked


def point_kernel(place_ref, mixing, renewing, *rest):
    own = [source_of(place_ref[1], place_ref[2], slot) < 4 for slot in range(8)]
    points = rest[:8]
    outs = rest[8:16]
    highs, lows, rate_parts = rest[16:]
    for slot in range(8):
        for i in range(NV):
            row = (slot * NV + i) * 8
            for g in range(4):
                high, low = split(points[slot][i, g * 8 : (g + 1) * 8, :])
                highs[row : row + 8, cols(g)] = high
                lows[row : row + 8, cols(g)] = low
    both = jnp.dot(mixing[...], highs[...], preferred_element_type=F32)
    rest_ = jnp.dot(mixing[0:96, :], lows[...], preferred_element_type=F32)
    rates = jnp.tanh(both[0:96] + (both[96:] + rest_))
    high, low = split(rates)
    rate_parts[0:96, :] = high
    rate_parts[96:192, :] = low
    rate_parts[192:288, :] = high
    change = jnp.dot(renewing[...], rate_parts[...], preferred_element_type=F32)
    for g in range(4):
        rows = [points[slot][0, g * 8 : (g + 1) * 8, :] + change[slot * 48 : slot * 48 + 8, cols(g)] for slot in range(8)]
        square = jnp.zeros((8, LANE), F32)
        for slot in range(8):
            square = square + jnp.where(own[slot], rows[slot] * rows[slot], 0.0)
        factor = 1.0 / jnp.maximum(jnp.sqrt(square), 1.0)
        for slot in range(8):
            outs[slot][0, g * 8 : (g + 1) * 8, :] = jnp.where(own[slot], rows[slot] * factor, rows[slot])
            for i in range(1, NV):
                row = (slot * NV + i) * 8
                outs[slot][i, g * 8 : (g + 1) * 8, :] = (
                    points[slot][i, g * 8 : (g + 1) * 8, :] + change[row : row + 8, cols(g)]
                )


def merge_kernel(slots):
    def kernel(place_ref, *rest):
        pieces = rest[: len(slots)]
        out, sems = rest[-2:]
        x = place_ref[1]
        core = place_ref[2]
        pairs = []
        for piece, slot in zip(pieces, slots):
            dx, dc = SLOTS[slot]
            col = pl.multiple_of(((x + dx) & 3) * LANE, LANE)
            row = pl.multiple_of((core ^ dc) * 32, 32)
            pairs.append((piece, out.at[:, pl.ds(row, 32), pl.ds(col, LANE)]))
        for copy in fetch(pairs, sems):
            copy.wait()

    return kernel


def vmem():
    return pl.BlockSpec(memory_space=pltpu.VMEM)


def anywhere():
    return pl.BlockSpec(memory_space=pltpu.MemorySpace.HBM)


def position():
    zone = lax.axis_index("zone")
    var = lax.axis_index("var")
    return zone * NZ - 192, var >> 1, var & 1, zone & 1


def call(kernel, args, outs, scratch=(), far_args=(), copies=0, hbm_out=False, aliases=None):
    space = anywhere if hbm_out else vmem
    far_args = [pltpu.with_memory_space_constraint(a, pltpu.MemorySpace.HBM) for a in far_args]


    def placed(*refs):
        kernel(position(), *refs)

    return pl.pallas_call(
        placed,
        out_shape=tuple(jax.ShapeDtypeStruct(shape, dtype) for shape, dtype in outs),
        in_specs=[vmem() for _ in args] + [anywhere() for _ in far_args],
        out_specs=tuple(space() for _ in outs),
        scratch_shapes=[pltpu.VMEM(shape, dtype) for shape, dtype in scratch]
        + ([pltpu.SemaphoreType.DMA((copies,))] if copies else []),
        input_output_aliases=aliases or {},
        compiler_params=pltpu.CompilerParams(vmem_limit_bytes=32 << 20),
    )(*args, *far_args)


def per_device(history, adjacency, volume_op, face_lift, schmid_map, hardening):
    count = lax.axis_size("zone")
    groups = lax.axis_size("var")
    flat = history.reshape(ROWS, NZ)
    near = ((ROWS // 2, LANE), F32)
    far = ((ROWS + 8, LANE), F32)
    near_one, near_two, far_one, far_two, local, faces, volume, lifts = call(
        pack_kernel,
        (),
        [
            near, near, far, far, ((ROWS, NZ), F32), ((NFACE, NZ), jnp.int32), ((NP, NP), F32), ((NFACE * NP, NP), F32),
        ],
        far_args=(flat, adjacency, volume_op, face_lift.reshape(NFACE * NP, NP)),
        copies=7,
    )

    def swap_pairs(shift):
        pairs = []
        for z in range(count):
            other = ((z + shift) ^ 1) - shift
            for v in range(groups):
                target = other * groups + v if 0 <= other < count else z * groups + (v ^ 1)
                pairs.append((z * groups + v, target))
        return pairs

    one, two = swap_pairs(1), swap_pairs(0)
    axes = ("zone", "var")
    near_one = lax.ppermute(near_one, axes, one)
    near_two = lax.ppermute(near_two, axes, two)
    far_one = lax.ppermute(far_one, axes, one)
    far_two = lax.ppermute(far_two, axes, two)
    buffer = ((2, KDIM, NV * LANE), BF16)
    wide = lambda n: ((ROWS, n * LANE), F32)
    pair = lambda n: ((2 * ROWS, n * LANE), BF16)
    *inner, weights = call(
        inner_kernel,
        (local, faces, volume, lifts),
        [
            wide(5), pair(3), ((7, 256, MATMUL_FACES * LANE), BF16),
            wide(2), pair(2), wide(1), pair(1), ((2 * NP, KDIM), BF16),
        ],
        [buffer, buffer],
    )
    onehots = inner[2]
    middle = call(
        middle_kernel,
        (local, faces, near_one, near_two, *inner, weights),
        [wide(2), pair(2), wide(2), pair(2), wide(3), pair(3)],
        [pair(2), pair(2), wide(4), pair(4), buffer, buffer],
    )
    piece = ((NV, 32, LANE), F32)
    *ahead, t2, parts3 = call(
        edge_kernel,
        (local, faces, far_one, far_two, onehots, weights, *middle),
        [piece, piece, wide(5), pair(5)],
        [
            far, far, pair(2), pair(2), pair(2), pair(2), ((4, 256, MATMUL_FACES * LANE), BF16),
            wide(2), buffer, buffer,
        ],
    )
    ready = {(2, 0): ahead[0], (2, 1): ahead[1]}
    for dx in (1, 3, 0):
        ready[dx, 0], ready[dx, 1] = call(
            last_kernel(dx), (local, faces, weights, onehots, t2, parts3), [piece, piece], [buffer]
        )
    advected = [ready[slot] for slot in SLOTS]

    def exchange(piece, dx, dc):
        if dx == 0 and dc == 0:
            return piece
        pairs = [(v, ((v // 2 + dx) % 4) * 2 + ((v % 2) ^ dc)) for v in range(8)]
        return lax.ppermute(piece, "var", pairs)

    points = [exchange(piece, dx, dc) for piece, (dx, dc) in zip(advected, SLOTS)]
    mixing, renewing = call(
        table_kernel,
        (),
        [((192, ROWS), BF16), ((ROWS, 288), BF16)],
        [((12, 48), F32), ((12, 48), F32)],
        far_args=(schmid_map.T, hardening),
        copies=2,
    )
    renewed = call(
        point_kernel,
        (mixing, renewing, *points),
        [piece] * 8,
        [((ROWS, 512), BF16), ((ROWS, 512), BF16), ((288, 512), BF16)],
    )
    returned = [exchange(piece, (4 - dx) % 4, dc) for piece, (dx, dc) in zip(renewed, SLOTS)]
    out = call(
        merge_kernel(EARLY), [returned[i] for i in EARLY], [((NV, NP, NZ), F32)],
        copies=len(EARLY), hbm_out=True,
    )[0]
    return call(
        merge_kernel(LATE), [returned[i] for i in LATE], [((NV, NP, NZ), F32)],
        far_args=(out,), copies=len(LATE), hbm_out=True, aliases={len(LATE): 0},
    )[0]


def solution(mesh):
    in_specs = (P("var", None, "zone"), P(None, "zone"), P(), P(), P(), P())
    out_specs = P("var", None, "zone")

    return jax.shard_map(per_device, mesh=mesh, in_specs=in_specs, out_specs=out_specs, check_vma=False)
```

```python
import jax
import jax.numpy as jnp
from jax import lax
from jax.experimental import pallas as pl
from jax.experimental.pallas import tpu as pltpu
from jax.sharding import PartitionSpec as P


F32 = jnp.float32
BF16 = jnp.bfloat16
NV = 6
NP = 64
NZ = 512
ROWS = NV * NP
LANE = 128
HALF = 64
NFACE = 6
MATMUL_FACES = 4
KDIM = (NFACE + 1) * NP
SLOTS = [(0, 0), (2, 0), (2, 1), (1, 0), (3, 0), (1, 1), (3, 1), (0, 1)]
EARLY = (0, 1, 2, 7)
LATE = (3, 4, 5, 6)


def first_half(rows):
    return lax.broadcasted_iota(jnp.int32, (rows, LANE), 1) < HALF


def swap(x):
    return pltpu.roll(x, HALF, 1)


def straddle(left, right):
    return jnp.where(first_half(left.shape[0]), swap(left), swap(right))


def split(x):
    high = x.astype(BF16)
    low = (x - high.astype(F32)).astype(BF16)
    return high, low


def cols(b, n=1):
    return slice(b * LANE, (b + n) * LANE)


def put_parts(parts, where, x):
    high, low = split(x)
    parts[0:ROWS, where] = high
    parts[ROWS:, where] = low


def fetch(pairs, sems):
    copies = [pltpu.make_async_copy(source, target, sems.at[i]) for i, (source, target) in enumerate(pairs)]
    for copy in copies:
        copy.start()
    return copies


def pack_kernel(
    place_ref, history_hbm, adjacency_hbm, volume_hbm, face_hbm,
    near_one, near_two, far_one, far_two, history, adjacency, volume_op, face_lift, sems,
):
    half = ROWS // 2
    first = first_half(half)
    copies = fetch(
        [(history_hbm.at[r : r + 96, :], history.at[r : r + 96, :]) for r in range(0, ROWS, 96)]
        + [(adjacency_hbm, adjacency), (volume_hbm, volume_op), (face_hbm, face_lift)],
        sems,
    )
    for copy in copies:
        copy.wait()

    def put(near_up, near_down, far_up, far_down):
        near_up[...] = jnp.where(first, swap(history[0:half, cols(3)]), history[half:, cols(3)])
        near_down[...] = jnp.where(first, history[0:half, cols(0)], swap(history[half:, cols(0)]))
        far_up[0:ROWS, :] = straddle(history[:, cols(2)], history[:, cols(3)])
        far_down[0:ROWS, :] = straddle(history[:, cols(0)], history[:, cols(1)])
        for target, c in ((far_up, 3), (far_down, 0)):
            target[ROWS:, :] = jnp.zeros((8, LANE), F32)
            target[ROWS : ROWS + NFACE, :] = adjacency[:, cols(c)].astype(F32)

    @pl.when(place_ref[3] == 1)
    def _():
        put(near_one, near_two, far_one, far_two)

    @pl.when(place_ref[3] == 0)
    def _():
        put(near_two, near_one, far_two, far_one)


def place(adjacency, start):
    return jnp.where(adjacency < 0, 1000, adjacency - start)


def write_onehots(onehots, slot, rel):
    position = lax.broadcasted_iota(jnp.int32, (2 * LANE, LANE), 0)
    for face in range(MATMUL_FACES):
        hit = position == rel[face : face + 1, :]
        onehots[slot, :, cols(face)] = jnp.where(hit, 1.0, 0.0).astype(BF16)


def apply_block(close, beyond, parts, col, onehots, slot, rel, own, gathered, weights):
    for pair in range(MATMUL_FACES // 2):
        picked = jnp.dot(
            parts[:, pl.ds(col, 2 * LANE)], onehots[slot, :, cols(2 * pair, 2)], preferred_element_type=F32
        ).astype(BF16)
        for part in range(2):
            for v in range(NV):
                row = part * ROWS + v * NP
                for k in range(2):
                    face = 2 * pair + k
                    gathered[part, face * NP : (face + 1) * NP, cols(v)] = picked[row : row + NP, cols(k)]
    for face in range(MATMUL_FACES, NFACE):
        index = jnp.broadcast_to(rel[face : face + 1, :], (ROWS, LANE))
        lane = index & (LANE - 1)
        near = jnp.take_along_axis(close, lane, axis=1)
        far = jnp.take_along_axis(beyond, lane, axis=1)
        value = jnp.where(index >= 2 * LANE, 0.0, jnp.where(index >= LANE, far, near))
        for part, piece in enumerate(split(value)):
            for v in range(NV):
                gathered[part, face * NP : (face + 1) * NP, cols(v)] = piece[v * NP : (v + 1) * NP]
    for part, piece in enumerate(split(own)):
        for v in range(NV):
            gathered[part, NFACE * NP :, cols(v)] = piece[v * NP : (v + 1) * NP]
    both = jnp.dot(weights[...], gathered[0], preferred_element_type=F32)
    rest = jnp.dot(weights[0:NP, :], gathered[1], preferred_element_type=F32)
    value = both[0:NP] + (both[NP:] + rest)
    return [value[:, cols(v)] for v in range(NV)]


def finish(values, base, scale, target, parts, where):
    for v in range(NV):
        rows = slice(v * NP, (v + 1) * NP)
        result = base[rows] + values[v] * scale
        target[rows, where] = result
        high, low = split(result)
        parts[rows, where] = high
        parts[ROWS + v * NP : ROWS + (v + 1) * NP, where] = low


def mix(left, right):
    return jnp.where(first_half(NFACE), pltpu.roll(left, HALF, 1), pltpu.roll(right, HALF, 1))


def inner_kernel(
    place_ref, history, adjacency, volume_op, face_lift,
    u0, parts, onehots, t1, parts2, t2, parts3, weights,
    gat_a, gat_b,
):
    origin = place_ref[0]
    zero = jnp.zeros((ROWS, LANE), F32)
    blocks = [history[:, cols(b)] for b in range(4)]
    padded = [zero] + blocks + [zero]
    for c in range(5):
        u0[:, cols(c)] = straddle(padded[c], padded[c + 1])
    for c in range(1, 4):
        put_parts(parts, cols(c - 1), u0[:, cols(c)])
    for b in range(4):
        write_onehots(onehots, b, place(adjacency[:, cols(b)], origin + (128 * b + 128)))
    near = [mix(adjacency[:, cols(b)], adjacency[:, cols(b + 1)]) for b in range(3)]
    for b in range(3):
        write_onehots(onehots, 4 + b, place(near[b], origin + (128 * b + 192)))
    for lanes, matrix in ((slice(0, 384), face_lift[...].T), (slice(384, 448), volume_op[...].T)):
        high, low = split(matrix)
        weights[0:NP, lanes] = high
        weights[NP:, lanes] = low
    for b, gathered in ((2, gat_a), (3, gat_b)):
        rel = place(adjacency[:, cols(b - 1)], origin + 128 * b)
        values = apply_block(
            u0[:, cols(b - 1)], u0[:, cols(b)], parts, (b - 2) * LANE, onehots, b - 1, rel, blocks[b - 1], gathered, weights
        )
        finish(values, blocks[b - 1], 1.0 / 3.0, t1, parts2, cols(b - 2))
    rel = place(near[1], origin + 320)
    own = straddle(t1[:, cols(0)], t1[:, cols(1)])
    values = apply_block(t1[:, cols(0)], t1[:, cols(1)], parts2, 0, onehots, 5, rel, own, gat_a, weights)
    finish(values, u0[:, cols(2)], 0.5, t2, parts3, cols(0))


def middle_kernel(
    place_ref, history, adjacency, near_one, near_two, u0m, partsm, onehots, t1m, parts2m, t2m, parts3m, weights,
    ends, end_parts, rim, rim_parts, t2, parts3,
    left, right, t1, parts2, gat_a, gat_b,
):
    origin = place_ref[0]
    odd = place_ref[3] == 1
    half = ROWS // 2
    first = first_half(half)
    low = jnp.where(odd, near_two[...], near_one[...])
    high = jnp.where(odd, near_one[...], near_two[...])
    ends[0:half, cols(0)] = jnp.where(first, low, u0m[0:half, cols(0)])
    ends[half:, cols(0)] = jnp.where(first, swap(low), u0m[half:, cols(0)])
    ends[0:half, cols(1)] = jnp.where(first, u0m[0:half, cols(4)], swap(high))
    ends[half:, cols(1)] = jnp.where(first, u0m[half:, cols(4)], high)
    put_parts(end_parts, cols(0), ends[:, cols(0)])
    put_parts(end_parts, cols(1), ends[:, cols(1)])
    left[:, cols(0)] = end_parts[:, cols(0)]
    left[:, cols(1)] = partsm[:, cols(0)]
    right[:, cols(0)] = partsm[:, cols(2)]
    right[:, cols(1)] = end_parts[:, cols(1)]
    t1[:, cols(1, 2)] = t1m[...]
    parts2[:, cols(1, 2)] = parts2m[...]
    t2[:, cols(1)] = t2m[...]
    parts3[:, cols(1)] = parts3m[...]
    rel = place(adjacency[:, cols(0)], origin + 128)
    base = history[:, cols(0)]
    values = apply_block(ends[:, cols(0)], u0m[:, cols(1)], left, 0, onehots, 0, rel, base, gat_a, weights)
    finish(values, base, 1.0 / 3.0, t1, parts2, cols(0))
    rel = place(adjacency[:, cols(3)], origin + 512)
    base = history[:, cols(3)]
    values = apply_block(u0m[:, cols(3)], ends[:, cols(1)], right, 0, onehots, 3, rel, base, gat_b, weights)
    finish(values, base, 1.0 / 3.0, t1, parts2, cols(3))
    for b, gathered in ((0, gat_a), (2, gat_b)):
        rel = place(mix(adjacency[:, cols(b)], adjacency[:, cols(b + 1)]), origin + (128 * b + 192))
        close, beyond = t1[:, cols(b)], t1[:, cols(b + 1)]
        values = apply_block(
            close, beyond, parts2, b * LANE, onehots, 4 + b, rel, straddle(close, beyond), gathered, weights
        )
        finish(values, u0m[:, cols(b + 1)], 0.5, t2, parts3, cols(b))
    for i, c in ((0, 0), (1, 3)):
        rim[:, cols(i)] = t1[:, cols(c)]
        rim_parts[:, cols(i)] = parts2[:, cols(c)]


def edge_kernel(
    place_ref, history, adjacency, far_one, far_two, onehots, weights, ends, end_parts, rim, rim_parts, t2m, parts3m,
    *rest,
):
    outs = rest[:2]
    t2, parts3, low, high, left, right, left2, right2, edge, tips, gat_a, gat_b = rest[2:]
    origin = place_ref[0]
    odd = place_ref[3] == 1
    low[...] = jnp.where(odd, far_two[...], far_one[...])
    high[...] = jnp.where(odd, far_one[...], far_two[...])
    low_adj = low[ROWS:, :].astype(jnp.int32)[0:NFACE]
    high_adj = high[ROWS:, :].astype(jnp.int32)[0:NFACE]
    rels = [
        place(low_adj, origin),
        place(high_adj, origin + 640),
        place(mix(low_adj, adjacency[:, cols(0)]), origin + 64),
        place(mix(adjacency[:, cols(3)], high_adj), origin + 576),
    ]
    for slot, rel in enumerate(rels):
        write_onehots(edge, slot, rel)
    put_parts(left, cols(0), low[0:ROWS, :])
    left[:, cols(1)] = end_parts[:, cols(0)]
    right[:, cols(0)] = end_parts[:, cols(1)]
    put_parts(right, cols(1), high[0:ROWS, :])
    left2[:, cols(1)] = rim_parts[:, cols(0)]
    right2[:, cols(0)] = rim_parts[:, cols(1)]
    t2[:, cols(1, 3)] = t2m[...]
    parts3[:, cols(1, 3)] = parts3m[...]
    close, beyond = low[0:ROWS, :], ends[:, cols(0)]
    base = straddle(close, beyond)
    values = apply_block(close, beyond, left, 0, edge, 0, rels[0], base, gat_a, weights)
    finish(values, base, 1.0 / 3.0, tips, left2, cols(0))
    close, beyond = ends[:, cols(1)], high[0:ROWS, :]
    base = straddle(close, beyond)
    values = apply_block(close, beyond, right, 0, edge, 1, rels[1], base, gat_b, weights)
    finish(values, base, 1.0 / 3.0, tips, right2, cols(1))
    close, beyond = tips[:, cols(0)], rim[:, cols(0)]
    values = apply_block(close, beyond, left2, 0, edge, 2, rels[2], straddle(close, beyond), gat_a, weights)
    finish(values, ends[:, cols(0)], 0.5, t2, parts3, cols(0))
    close, beyond = rim[:, cols(1)], tips[:, cols(1)]
    values = apply_block(close, beyond, right2, 0, edge, 3, rels[3], straddle(close, beyond), gat_b, weights)
    finish(values, ends[:, cols(1)], 0.5, t2, parts3, cols(4))
    last_block(place_ref, 2, history, adjacency, weights, onehots, t2, parts3, gat_a, outs)


def last_block(place_ref, dx, history, adjacency, weights, onehots, t2, parts3, gathered, outs):
    b = (place_ref[1] + dx) & 3
    upper = place_ref[2] == 1
    col = pl.multiple_of(b * LANE, LANE)
    rel = place(adjacency[:, pl.ds(col, LANE)], place_ref[0] + 128 + col)
    close, beyond = t2[:, pl.ds(col, LANE)], t2[:, pl.ds(col + LANE, LANE)]
    values = apply_block(close, beyond, parts3, col, onehots, b, rel, straddle(close, beyond), gathered, weights)
    for v in range(NV):
        result = history[v * NP : (v + 1) * NP, pl.ds(col, LANE)] + values[v]
        below, above = result[0:32], result[32:64]
        outs[0][v] = jnp.where(upper, above, below)
        outs[1][v] = jnp.where(upper, below, above)


def last_kernel(steps):
    def kernel(place_ref, history, adjacency, weights, onehots, t2, parts3, *rest):
        outs = rest[: 2 * len(steps)]
        buffers = rest[2 * len(steps) :]
        for i, dx in enumerate(steps):
            last_block(
                place_ref, dx, history, adjacency, weights, onehots, t2, parts3, buffers[i], outs[2 * i : 2 * i + 2]
            )

    return kernel


def source_of(x, core, slot):
    dx, dc = SLOTS[slot]
    return ((x - dx) & 3) * 2 + (core ^ dc)


def table_kernel(place_ref, schmid_hbm, hardening_hbm, mixing, renewing, schmid_map, hardening, sems):
    x = place_ref[1]
    core = place_ref[2]
    for copy in fetch([(schmid_hbm, schmid_map), (hardening_hbm, hardening)], sems):
        copy.wait()

    def variable(index):
        total = jnp.zeros(index.shape, jnp.int32)
        for slot in range(8):
            inside = (index >= slot * 48) & (index < slot * 48 + 48)
            total = jnp.where(inside, source_of(x, core, slot) * NV + ((index - slot * 48) >> 3), total)
        return total

    def onehot(hit):
        return jnp.where(hit, 1.0, 0.0).astype(BF16)

    def iota(shape, axis):
        return lax.broadcasted_iota(jnp.int32, shape, axis)

    columns = onehot(iota((48, ROWS), 0) == variable(iota((48, ROWS), 1)))
    rows = onehot(iota((ROWS, 48), 1) == variable(iota((ROWS, 48), 0)))
    slips = onehot(iota((96, 12), 1) == (iota((96, 12), 0) >> 3))
    spread = onehot(iota((12, 96), 0) == (iota((12, 96), 1) >> 3))
    wide = onehot((iota((96, ROWS), 0) & 7) == (iota((96, ROWS), 1) & 7)).astype(F32)
    tall = onehot((iota((ROWS, 96), 0) & 7) == (iota((ROWS, 96), 1) & 7)).astype(F32)
    second = (((1,), (1,)), ((), ()))
    for part, piece in enumerate(split(schmid_map[...])):
        picked = jnp.dot(slips, piece, preferred_element_type=F32).astype(BF16)
        picked = jnp.dot(picked, columns, preferred_element_type=F32) * wide
        mixing[part * 96 : (part + 1) * 96, :] = picked.astype(BF16)
    for part, piece in enumerate(split(hardening[...])):
        picked = lax.dot_general(rows, piece, second, preferred_element_type=F32).astype(BF16)
        picked = (jnp.dot(picked, spread, preferred_element_type=F32) * tall).astype(BF16)
        if part == 0:
            renewing[:, 0:96] = picked
            renewing[:, 96:192] = picked
        else:
            renewing[:, 192:288] = picked


def point_kernel(place_ref, mixing, renewing, *rest):
    own = [source_of(place_ref[1], place_ref[2], slot) < 4 for slot in range(8)]
    points = rest[:8]
    outs = rest[8:16]
    highs, lows, rate_parts = rest[16:]
    for slot in range(8):
        for i in range(NV):
            row = (slot * NV + i) * 8
            for g in range(4):
                high, low = split(points[slot][i, g * 8 : (g + 1) * 8, :])
                highs[row : row + 8, cols(g)] = high
                lows[row : row + 8, cols(g)] = low
    both = jnp.dot(mixing[...], highs[...], preferred_element_type=F32)
    rest_ = jnp.dot(mixing[0:96, :], lows[...], preferred_element_type=F32)
    rates = jnp.tanh(both[0:96] + (both[96:] + rest_))
    high, low = split(rates)
    rate_parts[0:96, :] = high
    rate_parts[96:192, :] = low
    rate_parts[192:288, :] = high
    change = jnp.dot(renewing[...], rate_parts[...], preferred_element_type=F32)
    for g in range(4):
        rows = [points[slot][0, g * 8 : (g + 1) * 8, :] + change[slot * 48 : slot * 48 + 8, cols(g)] for slot in range(8)]
        square = jnp.zeros((8, LANE), F32)
        for slot in range(8):
            square = square + jnp.where(own[slot], rows[slot] * rows[slot], 0.0)
        factor = 1.0 / jnp.maximum(jnp.sqrt(square), 1.0)
        for slot in range(8):
            outs[slot][0, g * 8 : (g + 1) * 8, :] = jnp.where(own[slot], rows[slot] * factor, rows[slot])
            for i in range(1, NV):
                row = (slot * NV + i) * 8
                outs[slot][i, g * 8 : (g + 1) * 8, :] = (
                    points[slot][i, g * 8 : (g + 1) * 8, :] + change[row : row + 8, cols(g)]
                )


def merge_kernel(slots):
    def kernel(place_ref, *rest):
        pieces = rest[: len(slots)]
        out, sems = rest[-2:]
        x = place_ref[1]
        core = place_ref[2]
        pairs = []
        for piece, slot in zip(pieces, slots):
            dx, dc = SLOTS[slot]
            col = pl.multiple_of(((x + dx) & 3) * LANE, LANE)
            row = pl.multiple_of((core ^ dc) * 32, 32)
            pairs.append((piece, out.at[:, pl.ds(row, 32), pl.ds(col, LANE)]))
        for copy in fetch(pairs, sems):
            copy.wait()

    return kernel


def vmem():
    return pl.BlockSpec(memory_space=pltpu.VMEM)


def anywhere():
    return pl.BlockSpec(memory_space=pltpu.MemorySpace.HBM)


def position():
    zone = lax.axis_index("zone")
    var = lax.axis_index("var")
    return zone * NZ - 192, var >> 1, var & 1, zone & 1


def call(kernel, args, outs, scratch=(), far_args=(), copies=0, hbm_out=False, aliases=None):
    space = anywhere if hbm_out else vmem
    far_args = [pltpu.with_memory_space_constraint(a, pltpu.MemorySpace.HBM) for a in far_args]


    def placed(*refs):
        kernel(position(), *refs)

    return pl.pallas_call(
        placed,
        out_shape=tuple(jax.ShapeDtypeStruct(shape, dtype) for shape, dtype in outs),
        in_specs=[vmem() for _ in args] + [anywhere() for _ in far_args],
        out_specs=tuple(space() for _ in outs),
        scratch_shapes=[pltpu.VMEM(shape, dtype) for shape, dtype in scratch]
        + ([pltpu.SemaphoreType.DMA((copies,))] if copies else []),
        input_output_aliases=aliases or {},
        compiler_params=pltpu.CompilerParams(vmem_limit_bytes=32 << 20),
    )(*args, *far_args)


def per_device(history, adjacency, volume_op, face_lift, schmid_map, hardening):
    count = lax.axis_size("zone")
    groups = lax.axis_size("var")
    flat = history.reshape(ROWS, NZ)
    near = ((ROWS // 2, LANE), F32)
    far = ((ROWS + 8, LANE), F32)
    near_one, near_two, far_one, far_two, local, faces, volume, lifts = call(
        pack_kernel,
        (),
        [
            near, near, far, far, ((ROWS, NZ), F32), ((NFACE, NZ), jnp.int32), ((NP, NP), F32), ((NFACE * NP, NP), F32),
        ],
        far_args=(flat, adjacency, volume_op, face_lift.reshape(NFACE * NP, NP)),
        copies=7,
    )

    def swap_pairs(shift):
        pairs = []
        for z in range(count):
            other = ((z + shift) ^ 1) - shift
            for v in range(groups):
                target = other * groups + v if 0 <= other < count else z * groups + (v ^ 1)
                pairs.append((z * groups + v, target))
        return pairs

    one, two = swap_pairs(1), swap_pairs(0)
    axes = ("zone", "var")
    near_one = lax.ppermute(near_one, axes, one)
    near_two = lax.ppermute(near_two, axes, two)
    far_one = lax.ppermute(far_one, axes, one)
    far_two = lax.ppermute(far_two, axes, two)
    buffer = ((2, KDIM, NV * LANE), BF16)
    wide = lambda n: ((ROWS, n * LANE), F32)
    pair = lambda n: ((2 * ROWS, n * LANE), BF16)
    *inner, weights = call(
        inner_kernel,
        (local, faces, volume, lifts),
        [
            wide(5), pair(3), ((7, 256, MATMUL_FACES * LANE), BF16),
            wide(2), pair(2), wide(1), pair(1), ((2 * NP, KDIM), BF16),
        ],
        [buffer, buffer],
    )
    onehots = inner[2]
    middle = call(
        middle_kernel,
        (local, faces, near_one, near_two, *inner, weights),
        [wide(2), pair(2), wide(2), pair(2), wide(3), pair(3)],
        [pair(2), pair(2), wide(4), pair(4), buffer, buffer],
    )
    piece = ((NV, 32, LANE), F32)
    *ahead, t2, parts3 = call(
        edge_kernel,
        (local, faces, far_one, far_two, onehots, weights, *middle),
        [piece, piece, wide(5), pair(5)],
        [
            far, far, pair(2), pair(2), pair(2), pair(2), ((4, 256, MATMUL_FACES * LANE), BF16),
            wide(2), buffer, buffer,
        ],
    )
    ready = {(2, 0): ahead[0], (2, 1): ahead[1]}
    for steps in ((1, 3), (0,)):
        pieces = call(
            last_kernel(steps),
            (local, faces, weights, onehots, t2, parts3),
            [piece, piece] * len(steps),
            [buffer] * len(steps),
        )
        for i, dx in enumerate(steps):
            ready[dx, 0], ready[dx, 1] = pieces[2 * i : 2 * i + 2]
    advected = [ready[slot] for slot in SLOTS]

    def exchange(piece, dx, dc):
        if dx == 0 and dc == 0:
            return piece
        pairs = [(v, ((v // 2 + dx) % 4) * 2 + ((v % 2) ^ dc)) for v in range(8)]
        return lax.ppermute(piece, "var", pairs)

    points = [exchange(piece, dx, dc) for piece, (dx, dc) in zip(advected, SLOTS)]
    mixing, renewing = call(
        table_kernel,
        (),
        [((192, ROWS), BF16), ((ROWS, 288), BF16)],
        [((12, 48), F32), ((12, 48), F32)],
        far_args=(schmid_map.T, hardening),
        copies=2,
    )
    renewed = call(
        point_kernel,
        (mixing, renewing, *points),
        [piece] * 8,
        [((ROWS, 512), BF16), ((ROWS, 512), BF16), ((288, 512), BF16)],
    )
    returned = [exchange(piece, (4 - dx) % 4, dc) for piece, (dx, dc) in zip(renewed, SLOTS)]
    out = call(
        merge_kernel(EARLY), [returned[i] for i in EARLY], [((NV, NP, NZ), F32)],
        copies=len(EARLY), hbm_out=True,
    )[0]
    return call(
        merge_kernel(LATE), [returned[i] for i in LATE], [((NV, NP, NZ), F32)],
        far_args=(out,), copies=len(LATE), hbm_out=True, aliases={len(LATE): 0},
    )[0]


def solution(mesh):
    in_specs = (P("var", None, "zone"), P(None, "zone"), P(), P(), P(), P())
    out_specs = P("var", None, "zone")

    return jax.shard_map(per_device, mesh=mesh, in_specs=in_specs, out_specs=out_specs, check_vma=False)
```

```python
import jax
import jax.numpy as jnp
from jax import lax
from jax.experimental import pallas as pl
from jax.experimental.pallas import tpu as pltpu
from jax.sharding import PartitionSpec as P


F32 = jnp.float32
BF16 = jnp.bfloat16
NV = 6
NP = 64
NZ = 512
ROWS = NV * NP
LANE = 128
HALF = 64
NFACE = 6
MATMUL_FACES = 4
KDIM = (NFACE + 1) * NP
SLOTS = [(0, 0), (2, 0), (2, 1), (1, 0), (3, 0), (1, 1), (3, 1), (0, 1)]
EARLY = (0, 3, 4)
LATE = (1, 2, 5, 6, 7)


def first_half(rows):
    return lax.broadcasted_iota(jnp.int32, (rows, LANE), 1) < HALF


def swap(x):
    return pltpu.roll(x, HALF, 1)


def straddle(left, right):
    return jnp.where(first_half(left.shape[0]), swap(left), swap(right))


def split(x):
    high = x.astype(BF16)
    low = (x - high.astype(F32)).astype(BF16)
    return high, low


def cols(b, n=1):
    return slice(b * LANE, (b + n) * LANE)


def put_parts(parts, where, x):
    high, low = split(x)
    parts[0:ROWS, where] = high
    parts[ROWS:, where] = low


def fetch(pairs, sems):
    copies = [pltpu.make_async_copy(source, target, sems.at[i]) for i, (source, target) in enumerate(pairs)]
    for copy in copies:
        copy.start()
    return copies


def by_parity(place_ref, put, one, two):
    @pl.when(place_ref[3] == 1)
    def _():
        put(one, two)

    @pl.when(place_ref[3] == 0)
    def _():
        put(two, one)


def near_kernel(place_ref, history_hbm, adjacency_hbm, near_one, near_two, bottom, top, adjacency, sems):
    half = ROWS // 2
    first = first_half(half)
    pairs = [(history_hbm.at[:, cols(0)], bottom), (history_hbm.at[:, cols(3)], top), (adjacency_hbm, adjacency)]
    for copy in fetch(pairs, sems):
        copy.wait()

    def put(up, down):
        up[0:half, :] = jnp.where(first, swap(top[0:half, :]), top[half:, :])
        down[0:half, :] = jnp.where(first, bottom[0:half, :], swap(bottom[half:, :]))
        for target, c in ((up, 3), (down, 0)):
            target[half:, :] = jnp.zeros((8, LANE), F32)
            target[half : half + NFACE, :] = adjacency[:, cols(c)].astype(F32)

    by_parity(place_ref, put, near_one, near_two)


def far_kernel(
    place_ref, history_hbm, adjacency_hbm, volume_hbm, face_hbm,
    far_one, far_two, history, adjacency, volume_op, face_lift, sems,
):
    pairs = [(history_hbm.at[r : r + 96, :], history.at[r : r + 96, :]) for r in range(0, ROWS, 96)]
    pairs += [(adjacency_hbm, adjacency), (volume_hbm, volume_op), (face_hbm, face_lift)]
    for copy in fetch(pairs, sems):
        copy.wait()

    def put(up, down):
        up[...] = straddle(history[:, cols(2)], history[:, cols(3)])
        down[...] = straddle(history[:, cols(0)], history[:, cols(1)])

    by_parity(place_ref, put, far_one, far_two)


def place(adjacency, start):
    return jnp.where(adjacency < 0, 1000, adjacency - start)


def write_onehots(onehots, slot, rel):
    position = lax.broadcasted_iota(jnp.int32, (2 * LANE, LANE), 0)
    for face in range(MATMUL_FACES):
        hit = position == rel[face : face + 1, :]
        onehots[slot, :, cols(face)] = jnp.where(hit, 1.0, 0.0).astype(BF16)


def apply_block(close, beyond, parts, col, onehots, slot, rel, own, gathered, weights):
    for pair in range(MATMUL_FACES // 2):
        picked = jnp.dot(
            parts[:, pl.ds(col, 2 * LANE)], onehots[slot, :, cols(2 * pair, 2)], preferred_element_type=F32
        ).astype(BF16)
        for part in range(2):
            for v in range(NV):
                row = part * ROWS + v * NP
                for k in range(2):
                    face = 2 * pair + k
                    gathered[part, face * NP : (face + 1) * NP, cols(v)] = picked[row : row + NP, cols(k)]
    for face in range(MATMUL_FACES, NFACE):
        index = jnp.broadcast_to(rel[face : face + 1, :], (ROWS, LANE))
        lane = index & (LANE - 1)
        near = jnp.take_along_axis(close, lane, axis=1)
        far = jnp.take_along_axis(beyond, lane, axis=1)
        value = jnp.where(index >= 2 * LANE, 0.0, jnp.where(index >= LANE, far, near))
        for part, piece in enumerate(split(value)):
            for v in range(NV):
                gathered[part, face * NP : (face + 1) * NP, cols(v)] = piece[v * NP : (v + 1) * NP]
    for part, piece in enumerate(split(own)):
        for v in range(NV):
            gathered[part, NFACE * NP :, cols(v)] = piece[v * NP : (v + 1) * NP]
    both = jnp.dot(weights[...], gathered[0], preferred_element_type=F32)
    rest = jnp.dot(weights[0:NP, :], gathered[1], preferred_element_type=F32)
    value = both[0:NP] + (both[NP:] + rest)
    return [value[:, cols(v)] for v in range(NV)]


def finish(values, base, scale, target, parts, where):
    for v in range(NV):
        rows = slice(v * NP, (v + 1) * NP)
        result = base[rows] + values[v] * scale
        target[rows, where] = result
        high, low = split(result)
        parts[rows, where] = high
        parts[ROWS + v * NP : ROWS + (v + 1) * NP, where] = low


def mix(left, right):
    return jnp.where(first_half(NFACE), pltpu.roll(left, HALF, 1), pltpu.roll(right, HALF, 1))


def inner_kernel(
    place_ref, history, adjacency, volume_op, face_lift,
    u0, parts, onehots, t1, parts2, t2, parts3, weights,
    gat_a, gat_b,
):
    origin = place_ref[0]
    zero = jnp.zeros((ROWS, LANE), F32)
    blocks = [history[:, cols(b)] for b in range(4)]
    padded = [zero] + blocks + [zero]
    for c in range(5):
        u0[:, cols(c)] = straddle(padded[c], padded[c + 1])
    for c in range(1, 4):
        put_parts(parts, cols(c - 1), u0[:, cols(c)])
    for b in range(4):
        write_onehots(onehots, b, place(adjacency[:, cols(b)], origin + (128 * b + 128)))
    near = [mix(adjacency[:, cols(b)], adjacency[:, cols(b + 1)]) for b in range(3)]
    for b in range(3):
        write_onehots(onehots, 4 + b, place(near[b], origin + (128 * b + 192)))
    for lanes, matrix in ((slice(0, 384), face_lift[...].T), (slice(384, 448), volume_op[...].T)):
        high, low = split(matrix)
        weights[0:NP, lanes] = high
        weights[NP:, lanes] = low
    for b, gathered in ((2, gat_a), (3, gat_b)):
        rel = place(adjacency[:, cols(b - 1)], origin + 128 * b)
        values = apply_block(
            u0[:, cols(b - 1)], u0[:, cols(b)], parts, (b - 2) * LANE, onehots, b - 1, rel, blocks[b - 1], gathered, weights
        )
        finish(values, blocks[b - 1], 1.0 / 3.0, t1, parts2, cols(b - 2))
    rel = place(near[1], origin + 320)
    own = straddle(t1[:, cols(0)], t1[:, cols(1)])
    values = apply_block(t1[:, cols(0)], t1[:, cols(1)], parts2, 0, onehots, 5, rel, own, gat_a, weights)
    finish(values, u0[:, cols(2)], 0.5, t2, parts3, cols(0))


def middle_kernel(
    place_ref, history, adjacency, near_one, near_two, u0m, partsm, onehots, t1m, parts2m, t2m, parts3m, weights,
    ends, end_parts, rim, rim_parts, t2, parts3, edge, edge_rels,
    left, right, t1, parts2, gat_a, gat_b,
):
    origin = place_ref[0]
    odd = place_ref[3] == 1
    half = ROWS // 2
    first = first_half(half)
    low = jnp.where(odd, near_two[0:half, :], near_one[0:half, :])
    high = jnp.where(odd, near_one[0:half, :], near_two[0:half, :])
    low_adj = jnp.where(odd, near_two[half:, :], near_one[half:, :]).astype(jnp.int32)[0:NFACE]
    high_adj = jnp.where(odd, near_one[half:, :], near_two[half:, :]).astype(jnp.int32)[0:NFACE]
    rels = [
        place(low_adj, origin),
        place(high_adj, origin + 640),
        place(mix(low_adj, adjacency[:, cols(0)]), origin + 64),
        place(mix(adjacency[:, cols(3)], high_adj), origin + 576),
    ]
    for slot, rel in enumerate(rels):
        write_onehots(edge, slot, rel)
        edge_rels[slot, 0:NFACE, :] = rel
    ends[0:half, cols(0)] = jnp.where(first, low, u0m[0:half, cols(0)])
    ends[half:, cols(0)] = jnp.where(first, swap(low), u0m[half:, cols(0)])
    ends[0:half, cols(1)] = jnp.where(first, u0m[0:half, cols(4)], swap(high))
    ends[half:, cols(1)] = jnp.where(first, u0m[half:, cols(4)], high)
    put_parts(end_parts, cols(0), ends[:, cols(0)])
    put_parts(end_parts, cols(1), ends[:, cols(1)])
    left[:, cols(0)] = end_parts[:, cols(0)]
    left[:, cols(1)] = partsm[:, cols(0)]
    right[:, cols(0)] = partsm[:, cols(2)]
    right[:, cols(1)] = end_parts[:, cols(1)]
    t1[:, cols(1, 2)] = t1m[...]
    parts2[:, cols(1, 2)] = parts2m[...]
    t2[:, cols(1)] = t2m[...]
    parts3[:, cols(1)] = parts3m[...]
    rel = place(adjacency[:, cols(0)], origin + 128)
    base = history[:, cols(0)]
    values = apply_block(ends[:, cols(0)], u0m[:, cols(1)], left, 0, onehots, 0, rel, base, gat_a, weights)
    finish(values, base, 1.0 / 3.0, t1, parts2, cols(0))
    rel = place(adjacency[:, cols(3)], origin + 512)
    base = history[:, cols(3)]
    values = apply_block(u0m[:, cols(3)], ends[:, cols(1)], right, 0, onehots, 3, rel, base, gat_b, weights)
    finish(values, base, 1.0 / 3.0, t1, parts2, cols(3))
    for b, gathered in ((0, gat_a), (2, gat_b)):
        rel = place(mix(adjacency[:, cols(b)], adjacency[:, cols(b + 1)]), origin + (128 * b + 192))
        close, beyond = t1[:, cols(b)], t1[:, cols(b + 1)]
        values = apply_block(
            close, beyond, parts2, b * LANE, onehots, 4 + b, rel, straddle(close, beyond), gathered, weights
        )
        finish(values, u0m[:, cols(b + 1)], 0.5, t2, parts3, cols(b))
    for i, c in ((0, 0), (1, 3)):
        rim[:, cols(i)] = t1[:, cols(c)]
        rim_parts[:, cols(i)] = parts2[:, cols(c)]


def edge_kernel(
    place_ref, history, adjacency, far_one, far_two, onehots, weights, ends, end_parts, rim, rim_parts, t2m, parts3m,
    edge, edge_rels, *rest,
):
    outs = rest[:2]
    t2, parts3, low, high, left, right, left2, right2, tips, gat_a, gat_b = rest[2:]
    odd = place_ref[3] == 1
    low[...] = jnp.where(odd, far_two[...], far_one[...])
    high[...] = jnp.where(odd, far_one[...], far_two[...])
    rels = [edge_rels[slot, 0:NFACE, :] for slot in range(4)]
    put_parts(left, cols(0), low[0:ROWS, :])
    left[:, cols(1)] = end_parts[:, cols(0)]
    right[:, cols(0)] = end_parts[:, cols(1)]
    put_parts(right, cols(1), high[0:ROWS, :])
    left2[:, cols(1)] = rim_parts[:, cols(0)]
    right2[:, cols(0)] = rim_parts[:, cols(1)]
    t2[:, cols(1, 3)] = t2m[...]
    parts3[:, cols(1, 3)] = parts3m[...]
    close, beyond = low[0:ROWS, :], ends[:, cols(0)]
    base = straddle(close, beyond)
    values = apply_block(close, beyond, left, 0, edge, 0, rels[0], base, gat_a, weights)
    finish(values, base, 1.0 / 3.0, tips, left2, cols(0))
    close, beyond = ends[:, cols(1)], high[0:ROWS, :]
    base = straddle(close, beyond)
    values = apply_block(close, beyond, right, 0, edge, 1, rels[1], base, gat_b, weights)
    finish(values, base, 1.0 / 3.0, tips, right2, cols(1))
    close, beyond = tips[:, cols(0)], rim[:, cols(0)]
    values = apply_block(close, beyond, left2, 0, edge, 2, rels[2], straddle(close, beyond), gat_a, weights)
    finish(values, ends[:, cols(0)], 0.5, t2, parts3, cols(0))
    close, beyond = rim[:, cols(1)], tips[:, cols(1)]
    values = apply_block(close, beyond, right2, 0, edge, 3, rels[3], straddle(close, beyond), gat_b, weights)
    finish(values, ends[:, cols(1)], 0.5, t2, parts3, cols(4))
    last_block(place_ref, 2, history, adjacency, weights, onehots, t2, parts3, gat_a, outs)


def last_block(place_ref, dx, history, adjacency, weights, onehots, t2, parts3, gathered, outs):
    b = place_ref[1] ^ dx
    upper = place_ref[2] == 1
    col = pl.multiple_of(b * LANE, LANE)
    rel = place(adjacency[:, pl.ds(col, LANE)], place_ref[0] + 128 + col)
    close, beyond = t2[:, pl.ds(col, LANE)], t2[:, pl.ds(col + LANE, LANE)]
    values = apply_block(close, beyond, parts3, col, onehots, b, rel, straddle(close, beyond), gathered, weights)
    for v in range(NV):
        result = history[v * NP : (v + 1) * NP, pl.ds(col, LANE)] + values[v]
        below, above = result[0:32], result[32:64]
        outs[0][v] = jnp.where(upper, above, below)
        outs[1][v] = jnp.where(upper, below, above)


def last_kernel(steps):
    def kernel(place_ref, history, adjacency, weights, onehots, t2, parts3, *rest):
        outs = rest[: 2 * len(steps)]
        buffers = rest[2 * len(steps) :]
        for i, dx in enumerate(steps):
            last_block(
                place_ref, dx, history, adjacency, weights, onehots, t2, parts3, buffers[i], outs[2 * i : 2 * i + 2]
            )

    return kernel


def source_of(x, core, slot):
    dx, dc = SLOTS[slot]
    return (x ^ dx) * 2 + (core ^ dc)


def table_kernel(place_ref, schmid_hbm, hardening_hbm, mixing, renewing, schmid_map, hardening, sems):
    x = place_ref[1]
    core = place_ref[2]
    for copy in fetch([(schmid_hbm, schmid_map), (hardening_hbm, hardening)], sems):
        copy.wait()

    def variable(index):
        total = jnp.zeros(index.shape, jnp.int32)
        for slot in range(8):
            inside = (index >= slot * 48) & (index < slot * 48 + 48)
            total = jnp.where(inside, source_of(x, core, slot) * NV + ((index - slot * 48) >> 3), total)
        return total

    def onehot(hit):
        return jnp.where(hit, 1.0, 0.0).astype(BF16)

    def iota(shape, axis):
        return lax.broadcasted_iota(jnp.int32, shape, axis)

    columns = onehot(iota((48, ROWS), 0) == variable(iota((48, ROWS), 1)))
    rows = onehot(iota((ROWS, 48), 1) == variable(iota((ROWS, 48), 0)))
    slips = onehot(iota((96, 12), 1) == (iota((96, 12), 0) >> 3))
    spread = onehot(iota((12, 96), 0) == (iota((12, 96), 1) >> 3))
    wide = onehot((iota((96, ROWS), 0) & 7) == (iota((96, ROWS), 1) & 7)).astype(F32)
    tall = onehot((iota((ROWS, 96), 0) & 7) == (iota((ROWS, 96), 1) & 7)).astype(F32)
    second = (((1,), (1,)), ((), ()))
    for part, piece in enumerate(split(schmid_map[...])):
        picked = jnp.dot(slips, piece, preferred_element_type=F32).astype(BF16)
        picked = jnp.dot(picked, columns, preferred_element_type=F32) * wide
        mixing[part * 96 : (part + 1) * 96, :] = picked.astype(BF16)
    for part, piece in enumerate(split(hardening[...])):
        picked = lax.dot_general(rows, piece, second, preferred_element_type=F32).astype(BF16)
        picked = (jnp.dot(picked, spread, preferred_element_type=F32) * tall).astype(BF16)
        if part == 0:
            renewing[:, 0:96] = picked
            renewing[:, 96:192] = picked
        else:
            renewing[:, 192:288] = picked


def point_kernel(place_ref, mixing, renewing, *rest):
    own = [source_of(place_ref[1], place_ref[2], slot) < 4 for slot in range(8)]
    points = rest[:8]
    outs = rest[8:16]
    highs, lows, rate_parts = rest[16:]
    for slot in range(8):
        for i in range(NV):
            row = (slot * NV + i) * 8
            for g in range(4):
                high, low = split(points[slot][i, g * 8 : (g + 1) * 8, :])
                highs[row : row + 8, cols(g)] = high
                lows[row : row + 8, cols(g)] = low
    both = jnp.dot(mixing[...], highs[...], preferred_element_type=F32)
    rest_ = jnp.dot(mixing[0:96, :], lows[...], preferred_element_type=F32)
    rates = jnp.tanh(both[0:96] + (both[96:] + rest_))
    high, low = split(rates)
    rate_parts[0:96, :] = high
    rate_parts[96:192, :] = low
    rate_parts[192:288, :] = high
    change = jnp.dot(renewing[...], rate_parts[...], preferred_element_type=F32)
    for g in range(4):
        rows = [points[slot][0, g * 8 : (g + 1) * 8, :] + change[slot * 48 : slot * 48 + 8, cols(g)] for slot in range(8)]
        square = jnp.zeros((8, LANE), F32)
        for slot in range(8):
            square = square + jnp.where(own[slot], rows[slot] * rows[slot], 0.0)
        factor = 1.0 / jnp.maximum(jnp.sqrt(square), 1.0)
        for slot in range(8):
            outs[slot][0, g * 8 : (g + 1) * 8, :] = jnp.where(own[slot], rows[slot] * factor, rows[slot])
            for i in range(1, NV):
                row = (slot * NV + i) * 8
                outs[slot][i, g * 8 : (g + 1) * 8, :] = (
                    points[slot][i, g * 8 : (g + 1) * 8, :] + change[row : row + 8, cols(g)]
                )


def merge_kernel(slots):
    def kernel(place_ref, *rest):
        pieces = rest[: len(slots)]
        out, sems = rest[-2:]
        x = place_ref[1]
        core = place_ref[2]
        pairs = []
        for piece, slot in zip(pieces, slots):
            dx, dc = SLOTS[slot]
            col = pl.multiple_of((x ^ dx) * LANE, LANE)
            row = pl.multiple_of((core ^ dc) * 32, 32)
            pairs.append((piece, out.at[:, pl.ds(row, 32), pl.ds(col, LANE)]))
        for copy in fetch(pairs, sems):
            copy.wait()

    return kernel


def vmem():
    return pl.BlockSpec(memory_space=pltpu.VMEM)


def anywhere():
    return pl.BlockSpec(memory_space=pltpu.MemorySpace.HBM)


def position():
    zone = lax.axis_index("zone")
    var = lax.axis_index("var")
    return zone * NZ - 192, var >> 1, var & 1, zone & 1


def call(kernel, args, outs, scratch=(), far_args=(), copies=0, hbm_out=False, aliases=None):
    space = anywhere if hbm_out else vmem
    far_args = [pltpu.with_memory_space_constraint(a, pltpu.MemorySpace.HBM) for a in far_args]


    def placed(*refs):
        kernel(position(), *refs)

    return pl.pallas_call(
        placed,
        out_shape=tuple(jax.ShapeDtypeStruct(shape, dtype) for shape, dtype in outs),
        in_specs=[vmem() for _ in args] + [anywhere() for _ in far_args],
        out_specs=tuple(space() for _ in outs),
        scratch_shapes=[pltpu.VMEM(shape, dtype) for shape, dtype in scratch]
        + ([pltpu.SemaphoreType.DMA((copies,))] if copies else []),
        input_output_aliases=aliases or {},
        compiler_params=pltpu.CompilerParams(vmem_limit_bytes=32 << 20),
    )(*args, *far_args)


def per_device(history, adjacency, volume_op, face_lift, schmid_map, hardening):
    count = lax.axis_size("zone")
    groups = lax.axis_size("var")
    flat = history.reshape(ROWS, NZ)
    near = ((ROWS // 2 + 8, LANE), F32)
    far = ((ROWS, LANE), F32)
    near_one, near_two = call(
        near_kernel, (), [near, near], [far, far, ((NFACE, NZ), jnp.int32)], far_args=(flat, adjacency), copies=3
    )
    far_one, far_two, local, faces, volume, lifts = call(
        far_kernel,
        (),
        [far, far, ((ROWS, NZ), F32), ((NFACE, NZ), jnp.int32), ((NP, NP), F32), ((NFACE * NP, NP), F32)],
        far_args=(flat, adjacency, volume_op, face_lift.reshape(NFACE * NP, NP)),
        copies=7,
    )

    def swap_pairs(shift):
        pairs = []
        for z in range(count):
            other = ((z + shift) ^ 1) - shift
            for v in range(groups):
                target = other * groups + v if 0 <= other < count else z * groups + (v ^ 1)
                pairs.append((z * groups + v, target))
        return pairs

    one, two = swap_pairs(1), swap_pairs(0)
    axes = ("zone", "var")
    near_one = lax.ppermute(near_one, axes, one)
    near_two = lax.ppermute(near_two, axes, two)
    far_one = lax.ppermute(far_one, axes, one)
    far_two = lax.ppermute(far_two, axes, two)
    buffer = ((2, KDIM, NV * LANE), BF16)
    wide = lambda n: ((ROWS, n * LANE), F32)
    pair = lambda n: ((2 * ROWS, n * LANE), BF16)
    *inner, weights = call(
        inner_kernel,
        (local, faces, volume, lifts),
        [
            wide(5), pair(3), ((7, 256, MATMUL_FACES * LANE), BF16),
            wide(2), pair(2), wide(1), pair(1), ((2 * NP, KDIM), BF16),
        ],
        [buffer, buffer],
    )
    onehots = inner[2]
    middle = call(
        middle_kernel,
        (local, faces, near_one, near_two, *inner, weights),
        [
            wide(2), pair(2), wide(2), pair(2), wide(3), pair(3),
            ((4, 256, MATMUL_FACES * LANE), BF16), ((4, 8, LANE), jnp.int32),
        ],
        [pair(2), pair(2), wide(4), pair(4), buffer, buffer],
    )
    piece = ((NV, 32, LANE), F32)
    *ahead, t2, parts3 = call(
        edge_kernel,
        (local, faces, far_one, far_two, onehots, weights, *middle),
        [piece, piece, wide(5), pair(5)],
        [
            far, far, pair(2), pair(2), pair(2), pair(2), wide(2), buffer, buffer,
        ],
    )
    ready = {(2, 0): ahead[0], (2, 1): ahead[1]}
    for steps in ((1, 3), (0,)):
        pieces = call(
            last_kernel(steps),
            (local, faces, weights, onehots, t2, parts3),
            [piece, piece] * len(steps),
            [buffer] * len(steps),
        )
        for i, dx in enumerate(steps):
            ready[dx, 0], ready[dx, 1] = pieces[2 * i : 2 * i + 2]
    advected = [ready[slot] for slot in SLOTS]

    def exchange(piece, dx, dc):
        if dx == 0 and dc == 0:
            return piece
        pairs = [(v, v ^ (2 * dx + dc)) for v in range(groups)]
        return lax.ppermute(piece, "var", pairs)

    points = [exchange(piece, dx, dc) for piece, (dx, dc) in zip(advected, SLOTS)]
    mixing, renewing = call(
        table_kernel,
        (),
        [((192, ROWS), BF16), ((ROWS, 288), BF16)],
        [((12, 48), F32), ((12, 48), F32)],
        far_args=(schmid_map.T, hardening),
        copies=2,
    )
    renewed = call(
        point_kernel,
        (mixing, renewing, *points),
        [piece] * 8,
        [((ROWS, 512), BF16), ((ROWS, 512), BF16), ((288, 512), BF16)],
    )
    returned = [exchange(piece, dx, dc) for piece, (dx, dc) in zip(renewed, SLOTS)]
    out = call(
        merge_kernel(EARLY), [returned[i] for i in EARLY], [((NV, NP, NZ), F32)],
        copies=len(EARLY), hbm_out=True,
    )[0]
    return call(
        merge_kernel(LATE), [returned[i] for i in LATE], [((NV, NP, NZ), F32)],
        far_args=(out,), copies=len(LATE), hbm_out=True, aliases={len(LATE): 0},
    )[0]


def solution(mesh):
    in_specs = (P("var", None, "zone"), P(None, "zone"), P(), P(), P(), P())
    out_specs = P("var", None, "zone")

    return jax.shard_map(per_device, mesh=mesh, in_specs=in_specs, out_specs=out_specs, check_vma=False)
```

```python
import jax
import jax.numpy as jnp
from jax import lax
from jax.experimental import pallas as pl
from jax.experimental.pallas import tpu as pltpu
from jax.sharding import PartitionSpec as P


F32 = jnp.float32
BF16 = jnp.bfloat16
NV = 6
NP = 64
NZ = 512
ROWS = NV * NP
LANE = 128
HALF = 64
NFACE = 6
MATMUL_FACES = 4
KDIM = (NFACE + 1) * NP
SLOTS = [(0, 0), (2, 0), (2, 1), (1, 0), (3, 0), (1, 1), (3, 1), (0, 1)]
EARLY = (0, 3, 4)
LATE = (1, 2, 5, 6, 7)


def first_half(rows):
    return lax.broadcasted_iota(jnp.int32, (rows, LANE), 1) < HALF


def swap(x):
    return pltpu.roll(x, HALF, 1)


def straddle(left, right):
    return jnp.where(first_half(left.shape[0]), swap(left), swap(right))


def split(x):
    high = x.astype(BF16)
    low = (x - high.astype(F32)).astype(BF16)
    return high, low


def cols(b, n=1):
    return slice(b * LANE, (b + n) * LANE)


def put_parts(parts, where, x):
    high, low = split(x)
    parts[0:ROWS, where] = high
    parts[ROWS:, where] = low


def fetch(pairs, sems):
    copies = [pltpu.make_async_copy(source, target, sems.at[i]) for i, (source, target) in enumerate(pairs)]
    for copy in copies:
        copy.start()
    return copies


def pack_kernel(
    place_ref, history_hbm, adjacency_hbm, volume_hbm, face_hbm,
    near_one, near_two, far_one, far_two, history, adjacency, volume_op, face_lift, sems,
):
    half = ROWS // 2
    first = first_half(half)
    copies = fetch(
        [(history_hbm.at[r : r + 96, :], history.at[r : r + 96, :]) for r in range(0, ROWS, 96)]
        + [(adjacency_hbm, adjacency), (volume_hbm, volume_op), (face_hbm, face_lift)],
        sems,
    )
    for copy in copies:
        copy.wait()

    def put(near_up, near_down, far_up, far_down):
        near_up[...] = jnp.where(first, swap(history[0:half, cols(3)]), history[half:, cols(3)])
        near_down[...] = jnp.where(first, history[0:half, cols(0)], swap(history[half:, cols(0)]))
        far_up[0:ROWS, :] = straddle(history[:, cols(2)], history[:, cols(3)])
        far_down[0:ROWS, :] = straddle(history[:, cols(0)], history[:, cols(1)])
        for target, c in ((far_up, 3), (far_down, 0)):
            target[ROWS:, :] = jnp.zeros((8, LANE), F32)
            target[ROWS : ROWS + NFACE, :] = adjacency[:, cols(c)].astype(F32)

    @pl.when(place_ref[3] == 1)
    def _():
        put(near_one, near_two, far_one, far_two)

    @pl.when(place_ref[3] == 0)
    def _():
        put(near_two, near_one, far_two, far_one)


def place(adjacency, start):
    return jnp.where(adjacency < 0, 1000, adjacency - start)


def write_onehots(onehots, slot, rel):
    position = lax.broadcasted_iota(jnp.int32, (2 * LANE, LANE), 0)
    for face in range(MATMUL_FACES):
        hit = position == rel[face : face + 1, :]
        onehots[slot, :, cols(face)] = jnp.where(hit, 1.0, 0.0).astype(BF16)


def apply_block(close, beyond, parts, col, onehots, slot, rel, own, gathered, weights):
    for pair in range(MATMUL_FACES // 2):
        picked = jnp.dot(
            parts[:, pl.ds(col, 2 * LANE)], onehots[slot, :, cols(2 * pair, 2)], preferred_element_type=F32
        ).astype(BF16)
        for part in range(2):
            for v in range(NV):
                row = part * ROWS + v * NP
                for k in range(2):
                    face = 2 * pair + k
                    gathered[part, face * NP : (face + 1) * NP, cols(v)] = picked[row : row + NP, cols(k)]
    for face in range(MATMUL_FACES, NFACE):
        index = jnp.broadcast_to(rel[face : face + 1, :], (ROWS, LANE))
        lane = index & (LANE - 1)
        near = jnp.take_along_axis(close, lane, axis=1)
        far = jnp.take_along_axis(beyond, lane, axis=1)
        value = jnp.where(index >= 2 * LANE, 0.0, jnp.where(index >= LANE, far, near))
        for part, piece in enumerate(split(value)):
            for v in range(NV):
                gathered[part, face * NP : (face + 1) * NP, cols(v)] = piece[v * NP : (v + 1) * NP]
    for part, piece in enumerate(split(own)):
        for v in range(NV):
            gathered[part, NFACE * NP :, cols(v)] = piece[v * NP : (v + 1) * NP]
    both = jnp.dot(weights[...], gathered[0], preferred_element_type=F32)
    rest = jnp.dot(weights[0:NP, :], gathered[1], preferred_element_type=F32)
    value = both[0:NP] + (both[NP:] + rest)
    return [value[:, cols(v)] for v in range(NV)]


def finish(values, base, scale, target, parts, where):
    for v in range(NV):
        rows = slice(v * NP, (v + 1) * NP)
        result = base[rows] + values[v] * scale
        target[rows, where] = result
        high, low = split(result)
        parts[rows, where] = high
        parts[ROWS + v * NP : ROWS + (v + 1) * NP, where] = low


def mix(left, right):
    return jnp.where(first_half(NFACE), pltpu.roll(left, HALF, 1), pltpu.roll(right, HALF, 1))


def inner_kernel(
    place_ref, history, adjacency, volume_op, face_lift,
    u0, parts, onehots, t1, parts2, t2, parts3, weights,
    gat_a, gat_b,
):
    origin = place_ref[0]
    zero = jnp.zeros((ROWS, LANE), F32)
    blocks = [history[:, cols(b)] for b in range(4)]
    padded = [zero] + blocks + [zero]
    for c in range(5):
        u0[:, cols(c)] = straddle(padded[c], padded[c + 1])
    for c in range(1, 4):
        put_parts(parts, cols(c - 1), u0[:, cols(c)])
    for b in range(4):
        write_onehots(onehots, b, place(adjacency[:, cols(b)], origin + (128 * b + 128)))
    near = [mix(adjacency[:, cols(b)], adjacency[:, cols(b + 1)]) for b in range(3)]
    for b in range(3):
        write_onehots(onehots, 4 + b, place(near[b], origin + (128 * b + 192)))
    for lanes, matrix in ((slice(0, 384), face_lift[...].T), (slice(384, 448), volume_op[...].T)):
        high, low = split(matrix)
        weights[0:NP, lanes] = high
        weights[NP:, lanes] = low
    for b, gathered in ((2, gat_a), (3, gat_b)):
        rel = place(adjacency[:, cols(b - 1)], origin + 128 * b)
        values = apply_block(
            u0[:, cols(b - 1)], u0[:, cols(b)], parts, (b - 2) * LANE, onehots, b - 1, rel, blocks[b - 1], gathered, weights
        )
        finish(values, blocks[b - 1], 1.0 / 3.0, t1, parts2, cols(b - 2))
    rel = place(near[1], origin + 320)
    own = straddle(t1[:, cols(0)], t1[:, cols(1)])
    values = apply_block(t1[:, cols(0)], t1[:, cols(1)], parts2, 0, onehots, 5, rel, own, gat_a, weights)
    finish(values, u0[:, cols(2)], 0.5, t2, parts3, cols(0))


def middle_kernel(
    place_ref, history, adjacency, near_one, near_two, u0m, partsm, onehots, t1m, parts2m, t2m, parts3m, weights,
    ends, end_parts, rim, rim_parts, t2, parts3,
    left, right, t1, parts2, gat_a, gat_b,
):
    origin = place_ref[0]
    odd = place_ref[3] == 1
    half = ROWS // 2
    first = first_half(half)
    low = jnp.where(odd, near_two[...], near_one[...])
    high = jnp.where(odd, near_one[...], near_two[...])
    ends[0:half, cols(0)] = jnp.where(first, low, u0m[0:half, cols(0)])
    ends[half:, cols(0)] = jnp.where(first, swap(low), u0m[half:, cols(0)])
    ends[0:half, cols(1)] = jnp.where(first, u0m[0:half, cols(4)], swap(high))
    ends[half:, cols(1)] = jnp.where(first, u0m[half:, cols(4)], high)
    put_parts(end_parts, cols(0), ends[:, cols(0)])
    put_parts(end_parts, cols(1), ends[:, cols(1)])
    left[:, cols(0)] = end_parts[:, cols(0)]
    left[:, cols(1)] = partsm[:, cols(0)]
    right[:, cols(0)] = partsm[:, cols(2)]
    right[:, cols(1)] = end_parts[:, cols(1)]
    t1[:, cols(1, 2)] = t1m[...]
    parts2[:, cols(1, 2)] = parts2m[...]
    t2[:, cols(1)] = t2m[...]
    parts3[:, cols(1)] = parts3m[...]
    rel = place(adjacency[:, cols(0)], origin + 128)
    base = history[:, cols(0)]
    values = apply_block(ends[:, cols(0)], u0m[:, cols(1)], left, 0, onehots, 0, rel, base, gat_a, weights)
    finish(values, base, 1.0 / 3.0, t1, parts2, cols(0))
    rel = place(adjacency[:, cols(3)], origin + 512)
    base = history[:, cols(3)]
    values = apply_block(u0m[:, cols(3)], ends[:, cols(1)], right, 0, onehots, 3, rel, base, gat_b, weights)
    finish(values, base, 1.0 / 3.0, t1, parts2, cols(3))
    for b, gathered in ((0, gat_a), (2, gat_b)):
        rel = place(mix(adjacency[:, cols(b)], adjacency[:, cols(b + 1)]), origin + (128 * b + 192))
        close, beyond = t1[:, cols(b)], t1[:, cols(b + 1)]
        values = apply_block(
            close, beyond, parts2, b * LANE, onehots, 4 + b, rel, straddle(close, beyond), gathered, weights
        )
        finish(values, u0m[:, cols(b + 1)], 0.5, t2, parts3, cols(b))
    for i, c in ((0, 0), (1, 3)):
        rim[:, cols(i)] = t1[:, cols(c)]
        rim_parts[:, cols(i)] = parts2[:, cols(c)]


def edge_kernel(
    place_ref, history, adjacency, far_one, far_two, onehots, weights, ends, end_parts, rim, rim_parts, t2m, parts3m,
    *rest,
):
    outs = rest[:2]
    t2, parts3, low, high, left, right, left2, right2, edge, tips, gat_a, gat_b = rest[2:]
    origin = place_ref[0]
    odd = place_ref[3] == 1
    low[...] = jnp.where(odd, far_two[...], far_one[...])
    high[...] = jnp.where(odd, far_one[...], far_two[...])
    low_adj = low[ROWS:, :].astype(jnp.int32)[0:NFACE]
    high_adj = high[ROWS:, :].astype(jnp.int32)[0:NFACE]
    rels = [
        place(low_adj, origin),
        place(high_adj, origin + 640),
        place(mix(low_adj, adjacency[:, cols(0)]), origin + 64),
        place(mix(adjacency[:, cols(3)], high_adj), origin + 576),
    ]
    for slot, rel in enumerate(rels):
        write_onehots(edge, slot, rel)
    put_parts(left, cols(0), low[0:ROWS, :])
    left[:, cols(1)] = end_parts[:, cols(0)]
    right[:, cols(0)] = end_parts[:, cols(1)]
    put_parts(right, cols(1), high[0:ROWS, :])
    left2[:, cols(1)] = rim_parts[:, cols(0)]
    right2[:, cols(0)] = rim_parts[:, cols(1)]
    t2[:, cols(1, 3)] = t2m[...]
    parts3[:, cols(1, 3)] = parts3m[...]
    close, beyond = low[0:ROWS, :], ends[:, cols(0)]
    base = straddle(close, beyond)
    values = apply_block(close, beyond, left, 0, edge, 0, rels[0], base, gat_a, weights)
    finish(values, base, 1.0 / 3.0, tips, left2, cols(0))
    close, beyond = ends[:, cols(1)], high[0:ROWS, :]
    base = straddle(close, beyond)
    values = apply_block(close, beyond, right, 0, edge, 1, rels[1], base, gat_b, weights)
    finish(values, base, 1.0 / 3.0, tips, right2, cols(1))
    close, beyond = tips[:, cols(0)], rim[:, cols(0)]
    values = apply_block(close, beyond, left2, 0, edge, 2, rels[2], straddle(close, beyond), gat_a, weights)
    finish(values, ends[:, cols(0)], 0.5, t2, parts3, cols(0))
    close, beyond = rim[:, cols(1)], tips[:, cols(1)]
    values = apply_block(close, beyond, right2, 0, edge, 3, rels[3], straddle(close, beyond), gat_b, weights)
    finish(values, ends[:, cols(1)], 0.5, t2, parts3, cols(4))
    last_block(place_ref, 2, history, adjacency, weights, onehots, t2, parts3, gat_a, outs)


def last_block(place_ref, dx, history, adjacency, weights, onehots, t2, parts3, gathered, outs):
    b = place_ref[1] ^ dx
    upper = place_ref[2] == 1
    col = pl.multiple_of(b * LANE, LANE)
    rel = place(adjacency[:, pl.ds(col, LANE)], place_ref[0] + 128 + col)
    close, beyond = t2[:, pl.ds(col, LANE)], t2[:, pl.ds(col + LANE, LANE)]
    values = apply_block(close, beyond, parts3, col, onehots, b, rel, straddle(close, beyond), gathered, weights)
    for v in range(NV):
        result = history[v * NP : (v + 1) * NP, pl.ds(col, LANE)] + values[v]
        below, above = result[0:32], result[32:64]
        outs[0][v] = jnp.where(upper, above, below)
        outs[1][v] = jnp.where(upper, below, above)


def last_kernel(steps):
    def kernel(place_ref, history, adjacency, weights, onehots, t2, parts3, *rest):
        outs = rest[: 2 * len(steps)]
        buffers = rest[2 * len(steps) :]
        for i, dx in enumerate(steps):
            last_block(
                place_ref, dx, history, adjacency, weights, onehots, t2, parts3, buffers[i], outs[2 * i : 2 * i + 2]
            )

    return kernel


def source_of(x, core, slot):
    dx, dc = SLOTS[slot]
    return (x ^ dx) * 2 + (core ^ dc)


def table_kernel(place_ref, schmid_hbm, hardening_hbm, mixing, renewing, schmid_map, hardening, sems):
    x = place_ref[1]
    core = place_ref[2]
    for copy in fetch([(schmid_hbm, schmid_map), (hardening_hbm, hardening)], sems):
        copy.wait()

    def variable(index):
        total = jnp.zeros(index.shape, jnp.int32)
        for slot in range(8):
            inside = (index >= slot * 48) & (index < slot * 48 + 48)
            total = jnp.where(inside, source_of(x, core, slot) * NV + ((index - slot * 48) >> 3), total)
        return total

    def onehot(hit):
        return jnp.where(hit, 1.0, 0.0).astype(BF16)

    def iota(shape, axis):
        return lax.broadcasted_iota(jnp.int32, shape, axis)

    columns = onehot(iota((48, ROWS), 0) == variable(iota((48, ROWS), 1)))
    rows = onehot(iota((ROWS, 48), 1) == variable(iota((ROWS, 48), 0)))
    slips = onehot(iota((96, 12), 1) == (iota((96, 12), 0) >> 3))
    spread = onehot(iota((12, 96), 0) == (iota((12, 96), 1) >> 3))
    wide = onehot((iota((96, ROWS), 0) & 7) == (iota((96, ROWS), 1) & 7)).astype(F32)
    tall = onehot((iota((ROWS, 96), 0) & 7) == (iota((ROWS, 96), 1) & 7)).astype(F32)
    second = (((1,), (1,)), ((), ()))
    for part, piece in enumerate(split(schmid_map[...])):
        picked = jnp.dot(slips, piece, preferred_element_type=F32).astype(BF16)
        picked = jnp.dot(picked, columns, preferred_element_type=F32) * wide
        mixing[part * 96 : (part + 1) * 96, :] = picked.astype(BF16)
    for part, piece in enumerate(split(hardening[...])):
        picked = lax.dot_general(rows, piece, second, preferred_element_type=F32).astype(BF16)
        picked = (jnp.dot(picked, spread, preferred_element_type=F32) * tall).astype(BF16)
        if part == 0:
            renewing[:, 0:96] = picked
            renewing[:, 96:192] = picked
        else:
            renewing[:, 192:288] = picked


def point_kernel(place_ref, mixing, renewing, *rest):
    own = [source_of(place_ref[1], place_ref[2], slot) < 4 for slot in range(8)]
    points = rest[:8]
    outs = rest[8:16]
    highs, lows, rate_parts = rest[16:]
    for slot in range(8):
        for i in range(NV):
            row = (slot * NV + i) * 8
            for g in range(4):
                high, low = split(points[slot][i, g * 8 : (g + 1) * 8, :])
                highs[row : row + 8, cols(g)] = high
                lows[row : row + 8, cols(g)] = low
    both = jnp.dot(mixing[...], highs[...], preferred_element_type=F32)
    rest_ = jnp.dot(mixing[0:96, :], lows[...], preferred_element_type=F32)
    rates = jnp.tanh(both[0:96] + (both[96:] + rest_))
    high, low = split(rates)
    rate_parts[0:96, :] = high
    rate_parts[96:192, :] = low
    rate_parts[192:288, :] = high
    change = jnp.dot(renewing[...], rate_parts[...], preferred_element_type=F32)
    for g in range(4):
        rows = [points[slot][0, g * 8 : (g + 1) * 8, :] + change[slot * 48 : slot * 48 + 8, cols(g)] for slot in range(8)]
        square = jnp.zeros((8, LANE), F32)
        for slot in range(8):
            square = square + jnp.where(own[slot], rows[slot] * rows[slot], 0.0)
        factor = 1.0 / jnp.maximum(jnp.sqrt(square), 1.0)
        for slot in range(8):
            outs[slot][0, g * 8 : (g + 1) * 8, :] = jnp.where(own[slot], rows[slot] * factor, rows[slot])
            for i in range(1, NV):
                row = (slot * NV + i) * 8
                outs[slot][i, g * 8 : (g + 1) * 8, :] = (
                    points[slot][i, g * 8 : (g + 1) * 8, :] + change[row : row + 8, cols(g)]
                )


def merge_kernel(slots):
    def kernel(place_ref, *rest):
        pieces = rest[: len(slots)]
        out, sems = rest[-2:]
        x = place_ref[1]
        core = place_ref[2]
        pairs = []
        for piece, slot in zip(pieces, slots):
            dx, dc = SLOTS[slot]
            col = pl.multiple_of((x ^ dx) * LANE, LANE)
            row = pl.multiple_of((core ^ dc) * 32, 32)
            pairs.append((piece, out.at[:, pl.ds(row, 32), pl.ds(col, LANE)]))
        for copy in fetch(pairs, sems):
            copy.wait()

    return kernel


def vmem():
    return pl.BlockSpec(memory_space=pltpu.VMEM)


def anywhere():
    return pl.BlockSpec(memory_space=pltpu.MemorySpace.HBM)


def position():
    zone = lax.axis_index("zone")
    var = lax.axis_index("var")
    return zone * NZ - 192, var >> 1, var & 1, zone & 1


def call(kernel, args, outs, scratch=(), far_args=(), copies=0, hbm_out=False, aliases=None):
    space = anywhere if hbm_out else vmem
    far_args = [pltpu.with_memory_space_constraint(a, pltpu.MemorySpace.HBM) for a in far_args]


    def placed(*refs):
        kernel(position(), *refs)

    return pl.pallas_call(
        placed,
        out_shape=tuple(jax.ShapeDtypeStruct(shape, dtype) for shape, dtype in outs),
        in_specs=[vmem() for _ in args] + [anywhere() for _ in far_args],
        out_specs=tuple(space() for _ in outs),
        scratch_shapes=[pltpu.VMEM(shape, dtype) for shape, dtype in scratch]
        + ([pltpu.SemaphoreType.DMA((copies,))] if copies else []),
        input_output_aliases=aliases or {},
        compiler_params=pltpu.CompilerParams(vmem_limit_bytes=32 << 20),
    )(*args, *far_args)


def per_device(history, adjacency, volume_op, face_lift, schmid_map, hardening):
    count = lax.axis_size("zone")
    groups = lax.axis_size("var")
    flat = history.reshape(ROWS, NZ)
    near = ((ROWS // 2, LANE), F32)
    far = ((ROWS + 8, LANE), F32)
    near_one, near_two, far_one, far_two, local, faces, volume, lifts = call(
        pack_kernel,
        (),
        [
            near, near, far, far, ((ROWS, NZ), F32), ((NFACE, NZ), jnp.int32), ((NP, NP), F32), ((NFACE * NP, NP), F32),
        ],
        far_args=(flat, adjacency, volume_op, face_lift.reshape(NFACE * NP, NP)),
        copies=7,
    )

    def swap_pairs(shift):
        pairs = []
        for z in range(count):
            other = ((z + shift) ^ 1) - shift
            for v in range(groups):
                target = other * groups + v if 0 <= other < count else z * groups + (v ^ 1)
                pairs.append((z * groups + v, target))
        return pairs

    one, two = swap_pairs(1), swap_pairs(0)
    axes = ("zone", "var")
    near_one = lax.ppermute(near_one, axes, one)
    near_two = lax.ppermute(near_two, axes, two)
    far_one = lax.ppermute(far_one, axes, one)
    far_two = lax.ppermute(far_two, axes, two)
    buffer = ((2, KDIM, NV * LANE), BF16)
    wide = lambda n: ((ROWS, n * LANE), F32)
    pair = lambda n: ((2 * ROWS, n * LANE), BF16)
    *inner, weights = call(
        inner_kernel,
        (local, faces, volume, lifts),
        [
            wide(5), pair(3), ((7, 256, MATMUL_FACES * LANE), BF16),
            wide(2), pair(2), wide(1), pair(1), ((2 * NP, KDIM), BF16),
        ],
        [buffer, buffer],
    )
    onehots = inner[2]
    middle = call(
        middle_kernel,
        (local, faces, near_one, near_two, *inner, weights),
        [wide(2), pair(2), wide(2), pair(2), wide(3), pair(3)],
        [pair(2), pair(2), wide(4), pair(4), buffer, buffer],
    )
    piece = ((NV, 32, LANE), F32)
    *ahead, t2, parts3 = call(
        edge_kernel,
        (local, faces, far_one, far_two, onehots, weights, *middle),
        [piece, piece, wide(5), pair(5)],
        [
            far, far, pair(2), pair(2), pair(2), pair(2), ((4, 256, MATMUL_FACES * LANE), BF16),
            wide(2), buffer, buffer,
        ],
    )
    ready = {(2, 0): ahead[0], (2, 1): ahead[1]}
    for steps in ((1, 3), (0,)):
        pieces = call(
            last_kernel(steps),
            (local, faces, weights, onehots, t2, parts3),
            [piece, piece] * len(steps),
            [buffer] * len(steps),
        )
        for i, dx in enumerate(steps):
            ready[dx, 0], ready[dx, 1] = pieces[2 * i : 2 * i + 2]
    advected = [ready[slot] for slot in SLOTS]

    def exchange(piece, dx, dc):
        if dx == 0 and dc == 0:
            return piece
        pairs = [(v, v ^ (2 * dx + dc)) for v in range(groups)]
        return lax.ppermute(piece, "var", pairs)

    points = [exchange(piece, dx, dc) for piece, (dx, dc) in zip(advected, SLOTS)]
    mixing, renewing = call(
        table_kernel,
        (),
        [((192, ROWS), BF16), ((ROWS, 288), BF16)],
        [((12, 48), F32), ((12, 48), F32)],
        far_args=(schmid_map.T, hardening),
        copies=2,
    )
    renewed = call(
        point_kernel,
        (mixing, renewing, *points),
        [piece] * 8,
        [((ROWS, 512), BF16), ((ROWS, 512), BF16), ((288, 512), BF16)],
    )
    returned = [exchange(piece, dx, dc) for piece, (dx, dc) in zip(renewed, SLOTS)]
    out = call(
        merge_kernel(EARLY), [returned[i] for i in EARLY], [((NV, NP, NZ), F32)],
        copies=len(EARLY), hbm_out=True,
    )[0]
    return call(
        merge_kernel(LATE), [returned[i] for i in LATE], [((NV, NP, NZ), F32)],
        far_args=(out,), copies=len(LATE), hbm_out=True, aliases={len(LATE): 0},
    )[0]


def solution(mesh):
    in_specs = (P("var", None, "zone"), P(None, "zone"), P(), P(), P(), P())
    out_specs = P("var", None, "zone")

    return jax.shard_map(per_device, mesh=mesh, in_specs=in_specs, out_specs=out_specs, check_vma=False)
```
